512 devices in a mesh: gx: 16 (over y, core), gy: 8 (over z), gz: 4 (over x).
Axes of the slice: x: 4, y: 8, z: 8, core: 2. Of those that a mesh axis runs over, the one named last changes fastest.
Arguments:
- source_field: float32 [2, 256, 128, 512], P(None, 'gx', 'gy', 'gz'), may hold values from -6 to 6
- mach_number: bfloat16 [256, 128, 512], P('gx', 'gy', 'gz'), may hold values from 0.14941406 to 0.59765625
Outputs:
- correction: float32 [2, 256, 128, 512], P(None, 'gx', 'gy', 'gz')
The draws below stay inside these ranges and needn't reach their ends.
All inputs are finite; a program needn't handle non-finite values.
Results may differ from the reference program's by a relative error of at most 0.0003.
Values sent between devices are 32-bit elements; how exact they have to be, the bound alone decides.
No kernel may reach another device: no remote copies, remote signals or barrier semaphores. Data moves between devices by JAX's collectives and lax.ppermute only.
A program may use at most 128 MiB of HBM per device.

```python
import math
import jax
import jax.numpy as jnp

LEVELS = 5
PRE = 2
POST = 2
COARSE_SWEEPS = 6
NX = 256
NY = 128
NZ = 512


def draw_source_field(key, part):
    extent = (2, NX, NY, NZ)
    result = jnp.clip(jax.random.normal(key, extent, jnp.float32), -6.0, 6.0)
    return result.astype(jnp.float32)


def shard_levels(stream_key, dims, shards, least, largest):
    def one(dim, parts):
        heights = jax.random.uniform(jax.random.fold_in(jax.random.fold_in(stream_key, 6), dim), (parts,), jnp.float32, least / len(shards), largest / len(shards))
        return jnp.repeat(jnp.exp(heights), dims[dim] // parts).reshape((-1,) + (1,) * (len(dims) - dim - 1))

    factor_of = one(*shards[0])
    for cut in shards[1:]:
        factor_of = factor_of * one(*cut)
    return factor_of


def setup_inputs(seed: int = 0) -> dict:
    streams_of = jax.random.split(jax.random.key(seed), 3)
    return {
        "source_field": draw_source_field(jax.random.fold_in(streams_of[2], 71), 0),
        "mach_number": jnp.clip(jnp.exp(math.log(0.59765625) - 1.3862944 * jax.random.uniform(streams_of[1], (NX, NY, NZ), jnp.float32) ** shard_levels(streams_of[1], (NX, NY, NZ), ((0, 16), (1, 8), (2, 4)), -0.2, 0.2)), 0.14941406, 0.59765625).astype(jnp.bfloat16),
    }


wave_step = 0.25
jacobi_weight = 0.5


def complex_times(values, factor):
    real_part = values[0] * factor[0] - values[1] * factor[1]
    imaginary = values[0] * factor[1] + values[1] * factor[0]
    return jnp.stack([real_part, imaginary])


def inverse_diagonal(mach_field, grid_level):
    diffusion_scale = 0.25 ** grid_level
    wave_square = wave_step * wave_step
    axial_weight = 1.0 - mach_field * mach_field
    diagonal_real = diffusion_scale * (2.0 * axial_weight + 4.0) - wave_square
    diagonal_imaginary = 0.5 * wave_square
    modulus = diagonal_real * diagonal_real + diagonal_imaginary * diagonal_imaginary
    return jnp.stack([diagonal_real / modulus, -diagonal_imaginary / modulus])


def operate(padded, mach_field, grid_level):
    centre = padded[:, 1:-1, 1:-1, 1:-1]
    east_cells = padded[:, 2:, 1:-1, 1:-1]
    west_cells = padded[:, :-2, 1:-1, 1:-1]
    north_cells = padded[:, 1:-1, 2:, 1:-1]
    south_cells = padded[:, 1:-1, :-2, 1:-1]
    upper_cells = padded[:, 1:-1, 1:-1, 2:]
    lower_cells = padded[:, 1:-1, 1:-1, :-2]
    diffusion_scale = 0.25 ** grid_level
    axial_weight = 1.0 - mach_field * mach_field
    spread = diffusion_scale * (axial_weight * (2.0 * centre - east_cells - west_cells)
                                + (2.0 * centre - north_cells - south_cells)
                                + (2.0 * centre - upper_cells - lower_cells))
    advect = wave_step * 0.5 ** grid_level * mach_field
    axial_slope = east_cells - west_cells
    wave_square = wave_step * wave_step
    real_part = spread[0] + advect * axial_slope[1] - wave_square * (centre[0] + 0.5 * centre[1])
    imaginary = spread[1] - advect * axial_slope[0] - wave_square * (centre[1] - 0.5 * centre[0])
    return jnp.stack([real_part, imaginary])


def jacobi_step(solution, padded, source, mach_field, inverse, grid_level):
    return solution + jacobi_weight * complex_times(source - operate(padded, mach_field, grid_level), inverse)


def restrict(values):
    leading = values.shape[:-3]
    leading_rank = len(leading)
    first_length, second_length, third_length = values.shape[-3:]
    grouped = values.reshape(leading + (first_length // 2, 2, second_length // 2, 2, third_length // 2, 2))
    return grouped.mean(axis=(leading_rank + 1, leading_rank + 3, leading_rank + 5))


def prolong(values):
    leading = values.shape[:-3]
    first_length, second_length, third_length = values.shape[-3:]
    expanded = values[..., :, None, :, None, :, None]
    expanded = jnp.broadcast_to(expanded, leading + (first_length, 2, second_length, 2, third_length, 2))
    return expanded.reshape(leading + (2 * first_length, 2 * second_length, 2 * third_length))


def pad_cells(solution):
    return jnp.pad(solution, ((0, 0), (1, 1), (1, 1), (1, 1)))


def coarse_solve(source, mach_field, grid_level):
    inverse = inverse_diagonal(mach_field, grid_level)
    solution = jacobi_weight * complex_times(source, inverse)
    for sweep_index in range(COARSE_SWEEPS - 1):
        solution = jacobi_step(solution, pad_cells(solution), source, mach_field, inverse, grid_level)
    return solution


def multigrid(source, mach_levels, grid_level):
    mach_field = mach_levels[grid_level]
    if grid_level == LEVELS - 1:
        return coarse_solve(source, mach_field, grid_level)
    inverse = inverse_diagonal(mach_field, grid_level)
    solution = jacobi_weight * complex_times(source, inverse)
    for sweep_index in range(PRE - 1):
        solution = jacobi_step(solution, pad_cells(solution), source, mach_field, inverse, grid_level)
    residual = source - operate(pad_cells(solution), mach_field, grid_level)
    coarse = multigrid(restrict(residual), mach_levels, grid_level + 1)
    solution = solution + prolong(coarse)
    for sweep_index in range(POST):
        solution = jacobi_step(solution, pad_cells(solution), source, mach_field, inverse, grid_level)
    return solution


def reference(source_field, mach_number):
    mach_levels = [mach_number.astype(jnp.float32)]
    for grid_level in range(1, LEVELS):
        mach_levels.append(restrict(mach_levels[-1]))
    return multigrid(source_field, mach_levels, 0)
```

```python
import functools

import jax
import jax.numpy as jnp
from jax import lax
from jax.experimental import pallas as pl
from jax.experimental.pallas import tpu as pltpu
from jax.sharding import PartitionSpec as P

F32, BF16 = jnp.float32, jnp.bfloat16
WAVE = 0.0625
DIAG_I = 0.5 * WAVE

X0, Y0, L0 = 22, 24, 256
X1, Y1, L1 = 16, 16, 128
X2, Y2 = 12, 32
X3, Y3, PAD3 = 32, 16, 4
X4, Y4 = 16, 8


def iota(shape, dim):
    return lax.broadcasted_iota(jnp.int32, shape, dim)


def split(x):
    high = x.astype(BF16)
    rest = x - high.astype(F32)
    middle = rest.astype(BF16)
    return high, middle, (rest - middle.astype(F32)).astype(BF16)


def select(x, matrix, dims=(((1,), (0,)), ((), ()))):
    parts = [lax.dot_general(p, matrix, dims, preferred_element_type=F32) for p in split(x)]
    return parts[0] + (parts[1] + parts[2])


def coefficients(mach, level):
    scale = 0.25**level
    axial = scale * (1.0 - mach * mach)
    advect = (0.25 * 0.5**level) * mach
    diagonal = 2.0 * axial + (4.0 * scale - WAVE)
    return axial, advect, diagonal


def half_inverse(mach, level):
    diagonal = coefficients(mach, level)[2]
    scale = 0.5 / (diagonal * diagonal + DIAG_I * DIAG_I)
    inside = mach > 0.0
    return jnp.where(inside, diagonal * scale, 0.0), jnp.where(inside, -DIAG_I * scale, 0.0)


def transverse(c, ymask, zmask):
    rows, lanes = c.shape
    north, south = pltpu.roll(c, rows - 1, 0), pltpu.roll(c, 1, 0)
    upper, lower = pltpu.roll(c, lanes - 1, 1), pltpu.roll(c, 1, 1)
    if ymask:
        at = iota(c.shape, 0)
        north = jnp.where(at == rows - 1, 0.0, north)
        south = jnp.where(at == 0, 0.0, south)
    if zmask:
        at = iota(c.shape, 1)
        upper = jnp.where(at == lanes - 1, 0.0, upper)
        lower = jnp.where(at == 0, 0.0, lower)
    return (north + south) + (upper + lower)


def balance(g_r, g_i, mach, v, i, level, ymask, zmask):
    axial, advect, diagonal = coefficients(mach, level)
    scale = 0.25**level
    c_r, c_i = v[0, i], v[1, i]
    e_r, w_r, e_i, w_i = v[0, i + 1], v[0, i - 1], v[1, i + 1], v[1, i - 1]
    t_r = g_r + axial * (e_r + w_r) - advect * (e_i - w_i)
    t_i = g_i + axial * (e_i + w_i) + advect * (e_r - w_r)
    return (
        t_r + scale * transverse(c_r, ymask, zmask),
        t_i + scale * transverse(c_i, ymask, zmask),
        c_r,
        c_i,
        diagonal,
    )


def first_loop(lo, hi, g, hd, v, level):
    def body(i, _):
        h_r, h_i = half_inverse(g[2, i], level)
        hd[0, i], hd[1, i] = h_r, h_i
        g_r, g_i = g[0, i], g[1, i]
        v[0, i] = h_r * g_r - h_i * g_i
        v[1, i] = h_r * g_i + h_i * g_r
        return 0

    lax.fori_loop(lo, hi, body, 0)


def relax_loop(lo, count, g, hd, v, write, level, ymask=False, zmask=False):
    def body(j, _):
        i = lo + j
        t_r, t_i, c_r, c_i, _d = balance(g[0, i], g[1, i], g[2, i], v, i, level, ymask, zmask)
        h_r, h_i = hd[0, i], hd[1, i]
        write(j, i, 0.5 * c_r + (h_r * t_r - h_i * t_i), 0.5 * c_i + (h_r * t_i + h_i * t_r))
        return 0

    lax.fori_loop(0, count, body, 0)


def writer(out):
    def write(j, i, re, im):
        out[0, i], out[1, i] = re, im

    return write


def residual(g, v, i, level, ymask=False, zmask=False):
    t_r, t_i, c_r, c_i, d = balance(g[0, i], g[1, i], g[2, i], v, i, level, ymask, zmask)
    return t_r - (d * c_r - DIAG_I * c_i), t_i - (d * c_i + DIAG_I * c_r)


def residual_pair(g, v, i, level, ymask=False, zmask=False):
    a = residual(g, v, i, level, ymask, zmask)
    b = residual(g, v, i + 1, level, ymask, zmask)
    return a[0] + b[0], a[1] + b[1], g[2, i] + g[2, i + 1]


def pair_rows(ref, rows):
    return ref[pl.ds(0, rows // 2, stride=2), :] + ref[pl.ds(1, rows // 2, stride=2), :]


def twin_rows(ref, value):
    rows = value.shape[0]
    ref[pl.ds(0, rows, stride=2), :] = value
    ref[pl.ds(1, rows, stride=2), :] = value


def matrix(rows, lanes, rule, value=1.0):
    shape = (rows, lanes)
    return jnp.where(rule(iota(shape, 0), iota(shape, 1)), value, 0.0).astype(BF16)


def gather_kernel(own_lanes, width, own, ylo, yhi, xlo, xhi, f, packed):
    count = own.shape[1]
    rows = own.shape[2]
    hx = xlo.shape[1]
    for c in range(3):
        f[c, 0:hx] = xlo[c]
        f[c, hx : hx + count, 0:4] = ylo[c]
        f[c, hx : hx + count, 4 : 4 + rows] = own[c]
        f[c, hx : hx + count, 4 + rows :] = yhi[c]
        f[c, hx + count :] = xhi[c]
    edge = matrix(
        8,
        128,
        lambda r, l: ((r < 4) & (l == r)) | ((r >= 4) & (l == own_lanes - 8 + r)),
    )
    flat = f[...].reshape(-1, 128)
    total = None
    for part in split(flat):
        term = lax.dot_general(edge, part, (((1,), (1,)), ((), ())), preferred_element_type=F32)
        total = term if total is None else total + term
    packed[...] = total


def unpack_lanes(lower, upper, lower_start, upper_start):
    both = jnp.concatenate([upper[...], lower[...]], axis=0)
    place = matrix(
        16,
        128,
        lambda r, l: ((r < 4) & (l == upper_start + r)) | ((r >= 12) & (l == lower_start + r - 12)),
    )
    return select(both, place, (((0,), (0,)), ((), ())))


def down0_kernel(f, lower, upper, g, hd, v2, coarse, v1, sums):
    tail = unpack_lanes(lower, upper, 124, 0).reshape(3, X0, Y0, 128)
    g[:, :, :, 0:128] = f[...]
    g[:, :, :, 128:256] = tail
    first_loop(0, X0, g, hd, v1, 0)
    relax_loop(1, X0 - 2, g, hd, v1, writer(v2), 0)

    def body(k, _):
        parts = residual_pair(g, v2, 3 + 2 * k, 0)
        for c in range(3):
            row = pl.multiple_of((c * 8 + k) * 16, 16)
            sums[pl.ds(row, 16), :] = parts[c][4:20, 0:128]
        return 0

    lax.fori_loop(0, 8, body, 0)
    halve = matrix(128, 128, lambda r, l: r // 2 == l, 0.125)
    coarse[...] = select(pair_rows(sums, 384), halve).reshape(3, 8, 8, 128)


def down1_kernel(f, lower, upper, g, hd, v2, chunk, v1, sums, g2, hd2, va, vb):
    tail = unpack_lanes(lower, upper, 124, 64).reshape(3, X1, Y1, 128)
    g[...] = f[...] + tail
    first_loop(0, X1, g, hd, v1, 1)
    relax_loop(1, X1 - 2, g, hd, v1, writer(v2), 1)

    def body(k, _):
        parts = residual_pair(g, v2, 2 + 2 * k, 1)
        for c in range(3):
            row = pl.multiple_of((c * 6 + k) * 16, 16)
            sums[pl.ds(row, 16), :] = parts[c]
        return 0

    lax.fori_loop(0, 6, body, 0)
    halve = matrix(
        128,
        128,
        lambda r, l: ((r < 66) & (r // 2 == l)) | ((r >= 124) & (r // 2 + 64 == l)),
        0.125,
    )
    g2[...] = select(pair_rows(sums, 288), halve).reshape(3, 6, 8, 128)
    first_loop(0, 6, g2, hd2, va, 2)
    relax_loop(1, 4, g2, hd2, va, writer(vb), 2)
    lane = iota((8, 128), 1) // 32
    chunk[...] = jnp.zeros_like(chunk)
    for c in range(5):
        source = (lambda x: g2[c, x]) if c < 3 else (lambda x: vb[c - 3, x])
        total = source(1)
        for x in range(1, 4):
            total = jnp.where(lane == x, pltpu.roll(source(1 + x), 32 * x, 1), total)
        chunk[4 * c : 4 * c + 4, :] = total[2:6, :]


def down2_kernel(own, left, right, a, chunk, planes, sums):
    lane = iota((Y2, 128), 1) // 32
    for p, piece in enumerate((left, own, right)):

        def body(c, _):
            for gz in range(4):
                for gy in range(8):
                    planes[gz, 4 * gy : 4 * gy + 4, :] = piece[gy * 4 + gz, pl.ds(4 * c, 4), :]
            for x in range(4):
                total = None
                for gz in range(4):
                    value = planes[gz]
                    if gz != x:
                        value = pltpu.roll(value, (32 * (gz - x)) % 128, 1)
                    total = value if total is None else jnp.where(lane == gz, value, total)
                a[c, 4 * p + x] = total
            return 0

        lax.fori_loop(0, 5, body, 0)
    v = a.at[3:5]
    for k in range(2):
        parts = residual_pair(a, v, 4 + 2 * k, 2, True, True)
        for c in range(3):
            sums[k, Y2 * c : Y2 * (c + 1), :] = parts[c]
    total = None
    for k in range(2):
        halve = matrix(128, 128, lambda r, l: r // 2 + 64 * k == l, 0.125)
        term = select(pair_rows(sums.at[k], 3 * Y2), halve)
        total = term if total is None else total + term
    chunk[...] = total


def up_kernel(
    index, parts3, a, g1, hd1, v21, g0, hd0, v20, out,
    g3, hd3, va3, vb3, s3, g4, hd4, va4, vb4, t4, w3, t3, hd2, va2, vb2, w2, t2, va1, vb1, t1, va0, vb0,
):
    gx, gy, gz = index[0], index[1], index[2]
    zero3 = jnp.zeros((Y3, 128), F32)
    for ref in (g3, hd3, va3, vb3):
        for c in range(ref.shape[0]):
            for i in range(PAD3):
                ref[c, i] = zero3
                ref[c, PAD3 + X3 + i] = zero3
    low = iota((Y3, 128), 1) < 64

    def spread(s, _):
        for c in range(3):
            value = parts3[s, Y3 * c : Y3 * (c + 1), :]
            g3[c, PAD3 + 2 * s] = jnp.where(low, value, 0.0)
            g3[c, PAD3 + 2 * s + 1] = jnp.where(low, pltpu.roll(value, 64, 1), 0.0)
        return 0

    lax.fori_loop(0, 16, spread, 0)
    first_loop(PAD3, PAD3 + X3, g3, hd3, va3, 3)
    relax_loop(PAD3, X3, g3, hd3, va3, writer(vb3), 3, True)

    def body3(k, _):
        parts = residual_pair(g3, vb3, PAD3 + 2 * k, 3, True)
        for c in range(3):
            s3[pl.ds(pl.multiple_of((c * X4 + k) * Y3, Y3), Y3), :] = parts[c]
        return 0

    lax.fori_loop(0, X4, body3, 0)
    halve = matrix(128, 128, lambda r, l: (r // 2 == l) & (r < 64), 0.125)
    g4[:, 1 : 1 + X4] = select(pair_rows(s3, 3 * X4 * Y3), halve).reshape(3, X4, Y4, 128)
    for ref in (va4, vb4):
        for c in range(2):
            ref[c, 0] = jnp.zeros((Y4, 128), F32)
            ref[c, X4 + 1] = jnp.zeros((Y4, 128), F32)
    first_loop(1, X4 + 1, g4, hd4, va4, 4)
    src, dst = va4, vb4
    for _ in range(5):
        relax_loop(1, X4, g4, hd4, src, writer(dst), 4, True)
        src, dst = dst, src
    double = matrix(128, 128, lambda r, l: l // 2 == r)
    twin_rows(t4, select(src[:, 1 : 1 + X4].reshape(2 * X4 * Y4, 128), double))

    def add3(k, _):
        for c in range(2):
            value = t4[pl.ds(pl.multiple_of((c * X4 + k) * Y3, Y3), Y3), :]
            vb3[c, PAD3 + 2 * k] = vb3[c, PAD3 + 2 * k] + value
            vb3[c, PAD3 + 2 * k + 1] = vb3[c, PAD3 + 2 * k + 1] + value
        return 0

    lax.fori_loop(0, X4, add3, 0)
    base = PAD3 + 2 * gx
    relax_loop(base - 3, 8, g3, hd3, vb3, writer(va3), 3, True)

    def write3(j, i, re, im):
        w3[0, j], w3[1, j] = re, im

    relax_loop(base - 2, 6, g3, hd3, va3, write3, 3, True)
    twin_rows(t3, select(w3[...].reshape(2 * 6 * Y3, 128), double))

    def start2(i, _):
        hd2[0, i], hd2[1, i] = half_inverse(a[2, i], 2)
        for c in range(2):
            row = pl.multiple_of((c * 6 + i // 2) * Y2, Y2)
            va2[c, i] = a[3 + c, i] + jnp.where(a[2, i] > 0.0, t3[pl.ds(row, Y2), :], 0.0)
        return 0

    lax.fori_loop(0, X2, start2, 0)
    relax_loop(1, X2 - 2, a, hd2, va2, writer(vb2), 2, True, True)
    w2[...] = jnp.zeros_like(w2)

    def write2(j, i, re, im):
        w2[0, j, 8 : 8 + Y2], w2[1, j, 8 : 8 + Y2] = re, im

    relax_loop(2, X2 - 4, a, hd2, vb2, write2, 2, True, True)
    rows = w2[:, :, pl.ds(4 * gy + 6, 8), :].reshape(2 * 8 * 8, 128)

    def place1(r, l):
        at = jnp.where(l < 96, l, l - 128)
        return r == 32 * gz + (at + 128) // 2 - 64

    twin_rows(t2, select(rows, matrix(128, 128, place1)))

    def start1(i, _):
        for c in range(2):
            row = pl.multiple_of((c * 8 + i // 2) * Y1, Y1)
            va1[c, i] = v21[c, i] + t2[pl.ds(row, Y1), :]
        return 0

    lax.fori_loop(1, X1 - 1, start1, 0)
    relax_loop(2, X1 - 4, g1, hd1, va1, writer(vb1), 1)
    relax_loop(3, X1 - 6, g1, hd1, vb1, writer(va1), 1)
    own = va1[:, 3:13].reshape(2 * 10 * Y1, 128)
    for half in range(2):
        place = matrix(128, 128, lambda r, l: r == (l + 128 * half) // 2)
        twin_rows(t1.at[half], select(own, place))

    def start0(k, _):
        for c in range(2):
            row = (c * 10 + k) * 32 + 4
            for half in range(2):
                lanes = slice(128 * half, 128 * half + 128)
                value = t1[half, pl.ds(row, Y0), :]
                for i in range(2):
                    va0[c, 2 * k + 1 + i, :, lanes] = v20[c, 2 * k + 1 + i, :, lanes] + value
        return 0

    lax.fori_loop(0, 10, start0, 0)
    relax_loop(2, X0 - 4, g0, hd0, va0, writer(vb0), 0)

    def write0(j, i, re, im):
        out[0, j], out[1, j] = re[4:20, 0:128], im[4:20, 0:128]

    relax_loop(3, X0 - 6, g0, hd0, vb0, write0, 0)


def vmem(*shape):
    return pltpu.VMEM(shape, F32)


def call(kernel, outs, scratch, *args, smem_first=False):
    spec = pl.BlockSpec(memory_space=pltpu.VMEM)
    specs = [spec] * len(args)
    if smem_first:
        specs[0] = pl.BlockSpec(memory_space=pltpu.SMEM)
    return pl.pallas_call(
        kernel,
        out_shape=[jax.ShapeDtypeStruct(s, F32) for s in outs],
        in_specs=specs,
        out_specs=[spec] * len(outs),
        scratch_shapes=[vmem(*s) for s in scratch],
        compiler_params=pltpu.CompilerParams(vmem_limit_bytes=48 << 20),
    )(*args)


def shift(block, axis, step):
    count = lax.axis_size(axis)
    pairs = [(i, i + step) for i in range(count) if 0 <= i + step < count]
    return lax.ppermute(block, axis, pairs)


def with_halos(own, hx, own_lanes):
    rows = own.shape[2]
    count = own.shape[1]
    ylo = shift(own[:, :, rows - 4 :], "gy", 1)
    yhi = shift(own[:, :, :4], "gy", -1)

    def edge(at):
        return jnp.concatenate([x[:, at : at + hx] for x in (ylo, own, yhi)], axis=2)

    xlo = shift(edge(count - hx), "gx", 1)
    xhi = shift(edge(0), "gx", -1)
    shape = (3, count + 2 * hx, rows + 8, 128)
    flat = shape[0] * shape[1] * shape[2]
    f, packed = call(
        functools.partial(gather_kernel, own_lanes, None), [shape, (8, flat)], [], own, ylo, yhi, xlo, xhi
    )
    return f, shift(packed, "gz", 1), shift(packed, "gz", -1)


def everyone(block, axes):
    count = lax.axis_size(axes)
    return lax.all_to_all(jnp.broadcast_to(block, (count,) + block.shape), axes, 0, 0)


def shards(source_field, mach_number):
    own0 = jnp.concatenate([source_field, mach_number.astype(F32)[None]], axis=0)
    f0, lower0, upper0 = with_halos(own0, 3, 128)
    full0 = (X0, Y0, L0)
    g0, hd0, v20, own1 = call(
        down0_kernel,
        [(3,) + full0, (2,) + full0, (2,) + full0, (3, 8, 8, 128)],
        [(2,) + full0, (384, 128)],
        f0, lower0, upper0,
    )
    f1, lower1, upper1 = with_halos(own1, 4, 64)
    full1 = (X1, Y1, L1)
    g1, hd1, v21, chunk2 = call(
        down1_kernel,
        [(3,) + full1, (2,) + full1, (2,) + full1, (24, 128)],
        [(2,) + full1, (288, 128), (3, 6, 8, 128)] + [(2, 6, 8, 128)] * 3,
        f1, lower1, upper1,
    )
    own2 = everyone(chunk2, ("gy", "gz"))
    left2 = shift(own2, "gx", 1)
    right2 = shift(own2, "gx", -1)
    a, chunk3 = call(
        down2_kernel,
        [(5, X2, Y2, 128), (48, 128)],
        [(4, Y2, 128), (2, 96, 128)],
        own2, left2, right2,
    )
    parts3 = everyone(chunk3, "gx")
    index = jnp.stack([lax.axis_index(n) for n in ("gx", "gy", "gz")]).astype(jnp.int32)
    wide3 = (X3 + 2 * PAD3, Y3, 128)
    wide4 = (X4 + 2, Y4, 128)
    scratch = [(3,) + wide3, (2,) + wide3, (2,) + wide3, (2,) + wide3, (3 * X4 * Y3, 128)]
    scratch += [(3,) + wide4, (2,) + wide4, (2,) + wide4, (2,) + wide4, (2 * X4 * Y3, 128)]
    scratch += [(2, 6, Y3, 128), (2 * 6 * Y2, 128)] + [(2, X2, Y2, 128)] * 3
    scratch += [(2, 8, Y2 + 16, 128), (2 * 8 * Y1, 128), (2,) + full1, (2,) + full1]
    scratch += [(2, 2 * 10 * 32, 128), (2,) + full0, (2,) + full0]
    return call(
        up_kernel,
        [(2, 16, 16, 128)],
        scratch,
        index, parts3, a, g1, hd1, v21, g0, hd0, v20,
        smem_first=True,
    )[0]


def solution(mesh):
    return jax.shard_map(
        shards,
        mesh=mesh,
        in_specs=(P(None, "gx", "gy", "gz"), P("gx", "gy", "gz")),
        out_specs=P(None, "gx", "gy", "gz"),
        check_vma=False,
    )
```

```python
import functools

import jax
import jax.numpy as jnp
from jax import lax
from jax.experimental import pallas as pl
from jax.experimental.pallas import tpu as pltpu
from jax.sharding import PartitionSpec as P

F32, BF16 = jnp.float32, jnp.bfloat16
WAVE = 0.0625
DIAG_I = 0.5 * WAVE
MOST = (2, 7, 5, 8, 16)

X0, Y0, L0 = 22, 24, 256
HZ = 10
X1, Y1, L1 = 16, 16, 128
X2, Y2 = 12, 32
X3, Y3, PAD3 = 32, 16, 4
X4, Y4 = 16, 8


def iota(shape, dim):
    return lax.broadcasted_iota(jnp.int32, shape, dim)


def split(x):
    high = x.astype(BF16)
    rest = x - high.astype(F32)
    middle = rest.astype(BF16)
    return high, middle, (rest - middle.astype(F32)).astype(BF16)


def select(x, matrix, dims=(((1,), (0,)), ((), ()))):
    parts = [lax.dot_general(p, matrix, dims, preferred_element_type=F32) for p in split(x)]
    return parts[0] + (parts[1] + parts[2])


def coefficients(mach, level):
    scale = 0.25**level
    axial = scale * (1.0 - mach * mach)
    advect = (0.25 * 0.5**level) * mach
    diagonal = 2.0 * axial + (4.0 * scale - WAVE)
    return axial, advect, diagonal


def half_inverse(mach, level):
    diagonal = coefficients(mach, level)[2]
    scale = 0.5 / (diagonal * diagonal + DIAG_I * DIAG_I)
    inside = mach > 0.0
    return jnp.where(inside, diagonal * scale, 0.0), jnp.where(inside, -DIAG_I * scale, 0.0)


def transverse(c, ymask, zmask):
    rows, lanes = c.shape
    north, south = pltpu.roll(c, rows - 1, 0), pltpu.roll(c, 1, 0)
    upper, lower = pltpu.roll(c, lanes - 1, 1), pltpu.roll(c, 1, 1)
    if ymask:
        at = iota(c.shape, 0)
        north = jnp.where(at == rows - 1, 0.0, north)
        south = jnp.where(at == 0, 0.0, south)
    if zmask:
        at = iota(c.shape, 1)
        upper = jnp.where(at == lanes - 1, 0.0, upper)
        lower = jnp.where(at == 0, 0.0, lower)
    return (north + south) + (upper + lower)


def balance(g_r, g_i, mach, v, i, level, ymask, zmask):
    axial, advect, diagonal = coefficients(mach, level)
    scale = 0.25**level
    c_r, c_i = v[0, i], v[1, i]
    e_r, w_r, e_i, w_i = v[0, i + 1], v[0, i - 1], v[1, i + 1], v[1, i - 1]
    t_r = g_r + axial * (e_r + w_r) - advect * (e_i - w_i)
    t_i = g_i + axial * (e_i + w_i) + advect * (e_r - w_r)
    return (
        t_r + scale * transverse(c_r, ymask, zmask),
        t_i + scale * transverse(c_i, ymask, zmask),
        c_r,
        c_i,
        diagonal,
    )


def blocks(count, most, compute, store):
    unit = max(u for u in range(1, most + 1) if count % u == 0)

    def body(k, _):
        steps = [k * unit + u for u in range(unit)]
        for j, value in zip(steps, [compute(j) for j in steps]):
            store(j, value)
        return 0

    if count == unit:
        body(0, 0)
    else:
        lax.fori_loop(0, count // unit, body, 0)


def first_loop(lo, hi, g, hd, v, level):
    def compute(j):
        i = lo + j
        h_r, h_i = half_inverse(g[2, i], level)
        g_r, g_i = g[0, i], g[1, i]
        return h_r, h_i, h_r * g_r - h_i * g_i, h_r * g_i + h_i * g_r

    def store(j, value):
        i = lo + j
        hd[0, i], hd[1, i], v[0, i], v[1, i] = value

    blocks(hi - lo, MOST[level], compute, store)


def relax_loop(lo, count, g, hd, v, write, level, ymask=False, zmask=False):
    def compute(j):
        i = lo + j
        t_r, t_i, c_r, c_i, _ = balance(g[0, i], g[1, i], g[2, i], v, i, level, ymask, zmask)
        h_r, h_i = hd[0, i], hd[1, i]
        return 0.5 * c_r + (h_r * t_r - h_i * t_i), 0.5 * c_i + (h_r * t_i + h_i * t_r)

    blocks(count, MOST[level], compute, lambda j, value: write(j, lo + j, *value))


def writer(out):
    def write(j, i, re, im):
        out[0, i], out[1, i] = re, im

    return write


def residual(g, v, i, level, ymask=False, zmask=False):
    t_r, t_i, c_r, c_i, d = balance(g[0, i], g[1, i], g[2, i], v, i, level, ymask, zmask)
    return t_r - (d * c_r - DIAG_I * c_i), t_i - (d * c_i + DIAG_I * c_r)


def residual_pair(g, v, i, level, ymask=False, zmask=False):
    a = residual(g, v, i, level, ymask, zmask)
    b = residual(g, v, i + 1, level, ymask, zmask)
    return a[0] + b[0], a[1] + b[1], g[2, i] + g[2, i + 1]


def pair_rows(ref, rows):
    return ref[pl.ds(0, rows // 2, stride=2), :] + ref[pl.ds(1, rows // 2, stride=2), :]


def twin_rows(ref, value):
    rows = value.shape[0]
    ref[pl.ds(0, rows, stride=2), :] = value
    ref[pl.ds(1, rows, stride=2), :] = value


def matrix(rows, lanes, rule, value=1.0):
    shape = (rows, lanes)
    return jnp.where(rule(iota(shape, 0), iota(shape, 1)), value, 0.0).astype(BF16)


def assemble(own, ylo, yhi, xlo, xhi, f):
    count, rows, hx = own.shape[1], own.shape[2], xlo.shape[1]
    for c in range(3):
        f[c, 0:hx] = xlo[c]
        f[c, hx : hx + count, 0:4] = ylo[c]
        f[c, hx : hx + count, 4 : 4 + rows] = own[c]
        f[c, hx : hx + count, 4 + rows :] = yhi[c]
        f[c, hx + count :] = xhi[c]


def views(kept):
    return kept.at[0:3], kept.at[3:5], kept.at[5:7]


def gather0_kernel(own, ylo, yhi, xlo, xhi, f, low_lanes, high_lanes):
    assemble(own, ylo, yhi, xlo, xhi, f)
    parts = split(f[...].reshape(-1, 128))
    for out, start in ((low_lanes, 0), (high_lanes, 118)):
        edge = matrix(16, 128, lambda r, l: (r < HZ) & (l == start + r))
        dims = (((1,), (1,)), ((), ()))
        terms = [lax.dot_general(edge, p, dims, preferred_element_type=F32) for p in parts]
        out[...] = terms[0] + (terms[1] + terms[2])


def smooth0(f, lower, upper, g, hd, v2, v1):
    both = jnp.concatenate([upper[...], lower[...]], axis=0)
    place = matrix(32, 128, lambda r, l: ((r < HZ) & (l == r)) | ((r >= 16) & (l == r + 102)))
    tail = select(both, place, (((0,), (0,)), ((), ())))
    g[:, :, :, 0:128] = f[...]
    g[:, :, :, 128:256] = tail.reshape(3, X0, Y0, 128)
    first_loop(0, X0, g, hd, v1, 0)
    relax_loop(1, X0 - 2, g, hd, v1, writer(v2), 0)


def keep0_kernel(f, lower, upper, kept, v1):
    smooth0(f, lower, upper, *views(kept), v1)


def down0_kernel(f, lower, upper, coarse, g, hd, v2, v1, sums):
    smooth0(f, lower, upper, g, hd, v2, v1)

    def store(k, parts):
        for c in range(3):
            row = pl.multiple_of((c * 8 + k) * 16, 16)
            for half in range(2):
                sums[half, pl.ds(row, 16), :] = parts[c][4:20, 128 * half : 128 * half + 128]

    blocks(8, 1, lambda k: residual_pair(g, v2, 3 + 2 * k, 0), store)
    own = matrix(128, 128, lambda r, l: r // 2 == l, 0.125)
    rest = matrix(
        128,
        128,
        lambda r, l: ((r < 8) & (r // 2 + 64 == l)) | ((r >= 120) & (r // 2 + 64 == l)),
        0.125,
    )
    total = select(pair_rows(sums.at[0], 384), own) + select(pair_rows(sums.at[1], 384), rest)
    coarse[...] = total.reshape(3, 8, 8, 128)


def down1_kernel(own, ylo, yhi, xlo, xhi, kept, chunk, v1, sums, g2, hd2, va, vb):
    g, hd, v2 = views(kept)
    assemble(own, ylo, yhi, xlo, xhi, g)
    first_loop(0, X1, g, hd, v1, 1)
    relax_loop(1, X1 - 2, g, hd, v1, writer(v2), 1)

    def store(k, parts):
        for c in range(3):
            row = pl.multiple_of((c * 6 + k) * 16, 16)
            sums[pl.ds(row, 16), :] = parts[c]

    blocks(6, 3, lambda k: residual_pair(g, v2, 2 + 2 * k, 1), store)
    halve = matrix(
        128,
        128,
        lambda r, l: ((r < 66) & (r // 2 == l)) | ((r >= 124) & (r // 2 + 64 == l)),
        0.125,
    )
    g2[...] = select(pair_rows(sums, 288), halve).reshape(3, 6, 8, 128)
    first_loop(0, 6, g2, hd2, va, 2)
    relax_loop(1, 4, g2, hd2, va, writer(vb), 2)
    lane = iota((8, 128), 1) // 32
    for c in range(5):
        source = (lambda x: g2[c, x]) if c < 3 else (lambda x: vb[c - 3, x])
        total = source(1)
        for x in range(1, 4):
            total = jnp.where(lane == x, pltpu.roll(source(1 + x), 32 * x, 1), total)
        chunk[c] = total[2:6, :]


def down2_kernel(own, left, right, a, chunk, planes, sums):
    lane = iota((Y2, 128), 1) // 32
    for p, piece in enumerate((left, own, right)):

        def body(c, _):
            for gz in range(4):
                for gy in range(8):
                    planes[gz, 4 * gy : 4 * gy + 4, :] = piece[gy * 4 + gz, c]
            for x in range(4):
                total = None
                for gz in range(4):
                    value = planes[gz]
                    if gz != x:
                        value = pltpu.roll(value, (32 * (gz - x)) % 128, 1)
                    total = value if total is None else jnp.where(lane == gz, value, total)
                a[c, 4 * p + x] = total
            return 0

        lax.fori_loop(0, 5, body, 0)
    v = a.at[3:5]
    for k in range(2):
        parts = residual_pair(a, v, 4 + 2 * k, 2, True, True)
        for c in range(3):
            sums[k, Y2 * c : Y2 * (c + 1), :] = parts[c]
    total = None
    for k in range(2):
        halve = matrix(128, 128, lambda r, l: r // 2 + 64 * k == l, 0.125)
        term = select(pair_rows(sums.at[k], 3 * Y2), halve)
        total = term if total is None else total + term
    chunk[...] = total


def up_kernel(
    index, parts3, a, kept1, kept0, out,
    g3, hd3, va3, vb3, s3, g4, hd4, va4, vb4, t4, w3, t3, hd2, va2, vb2, w2, t2, va1, vb1, t1, va0, vb0,
):
    gx, gy, gz = index[0], index[1], index[2]
    g1, hd1, v21 = views(kept1)
    g0, hd0, v20 = views(kept0)
    zero3 = jnp.zeros((Y3, 128), F32)
    for ref in (g3, hd3, va3, vb3):
        for c in range(ref.shape[0]):
            for i in range(PAD3):
                ref[c, i] = zero3
                ref[c, PAD3 + X3 + i] = zero3
    low = iota((Y3, 128), 1) < 64

    def spread(s, _):
        for c in range(3):
            value = parts3[s, Y3 * c : Y3 * (c + 1), :]
            g3[c, PAD3 + 2 * s] = jnp.where(low, value, 0.0)
            g3[c, PAD3 + 2 * s + 1] = jnp.where(low, pltpu.roll(value, 64, 1), 0.0)
        return 0

    lax.fori_loop(0, 16, spread, 0)
    first_loop(PAD3, PAD3 + X3, g3, hd3, va3, 3)
    relax_loop(PAD3, X3, g3, hd3, va3, writer(vb3), 3, True)

    def keep3(k, parts):
        for c in range(3):
            s3[pl.ds(pl.multiple_of((c * X4 + k) * Y3, Y3), Y3), :] = parts[c]

    blocks(X4, 4, lambda k: residual_pair(g3, vb3, PAD3 + 2 * k, 3, True), keep3)
    halve = matrix(128, 128, lambda r, l: (r // 2 == l) & (r < 64), 0.125)
    g4[:, 1 : 1 + X4] = select(pair_rows(s3, 3 * X4 * Y3), halve).reshape(3, X4, Y4, 128)
    for ref in (va4, vb4):
        for c in range(2):
            ref[c, 0] = jnp.zeros((Y4, 128), F32)
            ref[c, X4 + 1] = jnp.zeros((Y4, 128), F32)
    first_loop(1, X4 + 1, g4, hd4, va4, 4)
    src, dst = va4, vb4
    for _ in range(5):
        relax_loop(1, X4, g4, hd4, src, writer(dst), 4, True)
        src, dst = dst, src
    double = matrix(128, 128, lambda r, l: l // 2 == r)
    twin_rows(t4, select(src[:, 1 : 1 + X4].reshape(2 * X4 * Y4, 128), double))

    def add3(k, _):
        for c in range(2):
            value = t4[pl.ds(pl.multiple_of((c * X4 + k) * Y3, Y3), Y3), :]
            vb3[c, PAD3 + 2 * k] = vb3[c, PAD3 + 2 * k] + value
            vb3[c, PAD3 + 2 * k + 1] = vb3[c, PAD3 + 2 * k + 1] + value
        return 0

    lax.fori_loop(0, X4, add3, 0)
    base = PAD3 + 2 * gx
    relax_loop(base - 3, 8, g3, hd3, vb3, writer(va3), 3, True)

    def write3(j, i, re, im):
        w3[0, j], w3[1, j] = re, im

    relax_loop(base - 2, 6, g3, hd3, va3, write3, 3, True)
    twin_rows(t3, select(w3[...].reshape(2 * 6 * Y3, 128), double))

    def start2(i, _):
        hd2[0, i], hd2[1, i] = half_inverse(a[2, i], 2)
        for c in range(2):
            row = pl.multiple_of((c * 6 + i // 2) * Y2, Y2)
            va2[c, i] = a[3 + c, i] + jnp.where(a[2, i] > 0.0, t3[pl.ds(row, Y2), :], 0.0)
        return 0

    lax.fori_loop(0, X2, start2, 0)
    relax_loop(1, X2 - 2, a, hd2, va2, writer(vb2), 2, True, True)
    w2[...] = jnp.zeros_like(w2)

    def write2(j, i, re, im):
        w2[0, j, 8 : 8 + Y2], w2[1, j, 8 : 8 + Y2] = re, im

    relax_loop(2, X2 - 4, a, hd2, vb2, write2, 2, True, True)
    rows = w2[:, :, pl.ds(4 * gy + 6, 8), :].reshape(2 * 8 * 8, 128)

    def place1(r, l):
        at = jnp.where(l < 96, l, l - 128)
        return r == 32 * gz + (at + 128) // 2 - 64

    twin_rows(t2, select(rows, matrix(128, 128, place1)))

    def start1(i, _):
        for c in range(2):
            row = pl.multiple_of((c * 8 + i // 2) * Y1, Y1)
            va1[c, i] = v21[c, i] + t2[pl.ds(row, Y1), :]
        return 0

    lax.fori_loop(1, X1 - 1, start1, 0)
    relax_loop(2, X1 - 4, g1, hd1, va1, writer(vb1), 1)
    relax_loop(3, X1 - 6, g1, hd1, vb1, writer(va1), 1)
    own = va1[:, 3:13].reshape(2 * 10 * Y1, 128)
    for half in range(2):
        place = matrix(128, 128, lambda r, l: r == (l + 128 * half) // 2)
        twin_rows(t1.at[half], select(own, place))

    def start0(k, _):
        for c in range(2):
            row = (c * 10 + k) * 32 + 4
            for half in range(2):
                lanes = slice(128 * half, 128 * half + 128)
                value = t1[half, pl.ds(row, Y0), :]
                for i in range(2):
                    va0[c, 2 * k + 1 + i, :, lanes] = v20[c, 2 * k + 1 + i, :, lanes] + value
        return 0

    lax.fori_loop(0, 10, start0, 0)
    relax_loop(2, X0 - 4, g0, hd0, va0, writer(vb0), 0)

    def write0(j, i, re, im):
        out[0, j], out[1, j] = re[4:20, 0:128], im[4:20, 0:128]

    relax_loop(3, X0 - 6, g0, hd0, vb0, write0, 0)


def call(kernel, outs, scratch, *args, limit=12, memory="", cost=None):
    memory = memory or "v" * (len(args) + len(outs))
    specs = [pl.BlockSpec(memory_space=pltpu.SMEM if m == "s" else pltpu.VMEM) for m in memory]
    return pl.pallas_call(
        kernel,
        out_shape=[jax.ShapeDtypeStruct(s, F32) for s in outs],
        in_specs=specs[: len(args)],
        out_specs=specs[len(args) :],
        scratch_shapes=[pltpu.VMEM(s, F32) for s in scratch],
        compiler_params=pltpu.CompilerParams(vmem_limit_bytes=limit << 20),
        cost_estimate=cost and pl.CostEstimate(cost[0], 0, cost[1]),
    )(*args)


def shift(block, axis, step):
    count = lax.axis_size(axis)
    pairs = [(i, i + step) for i in range(count) if 0 <= i + step < count]
    return lax.ppermute(block, axis, pairs)


def halos(own, hx):
    count, rows = own.shape[1], own.shape[2]
    ylo = shift(own[:, :, rows - 4 :], "gy", 1)
    yhi = shift(own[:, :, :4], "gy", -1)

    def edge(at):
        return jnp.concatenate([x[:, at : at + hx] for x in (ylo, own, yhi)], axis=2)

    return own, ylo, yhi, shift(edge(count - hx), "gx", 1), shift(edge(0), "gx", -1)


def everyone(block, axes):
    count = lax.axis_size(axes)
    return lax.all_to_all(jnp.broadcast_to(block, (count,) + block.shape), axes, 0, 0)


def shards(source_field, mach_number):
    own0 = jnp.concatenate([source_field, mach_number.astype(F32)[None]], axis=0)
    flat = (16, 3 * X0 * Y0)
    f0, low, high = call(gather0_kernel, [(3, X0, Y0, 128), flat, flat], [], *halos(own0, 3))
    full0, full1 = (X0, Y0, L0), (X1, Y1, L1)
    block0 = (f0, shift(high, "gz", 1), shift(low, "gz", -1))
    smoothed0 = [(3,) + full0] + [(2,) + full0] * 3
    (own1,) = call(
        down0_kernel, [(3, 8, 8, 128)], smoothed0 + [(2, 384, 128)], *block0
    )
    kept1, chunk2 = call(
        down1_kernel,
        [(7,) + full1, (5, 4, 128)],
        [(2,) + full1, (288, 128), (3, 6, 8, 128)] + [(2, 6, 8, 128)] * 3,
        *halos(own1, 4),
    )
    own2 = everyone(chunk2, ("gy", "gz"))
    a, chunk3 = call(
        down2_kernel,
        [(5, X2, Y2, 128), (48, 128)],
        [(4, Y2, 128), (2, 96, 128)],
        own2, shift(own2, "gx", 1), shift(own2, "gx", -1),
    )
    parts3 = everyone(chunk3, "gx")
    (kept0,) = call(keep0_kernel, [(7,) + full0], [(2,) + full0], *block0, cost=(60 << 20, 8 << 20))
    index = jnp.stack([lax.axis_index(n) for n in ("gx", "gy", "gz")]).astype(jnp.int32)
    wide3 = (X3 + 2 * PAD3, Y3, 128)
    wide4 = (X4 + 2, Y4, 128)
    scratch = [(3,) + wide3, (2,) + wide3, (2,) + wide3, (2,) + wide3, (3 * X4 * Y3, 128)]
    scratch += [(3,) + wide4, (2,) + wide4, (2,) + wide4, (2,) + wide4, (2 * X4 * Y3, 128)]
    scratch += [(2, 6, Y3, 128), (2 * 6 * Y2, 128)] + [(2, X2, Y2, 128)] * 3
    scratch += [(2, 8, Y2 + 16, 128), (2 * 8 * Y1, 128), (2,) + full1, (2,) + full1]
    scratch += [(2, 2 * 10 * 32, 128), (2,) + full0, (2,) + full0]
    return call(
        up_kernel,
        [(2, 16, 16, 128)],
        scratch,
        index, parts3, a, kept1, kept0,
        limit=16,
        memory="svvvvv",
    )[0]


def solution(mesh):
    return jax.shard_map(
        shards,
        mesh=mesh,
        in_specs=(P(None, "gx", "gy", "gz"), P("gx", "gy", "gz")),
        out_specs=P(None, "gx", "gy", "gz"),
        check_vma=False,
    )
```

```python
import functools

import jax
import jax.numpy as jnp
from jax import lax
from jax.experimental import pallas as pl
from jax.experimental.pallas import tpu as pltpu
from jax.sharding import PartitionSpec as P

F32, BF16 = jnp.float32, jnp.bfloat16
WAVE = 0.0625
DIAG_I = 0.5 * WAVE
MOST = (2, 5, 6, 8, 16)

X0, Y0, L0 = 22, 24, 256
HZ = 14
X1D, Y1D = 20, 24
X1, Y1, L1 = 16, 16, 128
X2D, Y2 = 8, 16
X2 = 12
X3, Y3, PAD3 = 32, 16, 4
X4, Y4 = 16, 8


def iota(shape, dim):
    return lax.broadcasted_iota(jnp.int32, shape, dim)


def split(x):
    high = x.astype(BF16)
    rest = x - high.astype(F32)
    middle = rest.astype(BF16)
    return high, middle, (rest - middle.astype(F32)).astype(BF16)


def select(x, matrix, dims=(((1,), (0,)), ((), ()))):
    parts = [lax.dot_general(p, matrix, dims, preferred_element_type=F32) for p in split(x)]
    return parts[0] + (parts[1] + parts[2])


def coefficients(mach, level):
    scale = 0.25**level
    axial = scale * (1.0 - mach * mach)
    advect = (0.25 * 0.5**level) * mach
    diagonal = 2.0 * axial + (4.0 * scale - WAVE)
    return axial, advect, diagonal


def half_inverse(mach, level):
    diagonal = coefficients(mach, level)[2]
    scale = 0.5 / (diagonal * diagonal + DIAG_I * DIAG_I)
    inside = mach > 0.0
    return jnp.where(inside, diagonal * scale, 0.0), jnp.where(inside, -DIAG_I * scale, 0.0)


def transverse(c, ymask, zmask):
    rows, lanes = c.shape
    north, south = pltpu.roll(c, rows - 1, 0), pltpu.roll(c, 1, 0)
    upper, lower = pltpu.roll(c, lanes - 1, 1), pltpu.roll(c, 1, 1)
    if ymask:
        at = iota(c.shape, 0)
        north = jnp.where(at == rows - 1, 0.0, north)
        south = jnp.where(at == 0, 0.0, south)
    if zmask:
        at = iota(c.shape, 1)
        upper = jnp.where(at == lanes - 1, 0.0, upper)
        lower = jnp.where(at == 0, 0.0, lower)
    return (north + south) + (upper + lower)


def balance(source, mach, v, i, level, ymask, zmask):
    axial, advect, diagonal = coefficients(mach, level)
    scale = 0.25**level
    c_r, c_i = v[0, i], v[1, i]
    e_r, w_r, e_i, w_i = v[0, i + 1], v[0, i - 1], v[1, i + 1], v[1, i - 1]
    t_r = axial * (e_r + w_r) - advect * (e_i - w_i)
    t_i = axial * (e_i + w_i) + advect * (e_r - w_r)
    if source is not None:
        t_r, t_i = t_r + source[0], t_i + source[1]
    return (
        t_r + scale * transverse(c_r, ymask, zmask),
        t_i + scale * transverse(c_i, ymask, zmask),
        c_r,
        c_i,
        diagonal,
    )


def blocks(count, most, compute, store):
    unit = max(u for u in range(1, most + 1) if count % u == 0)

    def body(k, _):
        steps = [k * unit + u for u in range(unit)]
        for j, value in zip(steps, [compute(j) for j in steps]):
            store(j, value)
        return 0

    if count == unit:
        body(0, 0)
    else:
        lax.fori_loop(0, count // unit, body, 0)


def first_loop(lo, hi, g, hd, v, level):
    def compute(j):
        i = lo + j
        h_r, h_i = half_inverse(g[2, i], level)
        g_r, g_i = g[0, i], g[1, i]
        return h_r, h_i, h_r * g_r - h_i * g_i, h_r * g_i + h_i * g_r

    def store(j, value):
        i = lo + j
        hd[0, i], hd[1, i], v[0, i], v[1, i] = value

    blocks(hi - lo, MOST[level], compute, store)


def relax_loop(lo, count, g, hd, v, write, level, ymask=False, zmask=False):
    def compute(j):
        i = lo + j
        t_r, t_i, c_r, c_i, _ = balance((g[0, i], g[1, i]), g[2, i], v, i, level, ymask, zmask)
        h_r, h_i = hd[0, i], hd[1, i]
        return 0.5 * c_r + (h_r * t_r - h_i * t_i), 0.5 * c_i + (h_r * t_i + h_i * t_r)

    blocks(count, MOST[level], compute, lambda j, value: write(j, lo + j, *value))


def free_loop(lo, count, coef, v, write, level):
    def compute(j):
        i = lo + j
        t_r, t_i, c_r, c_i, _ = balance(None, coef[0, i - 2], v, i, level, False, False)
        h_r, h_i = coef[1, i - 2], coef[2, i - 2]
        return 0.5 * c_r + (h_r * t_r - h_i * t_i), 0.5 * c_i + (h_r * t_i + h_i * t_r)

    blocks(count, MOST[level], compute, lambda j, value: write(j, lo + j, *value))


def writer(out):
    def write(j, i, re, im):
        out[0, i], out[1, i] = re, im

    return write


def residual(g, v, i, level, ymask=False, zmask=False):
    t_r, t_i, c_r, c_i, d = balance((g[0, i], g[1, i]), g[2, i], v, i, level, ymask, zmask)
    return t_r - (d * c_r - DIAG_I * c_i), t_i - (d * c_i + DIAG_I * c_r)


def residual_pair(g, v, i, level, ymask=False, zmask=False):
    a = residual(g, v, i, level, ymask, zmask)
    b = residual(g, v, i + 1, level, ymask, zmask)
    return a[0] + b[0], a[1] + b[1], g[2, i] + g[2, i + 1]


def pair_rows(ref, rows):
    return ref[pl.ds(0, rows // 2, stride=2), :] + ref[pl.ds(1, rows // 2, stride=2), :]


def twin_rows(ref, value):
    rows = value.shape[0]
    ref[pl.ds(0, rows, stride=2), :] = value
    ref[pl.ds(1, rows, stride=2), :] = value


def matrix(rows, lanes, rule, value=1.0):
    shape = (rows, lanes)
    return jnp.where(rule(iota(shape, 0), iota(shape, 1)), value, 0.0).astype(BF16)


def assemble(own, ylo, yhi, xlo, xhi, f):
    count, rows, hx, hy = own.shape[1], own.shape[2], xlo.shape[1], ylo.shape[2]
    for c in range(3):
        f[c, 0:hx] = xlo[c]
        f[c, hx : hx + count, 0:hy] = ylo[c]
        f[c, hx : hx + count, hy : hy + rows] = own[c]
        f[c, hx : hx + count, hy + rows :] = yhi[c]
        f[c, hx + count :] = xhi[c]


def gather0_kernel(own, ylo, yhi, xlo, xhi, f, low_lanes, high_lanes):
    assemble(own, ylo, yhi, xlo, xhi, f)
    parts = split(f[...].reshape(-1, 128))
    for out, start in ((low_lanes, 0), (high_lanes, 128 - HZ)):
        edge = matrix(16, 128, lambda r, l: (r < HZ) & (l == start + r))
        dims = (((1,), (1,)), ((), ()))
        terms = [lax.dot_general(edge, p, dims, preferred_element_type=F32) for p in parts]
        out[...] = terms[0] + (terms[1] + terms[2])


def smooth0(f, lower, upper, g, hd, v2, v1):
    both = jnp.concatenate([upper[...], lower[...]], axis=0)
    place = matrix(32, 128, lambda r, l: ((r < HZ) & (l == r)) | ((r >= 16) & (l == r + 112 - HZ)))
    tail = select(both, place, (((0,), (0,)), ((), ())))
    g[:, :, :, 0:128] = f[...]
    g[:, :, :, 128:256] = tail.reshape(3, X0, Y0, 128)
    first_loop(0, X0, g, hd, v1, 0)
    relax_loop(1, X0 - 2, g, hd, v1, writer(v2), 0)


def keep0_kernel(f, lower, upper, base, coef, g, hd, v2, v1):
    smooth0(f, lower, upper, g, hd, v2, v1)
    coef[0] = g[2, 2:20]
    coef[1:3] = hd[:, 2:20]
    relax_loop(2, X0 - 4, g, hd, v2, writer(v1), 0)

    def write(j, i, re, im):
        base[0, j], base[1, j] = re[4:20, 0:128], im[4:20, 0:128]

    relax_loop(3, X0 - 6, g, hd, v1, write, 0)


def down0_kernel(f, lower, upper, coarse, g, hd, v2, v1, sums):
    smooth0(f, lower, upper, g, hd, v2, v1)

    def store(k, parts):
        for c in range(3):
            row = pl.multiple_of((c * 8 + k) * 16, 16)
            for half in range(2):
                sums[half, pl.ds(row, 16), :] = parts[c][4:20, 128 * half : 128 * half + 128]

    blocks(8, 1, lambda k: residual_pair(g, v2, 3 + 2 * k, 0), store)
    own = matrix(128, 128, lambda r, l: r // 2 == l, 0.125)
    rest = matrix(
        128,
        128,
        lambda r, l: ((r < 12) | (r >= 116)) & (r // 2 + 64 == l),
        0.125,
    )
    total = select(pair_rows(sums.at[0], 384), own) + select(pair_rows(sums.at[1], 384), rest)
    coarse[...] = total.reshape(3, 8, 8, 128)


def smooth1(halos, g, hd, v2, v1):
    assemble(*halos, g)
    first_loop(0, X1D, g, hd, v1, 1)
    relax_loop(1, X1D - 2, g, hd, v1, writer(v2), 1)


def keep1_kernel(own, ylo, yhi, xlo, xhi, base, coef, g, hd, v2, v1):
    smooth1((own, ylo, yhi, xlo, xhi), g, hd, v2, v1)
    coef[0] = g[2, 4:16, 4:20]
    coef[1:3] = hd[:, 4:16, 4:20]
    relax_loop(4, X1D - 8, g, hd, v2, writer(v1), 1)

    def write(j, i, re, im):
        base[0, j], base[1, j] = re[4:20, :], im[4:20, :]

    relax_loop(5, X1D - 10, g, hd, v1, write, 1)


def down1_kernel(own, ylo, yhi, xlo, xhi, chunk, g, hd, v2, v1, sums, g2, hd2, va, vb):
    smooth1((own, ylo, yhi, xlo, xhi), g, hd, v2, v1)
    sums[...] = jnp.zeros_like(sums)

    def store(k, parts):
        for c in range(3):
            row = pl.multiple_of((c * X2D + k) * 2 * Y2, 2 * Y2)
            sums[pl.ds(row, Y1D), :] = parts[c]

    blocks(X2D, 2, lambda k: residual_pair(g, v2, 2 + 2 * k, 1), store)
    halve = matrix(
        128,
        128,
        lambda r, l: ((r < 68) & (r // 2 == l)) | ((r >= 124) & (r // 2 + 64 == l)),
        0.125,
    )
    g2[...] = select(pair_rows(sums, 6 * X2D * Y2), halve).reshape(3, X2D, Y2, 128)
    first_loop(0, X2D, g2, hd2, va, 2)
    relax_loop(1, X2D - 2, g2, hd2, va, writer(vb), 2)
    lane = iota((Y2, 128), 1) // 32
    for c in range(5):
        source = (lambda x: g2[c, x]) if c < 3 else (lambda x: vb[c - 3, x])
        total = source(2)
        for x in range(1, 4):
            total = jnp.where(lane == x, pltpu.roll(source(2 + x), 32 * x, 1), total)
        for half in range(2):
            rows = total[4 + 2 * half : 6 + 2 * half, :]
            chunk[:, 1 + 2 * c + half] = jnp.broadcast_to(rows, (32, 2, 128))
    pairs = [residual_pair(g2, vb, 2 + 2 * x, 2) for x in range(2)]
    for c in range(3):
        for x in range(2):
            row = (c * 2 + x) * Y2
            sums[row : row + Y2, :] = pairs[x][c]
    halve = matrix(128, 128, lambda r, l: (r < 32) & (r // 2 == l), 0.125)
    small = select(pair_rows(sums, 6 * Y2), halve)
    total = None
    for k in range(6):
        value = small[8 * k : 8 * k + 8, :]
        value = pltpu.roll(value, 16 * k, 1) if k else value
        total = value if total is None else total + value
    chunk[:, 0] = jnp.broadcast_to(total[2:4, :], (32, 2, 128))


def spread3_kernel(parts, chunk, planes):
    for gz in range(4):
        for gy in range(8):
            planes[gz, 2 * gy : 2 * gy + 2, :] = parts[gy * 4 + gz, 0]
    lane = iota((Y3, 128), 1) // 16
    for c in range(3):
        total = jnp.zeros((Y3, 128), F32)
        for x in range(2):
            for gz in range(4):
                at = 4 * x + gz
                step = (16 * (at - 2 * c - x)) % 128
                value = planes[gz]
                value = pltpu.roll(value, step, 1) if step else value
                total = jnp.where(lane == at, value, total)
        chunk[:, Y3 * c : Y3 * (c + 1), :] = jnp.broadcast_to(total, (16, Y3, 128))


def pick2_kernel(index, parts, sheet):
    for bz in range(3):
        for by in range(3):
            y, z = index[1] + (by - 1), index[2] + (bz - 1)
            inside = (y >= 0) & (y < 8) & (z >= 0) & (z < 4)
            at = jnp.clip(y, 0, 7) * 4 + jnp.clip(z, 0, 3)
            factor = jnp.where(inside, 1.0, 0.0)
            for c in range(5):
                for half in range(2):
                    rows = parts[at, 1 + 2 * c + half] * factor
                    sheet[(bz * 3 + by) * 5 + c, 2 * half : 2 * half + 2, :] = rows


def window2_kernel(west, own, east, a, planes):
    lane = iota((Y2, 128), 1) // 32
    planes[...] = jnp.zeros_like(planes)
    for bx, piece in enumerate((west, own, east)):

        def body(c, _):
            for bz in range(3):
                for by in range(3):
                    planes[bz, 4 * by : 4 * by + 4, :] = piece[(bz * 3 + by) * 5 + c]
            for x in range(4):
                total = jnp.zeros((Y2, 128), F32)
                for bz, group in enumerate((3, 0, 1)):
                    step = (32 * (group - x)) % 128
                    value = planes[bz]
                    value = pltpu.roll(value, step, 1) if step else value
                    total = jnp.where(lane == group, value, total)
                a[c, 4 * bx + x] = total
            return 0

        lax.fori_loop(0, 5, body, 0)


def up_kernel(
    index, parts3, a, base1, coef1, base0, coef0, out,
    g3, hd3, va3, vb3, s3, g4, hd4, va4, vb4, t4, w3, t3, hd2, va2, vb2, w2, t2, va1, vb1, t1, va0, vb0,
):
    gx, gy, gz = index[0], index[1], index[2]
    zero3 = jnp.zeros((Y3, 128), F32)
    for ref in (g3, hd3, va3, vb3):
        for c in range(ref.shape[0]):
            for i in range(PAD3):
                ref[c, i] = zero3
                ref[c, PAD3 + X3 + i] = zero3
    low = iota((Y3, 128), 1) < 64

    def spread(s, _):
        for c in range(3):
            value = parts3[s, Y3 * c : Y3 * (c + 1), :]
            g3[c, PAD3 + 2 * s] = jnp.where(low, value, 0.0)
            g3[c, PAD3 + 2 * s + 1] = jnp.where(low, pltpu.roll(value, 64, 1), 0.0)
        return 0

    lax.fori_loop(0, 16, spread, 0)
    first_loop(PAD3, PAD3 + X3, g3, hd3, va3, 3)
    relax_loop(PAD3, X3, g3, hd3, va3, writer(vb3), 3, True)

    def keep3(k, parts):
        for c in range(3):
            s3[pl.ds(pl.multiple_of((c * X4 + k) * Y3, Y3), Y3), :] = parts[c]

    blocks(X4, 4, lambda k: residual_pair(g3, vb3, PAD3 + 2 * k, 3, True), keep3)
    halve = matrix(128, 128, lambda r, l: (r // 2 == l) & (r < 64), 0.125)
    g4[:, 1 : 1 + X4] = select(pair_rows(s3, 3 * X4 * Y3), halve).reshape(3, X4, Y4, 128)
    for ref in (va4, vb4):
        for c in range(2):
            ref[c, 0] = jnp.zeros((Y4, 128), F32)
            ref[c, X4 + 1] = jnp.zeros((Y4, 128), F32)
    first_loop(1, X4 + 1, g4, hd4, va4, 4)
    src, dst = va4, vb4
    for _ in range(5):
        relax_loop(1, X4, g4, hd4, src, writer(dst), 4, True)
        src, dst = dst, src
    double = matrix(128, 128, lambda r, l: l // 2 == r)
    twin_rows(t4, select(src[:, 1 : 1 + X4].reshape(2 * X4 * Y4, 128), double))

    def add3(k, _):
        for c in range(2):
            value = t4[pl.ds(pl.multiple_of((c * X4 + k) * Y3, Y3), Y3), :]
            vb3[c, PAD3 + 2 * k] = vb3[c, PAD3 + 2 * k] + value
            vb3[c, PAD3 + 2 * k + 1] = vb3[c, PAD3 + 2 * k + 1] + value
        return 0

    lax.fori_loop(0, X4, add3, 0)
    base = PAD3 + 2 * gx
    relax_loop(base - 3, 8, g3, hd3, vb3, writer(va3), 3, True)

    w3[...] = jnp.zeros_like(w3)

    def write3(j, i, re, im):
        w3[0, j, 8 : 8 + Y3], w3[1, j, 8 : 8 + Y3] = re, im

    relax_loop(base - 2, 6, g3, hd3, va3, write3, 3, True)
    rows = w3[:, :, pl.ds(2 * gy + 6, 8), :].reshape(2 * 6 * 8, 128)

    def place2(r, l):
        at = jnp.where(l < 64, l, l - 128)
        return r == 16 * gz + (at + 128) // 2 - 64

    twin_rows(t3, select(rows, matrix(128, 128, place2)))

    def start2(i, _):
        hd2[0, i], hd2[1, i] = half_inverse(a[2, i], 2)
        for c in range(2):
            row = pl.multiple_of((c * 6 + i // 2) * Y2, Y2)
            va2[c, i] = a[3 + c, i] + jnp.where(a[2, i] > 0.0, t3[pl.ds(row, Y2), :], 0.0)
        return 0

    lax.fori_loop(0, X2, start2, 0)
    relax_loop(1, X2 - 2, a, hd2, va2, writer(vb2), 2)

    def write2(j, i, re, im):
        w2[0, j], w2[1, j] = re, im

    relax_loop(2, X2 - 4, a, hd2, vb2, write2, 2)
    double = matrix(128, 128, lambda r, l: jnp.where(l < 96, l // 2, l // 2 + 64) == r)
    twin_rows(t2, select(w2[:, :, 2:10, :].reshape(2 * 8 * 8, 128), double))

    def start1(i, _):
        for c in range(2):
            row = pl.multiple_of((c * 8 + i // 2) * Y1, Y1)
            va1[c, i] = t2[pl.ds(row, Y1), :]
        return 0

    lax.fori_loop(1, X1 - 1, start1, 0)
    free_loop(2, X1 - 4, coef1, va1, writer(vb1), 1)

    def write1(j, i, re, im):
        va1[0, i], va1[1, i] = base1[0, j] + re, base1[1, j] + im

    free_loop(3, X1 - 6, coef1, vb1, write1, 1)
    own = va1[:, 3:13].reshape(2 * 10 * Y1, 128)
    for half in range(2):
        place = matrix(128, 128, lambda r, l: r == (l + 128 * half) // 2)
        twin_rows(t1.at[half], select(own, place))

    def start0(k, _):
        for c in range(2):
            row = (c * 10 + k) * 32 + 4
            for half in range(2):
                lanes = slice(128 * half, 128 * half + 128)
                value = t1[half, pl.ds(row, Y0), :]
                for i in range(2):
                    va0[c, 2 * k + 1 + i, :, lanes] = value
        return 0

    lax.fori_loop(0, 10, start0, 0)
    free_loop(2, X0 - 4, coef0, va0, writer(vb0), 0)

    def write0(j, i, re, im):
        out[0, j] = base0[0, j] + re[4:20, 0:128]
        out[1, j] = base0[1, j] + im[4:20, 0:128]

    free_loop(3, X0 - 6, coef0, vb0, write0, 0)


def call(kernel, outs, scratch, *args, limit=12, memory="", cost=None):
    memory = memory or "v" * (len(args) + len(outs))
    specs = [pl.BlockSpec(memory_space=pltpu.SMEM if m == "s" else pltpu.VMEM) for m in memory]
    return pl.pallas_call(
        kernel,
        out_shape=[jax.ShapeDtypeStruct(s, F32) for s in outs],
        in_specs=specs[: len(args)],
        out_specs=specs[len(args) :],
        scratch_shapes=[pltpu.VMEM(s, F32) for s in scratch],
        compiler_params=pltpu.CompilerParams(vmem_limit_bytes=limit << 20),
        cost_estimate=cost and pl.CostEstimate(cost[0], 0, cost[1]),
    )(*args)


def shift(block, axis, step):
    count = lax.axis_size(axis)
    pairs = [(i, i + step) for i in range(count) if 0 <= i + step < count]
    return lax.ppermute(block, axis, pairs)


def halos(own, hx, hy):
    count, rows = own.shape[1], own.shape[2]
    ylo = shift(own[:, :, rows - hy :], "gy", 1)
    yhi = shift(own[:, :, :hy], "gy", -1)

    def edge(at):
        return jnp.concatenate([x[:, at : at + hx] for x in (ylo, own, yhi)], axis=2)

    return own, ylo, yhi, shift(edge(count - hx), "gx", 1), shift(edge(0), "gx", -1)


def around(block, axis):
    return shift(block, axis, 1), shift(block, axis, -1)


def shards(source_field, mach_number):
    own0 = jnp.concatenate([source_field, mach_number.astype(F32)[None]], axis=0)
    flat = (16, 3 * X0 * Y0)
    f0, low, high = call(gather0_kernel, [(3, X0, Y0, 128), flat, flat], [], *halos(own0, 3, 4))
    full0, full1 = (X0, Y0, L0), (X1, Y1, L1)
    block0 = (f0, shift(high, "gz", 1), shift(low, "gz", -1))
    smoothed0 = [(3,) + full0] + [(2,) + full0] * 3
    (own1,) = call(
        down0_kernel, [(3, 8, 8, 128)], smoothed0 + [(2, 384, 128)], *block0
    )
    wide1, wide2 = (X1D, Y1D, L1), (X2D, Y2, 128)
    block1 = halos(own1, 6, 8)
    smoothed1 = [(3,) + wide1] + [(2,) + wide1] * 3
    (chunk2,) = call(
        down1_kernel,
        [(32, 11, 2, 128)],
        smoothed1 + [(6 * X2D * Y2, 128), (3,) + wide2] + [(2,) + wide2] * 3,
        *block1,
    )
    parts2 = lax.all_to_all(chunk2, ("gy", "gz"), 0, 0)
    base0, coef0 = call(
        keep0_kernel,
        [(2, 16, 16, 128), (3, 18, Y0, L0)],
        smoothed0,
        *block0,
        cost=(60 << 20, 8 << 20),
    )
    base1, coef1 = call(
        keep1_kernel,
        [(2, 10, Y1, 128), (3, 12, Y1, 128)],
        smoothed1,
        *block1,
        cost=(8 << 20, 1 << 20),
    )
    parts2, *kept = lax.optimization_barrier((parts2, base1, coef1, base0, coef0))
    (chunk3,) = call(spread3_kernel, [(16, 48, 128)], [(4, Y3, 128)], parts2)
    parts3 = lax.all_to_all(chunk3, "gx", 0, 0)
    index = jnp.stack([lax.axis_index(n) for n in ("gx", "gy", "gz")]).astype(jnp.int32)
    (sheet,) = call(pick2_kernel, [(45, 4, 128)], [], index, parts2, memory="svv")
    west, east = around(sheet, "gx")
    (a,) = call(
        window2_kernel, [(5, X2, Y2, 128)], [(3, Y2, 128)], west, sheet, east, cost=(4 << 20, 1 << 20)
    )
    wide3 = (X3 + 2 * PAD3, Y3, 128)
    wide4 = (X4 + 2, Y4, 128)
    scratch = [(3,) + wide3, (2,) + wide3, (2,) + wide3, (2,) + wide3, (3 * X4 * Y3, 128)]
    scratch += [(3,) + wide4, (2,) + wide4, (2,) + wide4, (2,) + wide4, (2 * X4 * Y3, 128)]
    scratch += [(2, 6, Y3 + 16, 128), (2 * 6 * Y2, 128)] + [(2, X2, Y2, 128)] * 3
    scratch += [(2, 8, Y2, 128), (2 * 8 * Y1, 128), (2,) + full1, (2,) + full1]
    scratch += [(2, 2 * 10 * 32, 128), (2,) + full0, (2,) + full0]
    return call(
        up_kernel,
        [(2, 16, 16, 128)],
        scratch,
        index, parts3, a, *kept,
        limit=16,
        memory="svvvvvvv",
    )[0]


def solution(mesh):
    return jax.shard_map(
        shards,
        mesh=mesh,
        in_specs=(P(None, "gx", "gy", "gz"), P("gx", "gy", "gz")),
        out_specs=P(None, "gx", "gy", "gz"),
        check_vma=False,
    )
```

```python
import functools

import jax
import jax.numpy as jnp
from jax import lax
from jax.experimental import pallas as pl
from jax.experimental.pallas import tpu as pltpu
from jax.sharding import PartitionSpec as P

F32, BF16 = jnp.float32, jnp.bfloat16
WAVE = 0.0625
DIAG_I = 0.5 * WAVE
MOST = (11, 7, 6, 16, 16)

X0, Y0, L0 = 22, 24, 256
HZ = 14
X1D, Y1D = 20, 24
X1, Y1, L1 = 16, 16, 128
X2D, Y2 = 8, 16
X2 = 12
X3, Y3, PAD3 = 32, 16, 4
X4, Y4 = 16, 8


def iota(shape, dim):
    return lax.broadcasted_iota(jnp.int32, shape, dim)


def split(x):
    high = x.astype(BF16)
    rest = x - high.astype(F32)
    middle = rest.astype(BF16)
    return high, middle, (rest - middle.astype(F32)).astype(BF16)


def select(x, matrix, dims=(((1,), (0,)), ((), ()))):
    parts = [lax.dot_general(p, matrix, dims, preferred_element_type=F32) for p in split(x)]
    return parts[0] + (parts[1] + parts[2])


def coefficients(mach, level):
    scale = 0.25**level
    axial = scale * (1.0 - mach * mach)
    advect = (0.25 * 0.5**level) * mach
    diagonal = 2.0 * axial + (4.0 * scale - WAVE)
    return axial, advect, diagonal


def half_inverse(mach, level):
    diagonal = coefficients(mach, level)[2]
    scale = 0.5 / (diagonal * diagonal + DIAG_I * DIAG_I)
    inside = mach > 0.0
    return jnp.where(inside, diagonal * scale, 0.0), jnp.where(inside, -DIAG_I * scale, 0.0)


def transverse(c, ymask, zmask):
    rows, lanes = c.shape
    north, south = pltpu.roll(c, rows - 1, 0), pltpu.roll(c, 1, 0)
    upper, lower = pltpu.roll(c, lanes - 1, 1), pltpu.roll(c, 1, 1)
    if ymask:
        at = iota(c.shape, 0)
        north = jnp.where(at == rows - 1, 0.0, north)
        south = jnp.where(at == 0, 0.0, south)
    if zmask:
        at = iota(c.shape, 1)
        upper = jnp.where(at == lanes - 1, 0.0, upper)
        lower = jnp.where(at == 0, 0.0, lower)
    return (north + south) + (upper + lower)


def balance(source, mach, v, i, level, ymask, zmask):
    axial, advect, diagonal = coefficients(mach, level)
    scale = 0.25**level
    c_r, c_i = v[0, i], v[1, i]
    e_r, w_r, e_i, w_i = v[0, i + 1], v[0, i - 1], v[1, i + 1], v[1, i - 1]
    t_r = axial * (e_r + w_r) - advect * (e_i - w_i)
    t_i = axial * (e_i + w_i) + advect * (e_r - w_r)
    if source is not None:
        t_r, t_i = t_r + source[0], t_i + source[1]
    return (
        t_r + scale * transverse(c_r, ymask, zmask),
        t_i + scale * transverse(c_i, ymask, zmask),
        c_r,
        c_i,
        diagonal,
    )


def blocks(count, most, compute, store):
    unit = max(u for u in range(1, most + 1) if count % u == 0)

    def body(k, _):
        steps = [k * unit + u for u in range(unit)]
        for j, value in zip(steps, [compute(j) for j in steps]):
            store(j, value)
        return 0

    if count == unit:
        body(0, 0)
    else:
        lax.fori_loop(0, count // unit, body, 0)


def first_loop(lo, hi, g, hd, v, level):
    def compute(j):
        i = lo + j
        h_r, h_i = half_inverse(g[2, i], level)
        g_r, g_i = g[0, i], g[1, i]
        return h_r, h_i, h_r * g_r - h_i * g_i, h_r * g_i + h_i * g_r

    def store(j, value):
        i = lo + j
        hd[0, i], hd[1, i], v[0, i], v[1, i] = value

    blocks(hi - lo, MOST[level], compute, store)


def relax_loop(lo, count, g, hd, v, write, level, ymask=False, zmask=False, mach=None):
    mach = g.at[2] if mach is None else mach

    def compute(j):
        i = lo + j
        t_r, t_i, c_r, c_i, _ = balance((g[0, i], g[1, i]), mach[i], v, i, level, ymask, zmask)
        h_r, h_i = hd[0, i], hd[1, i]
        return 0.5 * c_r + (h_r * t_r - h_i * t_i), 0.5 * c_i + (h_r * t_i + h_i * t_r)

    blocks(count, MOST[level], compute, lambda j, value: write(j, lo + j, *value))


def free_loop(lo, count, coef, v, write, level):
    def compute(j):
        i = lo + j
        t_r, t_i, c_r, c_i, _ = balance(None, coef[0, i - 2], v, i, level, False, False)
        h_r, h_i = coef[1, i - 2], coef[2, i - 2]
        return 0.5 * c_r + (h_r * t_r - h_i * t_i), 0.5 * c_i + (h_r * t_i + h_i * t_r)

    blocks(count, MOST[level], compute, lambda j, value: write(j, lo + j, *value))


def writer(out):
    def write(j, i, re, im):
        out[0, i], out[1, i] = re, im

    return write


def residual(g, v, i, level, ymask=False, zmask=False):
    t_r, t_i, c_r, c_i, d = balance((g[0, i], g[1, i]), g[2, i], v, i, level, ymask, zmask)
    return t_r - (d * c_r - DIAG_I * c_i), t_i - (d * c_i + DIAG_I * c_r)


def residual_pair(g, v, i, level, ymask=False, zmask=False):
    a = residual(g, v, i, level, ymask, zmask)
    b = residual(g, v, i + 1, level, ymask, zmask)
    return a[0] + b[0], a[1] + b[1], g[2, i] + g[2, i + 1]


def pair_rows(ref, rows):
    return ref[pl.ds(0, rows // 2, stride=2), :] + ref[pl.ds(1, rows // 2, stride=2), :]


def twin_rows(ref, value):
    rows = value.shape[0]
    ref[pl.ds(0, rows, stride=2), :] = value
    ref[pl.ds(1, rows, stride=2), :] = value


def matrix(rows, lanes, rule, value=1.0):
    shape = (rows, lanes)
    return jnp.where(rule(iota(shape, 0), iota(shape, 1)), value, 0.0).astype(BF16)


def assemble(own, ylo, yhi, xlo, xhi, f):
    count, rows, hx, hy = own.shape[1], own.shape[2], xlo.shape[1], ylo.shape[2]
    for c in range(3):
        f[c, 0:hx] = xlo[c]
        f[c, hx : hx + count, 0:hy] = ylo[c]
        f[c, hx : hx + count, hy : hy + rows] = own[c]
        f[c, hx : hx + count, hy + rows :] = yhi[c]
        f[c, hx + count :] = xhi[c]


def start_kernel(source, mach, own, high, low):
    for c in range(3):
        own[c] = source[c] if c < 2 else mach[...].astype(F32)
        high[c], low[c] = own[c, :, 12:16], own[c, :, 0:4]


def gather0_kernel(own, ylo, yhi, xlo, xhi, f, low_lanes, high_lanes):
    assemble(own, ylo, yhi, xlo, xhi, f)
    parts = split(f[...].reshape(-1, 128))
    for out, start in ((low_lanes, 0), (high_lanes, 128 - HZ)):
        edge = matrix(16, 128, lambda r, l: (r < HZ) & (l == start + r))
        dims = (((1,), (1,)), ((), ()))
        terms = [lax.dot_general(edge, p, dims, preferred_element_type=F32) for p in parts]
        out[...] = terms[0] + (terms[1] + terms[2])


def smooth0(f, lower, upper, g, hd, v2, v1):
    both = jnp.concatenate([upper[...], lower[...]], axis=0)
    place = matrix(32, 128, lambda r, l: ((r < HZ) & (l == r)) | ((r >= 16) & (l == r + 112 - HZ)))
    tail = select(both, place, (((0,), (0,)), ((), ())))
    g[:, :, :, 0:128] = f[...]
    g[:, :, :, 128:256] = tail.reshape(3, X0, Y0, 128)
    first_loop(0, X0, g, hd, v1, 0)
    relax_loop(1, X0 - 2, g, hd, v1, writer(v2), 0)


def keep0_kernel(f, lower, upper, base, coef, g, hd, v2, v1):
    smooth0(f, lower, upper, g, hd, v2, v1)
    coef[0] = g[2, 2:20]
    coef[1:3] = hd[:, 2:20]
    relax_loop(2, X0 - 4, g, hd, v2, writer(v1), 0)

    def write(j, i, re, im):
        base[0, j], base[1, j] = re[4:20, 0:128], im[4:20, 0:128]

    relax_loop(3, X0 - 6, g, hd, v1, write, 0)


def down0_kernel(f, lower, upper, coarse, g, hd, v2, v1, sums):
    smooth0(f, lower, upper, g, hd, v2, v1)

    def store(k, parts):
        for c in range(3):
            row = pl.multiple_of((c * 8 + k) * 16, 16)
            for half in range(2):
                sums[half, pl.ds(row, 16), :] = parts[c][4:20, 128 * half : 128 * half + 128]

    blocks(8, 4, lambda k: residual_pair(g, v2, 3 + 2 * k, 0), store)
    own = matrix(128, 128, lambda r, l: r // 2 == l, 0.125)
    rest = matrix(
        128,
        128,
        lambda r, l: ((r < 12) | (r >= 116)) & (r // 2 + 64 == l),
        0.125,
    )
    total = select(pair_rows(sums.at[0], 384), own) + select(pair_rows(sums.at[1], 384), rest)
    coarse[...] = total.reshape(3, 8, 8, 128)


def smooth1(halos, g, hd, v2, v1):
    assemble(*halos, g)
    first_loop(0, X1D, g, hd, v1, 1)
    relax_loop(1, X1D - 2, g, hd, v1, writer(v2), 1)


def keep1_kernel(own, ylo, yhi, xlo, xhi, base, coef, mach2, g, hd, v2, v1, sums):
    smooth1((own, ylo, yhi, xlo, xhi), g, hd, v2, v1)
    coef[0] = g[2, 4:16, 4:20]
    coef[1:3] = hd[:, 4:16, 4:20]
    relax_loop(4, X1D - 8, g, hd, v2, writer(v1), 1)

    def write(j, i, re, im):
        base[0, j], base[1, j] = re[4:20, :], im[4:20, :]

    relax_loop(5, X1D - 10, g, hd, v1, write, 1)
    sums[...] = jnp.zeros_like(sums)
    for k in range(10):
        sums[2 * Y2 * k : 2 * Y2 * k + Y1D, :] = g[2, 2 * k] + g[2, 2 * k + 1]
    halve = matrix(
        128,
        128,
        lambda r, l: ((r < 70) & (r // 2 == l)) | ((r >= 122) & (r // 2 + 64 == l)),
        0.125,
    )
    mach2[0] = jnp.zeros((Y2, 128), F32)
    mach2[X2 - 1] = jnp.zeros((Y2, 128), F32)
    mach2[1 : X2 - 1] = select(pair_rows(sums, 20 * Y2), halve).reshape(10, Y2, 128)


def down1_kernel(own, ylo, yhi, xlo, xhi, chunk, g, hd, v2, v1, sums, g2, hd2, va, vb):
    smooth1((own, ylo, yhi, xlo, xhi), g, hd, v2, v1)
    sums[...] = jnp.zeros_like(sums)

    def store(k, parts):
        for c in range(3):
            row = pl.multiple_of((c * X2D + k) * 2 * Y2, 2 * Y2)
            sums[pl.ds(row, Y1D), :] = parts[c]

    blocks(X2D, 4, lambda k: residual_pair(g, v2, 2 + 2 * k, 1), store)
    halve = matrix(
        128,
        128,
        lambda r, l: ((r < 68) & (r // 2 == l)) | ((r >= 124) & (r // 2 + 64 == l)),
        0.125,
    )
    g2[...] = select(pair_rows(sums, 6 * X2D * Y2), halve).reshape(3, X2D, Y2, 128)
    first_loop(0, X2D, g2, hd2, va, 2)
    relax_loop(1, X2D - 2, g2, hd2, va, writer(vb), 2)
    lane = iota((Y2, 128), 1) // 32
    for c in range(4):
        source = (lambda x: g2[c, x]) if c < 2 else (lambda x: vb[c - 2, x])
        total = source(2)
        for x in range(1, 4):
            total = jnp.where(lane == x, pltpu.roll(source(2 + x), 32 * x, 1), total)
        for half in range(2):
            rows = total[4 + 2 * half : 6 + 2 * half, :]
            chunk[:, 1 + 2 * c + half] = jnp.broadcast_to(rows, (32, 2, 128))
    pairs = [residual_pair(g2, vb, 2 + 2 * x, 2) for x in range(2)]
    for c in range(3):
        for x in range(2):
            row = (c * 2 + x) * Y2
            sums[row : row + Y2, :] = pairs[x][c]
    halve = matrix(128, 128, lambda r, l: (r < 32) & (r // 2 == l), 0.125)
    small = select(pair_rows(sums, 6 * Y2), halve)
    total = None
    for k in range(6):
        value = small[8 * k : 8 * k + 8, :]
        value = pltpu.roll(value, 16 * k, 1) if k else value
        total = value if total is None else total + value
    chunk[:, 0] = jnp.broadcast_to(total[2:4, :], (32, 2, 128))


def spread3_kernel(parts, chunk, planes):
    for gz in range(4):
        for gy in range(8):
            planes[gz, 2 * gy : 2 * gy + 2, :] = parts[gy * 4 + gz, 0]
    lane = iota((Y3, 128), 1) // 16
    for c in range(3):
        total = jnp.zeros((Y3, 128), F32)
        for x in range(2):
            for gz in range(4):
                at = 4 * x + gz
                step = (16 * (at - 2 * c - x)) % 128
                value = planes[gz]
                value = pltpu.roll(value, step, 1) if step else value
                total = jnp.where(lane == at, value, total)
        chunk[:, Y3 * c : Y3 * (c + 1), :] = jnp.broadcast_to(total, (16, Y3, 128))


def pick2_kernel(index, parts, sheet):
    for bz in range(3):
        for by in range(3):
            y, z = index[1] + (by - 1), index[2] + (bz - 1)
            inside = (y >= 0) & (y < 8) & (z >= 0) & (z < 4)
            at = jnp.clip(y, 0, 7) * 4 + jnp.clip(z, 0, 3)
            factor = jnp.where(inside, 1.0, 0.0)
            for c in range(4):
                for half in range(2):
                    rows = parts[at, 1 + 2 * c + half] * factor
                    sheet[(bz * 3 + by) * 4 + c, 2 * half : 2 * half + 2, :] = rows


def window2_kernel(west, own, east, a, planes):
    lane = iota((Y2, 128), 1) // 32
    planes[...] = jnp.zeros_like(planes)
    for bx, piece in enumerate((west, own, east)):

        def body(c, _):
            for bz in range(3):
                for by in range(3):
                    planes[bz, 4 * by : 4 * by + 4, :] = piece[(bz * 3 + by) * 4 + c]
            for x in range(4):
                total = jnp.zeros((Y2, 128), F32)
                for bz, group in enumerate((3, 0, 1)):
                    step = (32 * (group - x)) % 128
                    value = planes[bz]
                    value = pltpu.roll(value, step, 1) if step else value
                    total = jnp.where(lane == group, value, total)
                a[c, 4 * bx + x] = total
            return 0

        lax.fori_loop(0, 4, body, 0)


def up_kernel(
    index, parts3, a, mach2, base1, coef1, base0, coef0, out,
    g3, hd3, va3, vb3, s3, g4, hd4, va4, vb4, t4, w3, t3, hd2, va2, vb2, w2, t2, va1, vb1, t1, va0, vb0,
):
    gx, gy, gz = index[0], index[1], index[2]
    zero3 = jnp.zeros((Y3, 128), F32)
    for ref in (g3, hd3, va3, vb3):
        for c in range(ref.shape[0]):
            for i in range(PAD3):
                ref[c, i] = zero3
                ref[c, PAD3 + X3 + i] = zero3
    low = iota((Y3, 128), 1) < 64

    def spread(s):
        values = [parts3[s, Y3 * c : Y3 * (c + 1), :] for c in range(3)]
        return [(jnp.where(low, v, 0.0), jnp.where(low, pltpu.roll(v, 64, 1), 0.0)) for v in values]

    def keep(s, values):
        for c in range(3):
            g3[c, PAD3 + 2 * s], g3[c, PAD3 + 2 * s + 1] = values[c]

    blocks(16, 4, spread, keep)
    first_loop(PAD3, PAD3 + X3, g3, hd3, va3, 3)
    relax_loop(PAD3, X3, g3, hd3, va3, writer(vb3), 3, True)

    def keep3(k, parts):
        for c in range(3):
            s3[pl.ds(pl.multiple_of((c * X4 + k) * Y3, Y3), Y3), :] = parts[c]

    blocks(X4, 8, lambda k: residual_pair(g3, vb3, PAD3 + 2 * k, 3, True), keep3)
    halve = matrix(128, 128, lambda r, l: (r // 2 == l) & (r < 64), 0.125)
    g4[:, 1 : 1 + X4] = select(pair_rows(s3, 3 * X4 * Y3), halve).reshape(3, X4, Y4, 128)
    for ref in (va4, vb4):
        for c in range(2):
            ref[c, 0] = jnp.zeros((Y4, 128), F32)
            ref[c, X4 + 1] = jnp.zeros((Y4, 128), F32)
    first_loop(1, X4 + 1, g4, hd4, va4, 4)
    src, dst = va4, vb4
    for _ in range(5):
        relax_loop(1, X4, g4, hd4, src, writer(dst), 4, True)
        src, dst = dst, src
    double = matrix(128, 128, lambda r, l: l // 2 == r)
    twin_rows(t4, select(src[:, 1 : 1 + X4].reshape(2 * X4 * Y4, 128), double))

    def add3(k):
        values = [t4[pl.ds(pl.multiple_of((c * X4 + k) * Y3, Y3), Y3), :] for c in range(2)]
        at = PAD3 + 2 * k
        return [(vb3[c, at] + values[c], vb3[c, at + 1] + values[c]) for c in range(2)]

    def put3(k, values):
        at = PAD3 + 2 * k
        for c in range(2):
            vb3[c, at], vb3[c, at + 1] = values[c]

    blocks(X4, 4, add3, put3)
    base = PAD3 + 2 * gx
    relax_loop(base - 3, 8, g3, hd3, vb3, writer(va3), 3, True)

    w3[...] = jnp.zeros_like(w3)

    def write3(j, i, re, im):
        w3[0, j, 8 : 8 + Y3], w3[1, j, 8 : 8 + Y3] = re, im

    relax_loop(base - 2, 6, g3, hd3, va3, write3, 3, True)
    rows = w3[:, :, pl.ds(2 * gy + 6, 8), :].reshape(2 * 6 * 8, 128)

    def place2(r, l):
        at = jnp.where(l < 64, l, l - 128)
        return r == 16 * gz + (at + 128) // 2 - 64

    twin_rows(t3, select(rows, matrix(128, 128, place2)))

    for i in range(X2):
        hd2[0, i], hd2[1, i] = half_inverse(mach2[i], 2)
        for c in range(2):
            row = (c * 6 + i // 2) * Y2
            va2[c, i] = a[2 + c, i] + t3[row : row + Y2, :]

    relax_loop(1, X2 - 2, a, hd2, va2, writer(vb2), 2, mach=mach2)

    def write2(j, i, re, im):
        w2[0, j], w2[1, j] = re, im

    relax_loop(2, X2 - 4, a, hd2, vb2, write2, 2, mach=mach2)
    double = matrix(128, 128, lambda r, l: jnp.where(l < 96, l // 2, l // 2 + 64) == r)
    twin_rows(t2, select(w2[:, :, 2:10, :].reshape(2 * 8 * 8, 128), double))

    for i in range(1, X1 - 1):
        for c in range(2):
            row = (c * 8 + i // 2) * Y1
            va1[c, i] = t2[row : row + Y1, :]

    free_loop(2, X1 - 4, coef1, va1, writer(vb1), 1)

    def write1(j, i, re, im):
        va1[0, i], va1[1, i] = base1[0, j] + re, base1[1, j] + im

    free_loop(3, X1 - 6, coef1, vb1, write1, 1)
    own = va1[:, 3:13].reshape(2 * 10 * Y1, 128)
    for half in range(2):
        place = matrix(128, 128, lambda r, l: r == (l + 128 * half) // 2)
        twin_rows(t1.at[half], select(own, place))

    def start0(k, _):
        for c in range(2):
            row = (c * 10 + k) * 32 + 4
            for half in range(2):
                lanes = slice(128 * half, 128 * half + 128)
                value = t1[half, pl.ds(row, Y0), :]
                for i in range(2):
                    va0[c, 2 * k + 1 + i, :, lanes] = value
        return 0

    lax.fori_loop(0, 10, start0, 0)
    free_loop(2, X0 - 4, coef0, va0, writer(vb0), 0)

    def write0(j, i, re, im):
        out[0, j] = base0[0, j] + re[4:20, 0:128]
        out[1, j] = base0[1, j] + im[4:20, 0:128]

    free_loop(3, X0 - 6, coef0, vb0, write0, 0)


def call(kernel, outs, scratch, *args, limit=12, memory="", cost=None):
    memory = memory or "v" * (len(args) + len(outs))
    specs = [pl.BlockSpec(memory_space=pltpu.SMEM if m == "s" else pltpu.VMEM) for m in memory]
    return pl.pallas_call(
        kernel,
        out_shape=[jax.ShapeDtypeStruct(s, F32) for s in outs],
        in_specs=specs[: len(args)],
        out_specs=specs[len(args) :],
        scratch_shapes=[pltpu.VMEM(s, F32) for s in scratch],
        compiler_params=pltpu.CompilerParams(vmem_limit_bytes=limit << 20),
        cost_estimate=cost and pl.CostEstimate(cost[0], 0, cost[1]),
    )(*args)


def shift(block, axis, step):
    count = lax.axis_size(axis)
    pairs = [(i, i + step) for i in range(count) if 0 <= i + step < count]
    return lax.ppermute(block, axis, pairs)


def halos(own, high, low, hx):
    count = own.shape[1]
    ylo, yhi = shift(high, "gy", 1), shift(low, "gy", -1)

    def edge(at):
        return jnp.concatenate([x[:, at : at + hx] for x in (ylo, own, yhi)], axis=2)

    return own, ylo, yhi, shift(edge(count - hx), "gx", 1), shift(edge(0), "gx", -1)


def around(block, axis):
    return shift(block, axis, 1), shift(block, axis, -1)


def shards(source_field, mach_number):
    edge = (3, 16, 4, 128)
    start = call(start_kernel, [(3, 16, 16, 128), edge, edge], [], source_field, mach_number)
    flat = (16, 3 * X0 * Y0)
    f0, low, high = call(gather0_kernel, [(3, X0, Y0, 128), flat, flat], [], *halos(*start, 3))
    full0, full1 = (X0, Y0, L0), (X1, Y1, L1)
    block0 = (f0, shift(high, "gz", 1), shift(low, "gz", -1))
    smoothed0 = [(3,) + full0] + [(2,) + full0] * 3
    (own1,) = call(
        down0_kernel, [(3, 8, 8, 128)], smoothed0 + [(2, 384, 128)], *block0
    )
    wide1, wide2 = (X1D, Y1D, L1), (X2D, Y2, 128)
    block1 = halos(own1, own1, own1, 6)
    smoothed1 = [(3,) + wide1] + [(2,) + wide1] * 3
    (chunk2,) = call(
        down1_kernel,
        [(32, 9, 2, 128)],
        smoothed1 + [(6 * X2D * Y2, 128), (3,) + wide2] + [(2,) + wide2] * 3,
        *block1,
    )
    parts2 = lax.all_to_all(chunk2, ("gy", "gz"), 0, 0)
    base0, coef0 = call(
        keep0_kernel,
        [(2, 16, 16, 128), (3, 18, Y0, L0)],
        smoothed0,
        *block0,
        cost=(60 << 20, 8 << 20),
    )
    base1, coef1, mach2 = call(
        keep1_kernel,
        [(2, 10, Y1, 128), (3, 12, Y1, 128), (X2, Y2, 128)],
        smoothed1 + [(20 * Y2, 128)],
        *block1,
        cost=(8 << 20, 1 << 20),
    )
    parts2, *kept = lax.optimization_barrier((parts2, mach2, base1, coef1, base0, coef0))
    (chunk3,) = call(spread3_kernel, [(16, 48, 128)], [(4, Y3, 128)], parts2)
    parts3 = lax.all_to_all(chunk3, "gx", 0, 0)
    index = jnp.stack([lax.axis_index(n) for n in ("gx", "gy", "gz")]).astype(jnp.int32)
    (sheet,) = call(pick2_kernel, [(36, 4, 128)], [], index, parts2, memory="svv")
    west, east = around(sheet, "gx")
    (a,) = call(
        window2_kernel, [(4, X2, Y2, 128)], [(3, Y2, 128)], west, sheet, east, cost=(4 << 20, 1 << 20)
    )
    wide3 = (X3 + 2 * PAD3, Y3, 128)
    wide4 = (X4 + 2, Y4, 128)
    scratch = [(3,) + wide3, (2,) + wide3, (2,) + wide3, (2,) + wide3, (3 * X4 * Y3, 128)]
    scratch += [(3,) + wide4, (2,) + wide4, (2,) + wide4, (2,) + wide4, (2 * X4 * Y3, 128)]
    scratch += [(2, 6, Y3 + 16, 128), (2 * 6 * Y2, 128)] + [(2, X2, Y2, 128)] * 3
    scratch += [(2, 8, Y2, 128), (2 * 8 * Y1, 128), (2,) + full1, (2,) + full1]
    scratch += [(2, 2 * 10 * 32, 128), (2,) + full0, (2,) + full0]
    return call(
        up_kernel,
        [(2, 16, 16, 128)],
        scratch,
        index, parts3, a, *kept,
        limit=16,
        memory="svvvvvvvv",
    )[0]


def solution(mesh):
    return jax.shard_map(
        shards,
        mesh=mesh,
        in_specs=(P(None, "gx", "gy", "gz"), P("gx", "gy", "gz")),
        out_specs=P(None, "gx", "gy", "gz"),
        check_vma=False,
    )
```

```python
import functools

import jax
import jax.numpy as jnp
from jax import lax
from jax.experimental import pallas as pl
from jax.experimental.pallas import tpu as pltpu
from jax.sharding import PartitionSpec as P

F32, BF16 = jnp.float32, jnp.bfloat16
WAVE = 0.0625
DIAG_I = 0.5 * WAVE
MOST = (11, 7, 6, 16, 16)

X0, Y0, L0 = 22, 24, 256
HZ = 14
X1D, Y1D = 20, 24
X1, Y1, L1 = 16, 16, 128
X2D, Y2 = 8, 16
X2 = 12
X3, Y3, PAD3 = 32, 16, 4
X4, Y4 = 16, 8


def iota(shape, dim):
    return lax.broadcasted_iota(jnp.int32, shape, dim)


def split(x):
    high = x.astype(BF16)
    rest = x - high.astype(F32)
    middle = rest.astype(BF16)
    return high, middle, (rest - middle.astype(F32)).astype(BF16)


def select(x, matrix, dims=(((1,), (0,)), ((), ()))):
    parts = [lax.dot_general(p, matrix, dims, preferred_element_type=F32) for p in split(x)]
    return parts[0] + (parts[1] + parts[2])


def coefficients(mach, level):
    scale = 0.25**level
    axial = scale * (1.0 - mach * mach)
    advect = (0.25 * 0.5**level) * mach
    diagonal = 2.0 * axial + (4.0 * scale - WAVE)
    return axial, advect, diagonal


def half_inverse(mach, level):
    diagonal = coefficients(mach, level)[2]
    scale = 0.5 / (diagonal * diagonal + DIAG_I * DIAG_I)
    inside = mach > 0.0
    return jnp.where(inside, diagonal * scale, 0.0), jnp.where(inside, -DIAG_I * scale, 0.0)


def transverse(c, ymask, zmask):
    rows, lanes = c.shape
    north, south = pltpu.roll(c, rows - 1, 0), pltpu.roll(c, 1, 0)
    upper, lower = pltpu.roll(c, lanes - 1, 1), pltpu.roll(c, 1, 1)
    if ymask:
        at = iota(c.shape, 0)
        north = jnp.where(at == rows - 1, 0.0, north)
        south = jnp.where(at == 0, 0.0, south)
    if zmask:
        at = iota(c.shape, 1)
        upper = jnp.where(at == lanes - 1, 0.0, upper)
        lower = jnp.where(at == 0, 0.0, lower)
    return (north + south) + (upper + lower)


def balance(source, mach, v, i, level, ymask, zmask):
    axial, advect, diagonal = coefficients(mach, level)
    scale = 0.25**level
    c_r, c_i = v[0, i], v[1, i]
    e_r, w_r, e_i, w_i = v[0, i + 1], v[0, i - 1], v[1, i + 1], v[1, i - 1]
    t_r = axial * (e_r + w_r) - advect * (e_i - w_i)
    t_i = axial * (e_i + w_i) + advect * (e_r - w_r)
    if source is not None:
        t_r, t_i = t_r + source[0], t_i + source[1]
    return (
        t_r + scale * transverse(c_r, ymask, zmask),
        t_i + scale * transverse(c_i, ymask, zmask),
        c_r,
        c_i,
        diagonal,
    )


def blocks(count, most, compute, store):
    unit = max(u for u in range(1, most + 1) if count % u == 0)

    def body(k, _):
        steps = [k * unit + u for u in range(unit)]
        for j, value in zip(steps, [compute(j) for j in steps]):
            store(j, value)
        return 0

    if count == unit:
        body(0, 0)
    else:
        lax.fori_loop(0, count // unit, body, 0)


def first_loop(lo, hi, g, hd, v, level):
    def compute(j):
        i = lo + j
        h_r, h_i = half_inverse(g[2, i], level)
        g_r, g_i = g[0, i], g[1, i]
        return h_r, h_i, h_r * g_r - h_i * g_i, h_r * g_i + h_i * g_r

    def store(j, value):
        i = lo + j
        hd[0, i], hd[1, i], v[0, i], v[1, i] = value

    blocks(hi - lo, MOST[level], compute, store)


def relax_loop(lo, count, g, hd, v, write, level, ymask=False, zmask=False, mach=None):
    mach = g.at[2] if mach is None else mach

    def compute(j):
        i = lo + j
        t_r, t_i, c_r, c_i, _ = balance((g[0, i], g[1, i]), mach[i], v, i, level, ymask, zmask)
        h_r, h_i = hd[0, i], hd[1, i]
        return 0.5 * c_r + (h_r * t_r - h_i * t_i), 0.5 * c_i + (h_r * t_i + h_i * t_r)

    blocks(count, MOST[level], compute, lambda j, value: write(j, lo + j, *value))


def free_loop(lo, count, coef, v, write, level):
    def compute(j):
        i = lo + j
        t_r, t_i, c_r, c_i, _ = balance(None, coef[0, i - 2], v, i, level, False, False)
        h_r, h_i = coef[1, i - 2], coef[2, i - 2]
        return 0.5 * c_r + (h_r * t_r - h_i * t_i), 0.5 * c_i + (h_r * t_i + h_i * t_r)

    blocks(count, MOST[level], compute, lambda j, value: write(j, lo + j, *value))


def writer(out):
    def write(j, i, re, im):
        out[0, i], out[1, i] = re, im

    return write


def residual(g, v, i, level, ymask=False, zmask=False):
    t_r, t_i, c_r, c_i, d = balance((g[0, i], g[1, i]), g[2, i], v, i, level, ymask, zmask)
    return t_r - (d * c_r - DIAG_I * c_i), t_i - (d * c_i + DIAG_I * c_r)


def residual_pair(g, v, i, level, ymask=False, zmask=False):
    a = residual(g, v, i, level, ymask, zmask)
    b = residual(g, v, i + 1, level, ymask, zmask)
    return a[0] + b[0], a[1] + b[1], g[2, i] + g[2, i + 1]


def pair_rows(ref, rows):
    return ref[pl.ds(0, rows // 2, stride=2), :] + ref[pl.ds(1, rows // 2, stride=2), :]


def twin_rows(ref, value):
    rows = value.shape[0]
    ref[pl.ds(0, rows, stride=2), :] = value
    ref[pl.ds(1, rows, stride=2), :] = value


def matrix(rows, lanes, rule, value=1.0):
    shape = (rows, lanes)
    return jnp.where(rule(iota(shape, 0), iota(shape, 1)), value, 0.0).astype(BF16)


def ends():
    at = lax.axis_index("gx")
    return jnp.where(at > 0, 1.0, 0.0), jnp.where(at < 15, 1.0, 0.0)


def assemble(own, ylo, yhi, xlo, xhi, f):
    count, rows, hx, hy = own.shape[1], own.shape[2], xlo.shape[1], ylo.shape[2]
    low, high = ends()
    for c in range(3):
        f[c, 0:hx] = xlo[c] if c < 2 else xlo[c] * low
        f[c, hx : hx + count, 0:hy] = ylo[c]
        f[c, hx : hx + count, hy : hy + rows] = own[c]
        f[c, hx : hx + count, hy + rows :] = yhi[c]
        f[c, hx + count :] = xhi[c] if c < 2 else xhi[c] * high


def start_kernel(source, mach, own, high, low):
    for c in range(3):
        own[c] = source[c] if c < 2 else mach[...].astype(F32)
        high[c], low[c] = own[c, :, 12:16], own[c, :, 0:4]


def gather0_kernel(own, ylo, yhi, xlo, xhi, f, low_lanes, high_lanes):
    assemble(own, ylo, yhi, xlo, xhi, f)
    parts = split(f[...].reshape(-1, 128))
    for out, start in ((low_lanes, 0), (high_lanes, 128 - HZ)):
        edge = matrix(16, 128, lambda r, l: (r < HZ) & (l == start + r))
        dims = (((1,), (1,)), ((), ()))
        terms = [lax.dot_general(edge, p, dims, preferred_element_type=F32) for p in parts]
        out[...] = terms[0] + (terms[1] + terms[2])


def smooth0(f, lower, upper, g, hd, v2, v1):
    both = jnp.concatenate([upper[...], lower[...]], axis=0)
    place = matrix(32, 128, lambda r, l: ((r < HZ) & (l == r)) | ((r >= 16) & (l == r + 112 - HZ)))
    tail = select(both, place, (((0,), (0,)), ((), ())))
    g[:, :, :, 0:128] = f[...]
    g[:, :, :, 128:256] = tail.reshape(3, X0, Y0, 128)
    first_loop(0, X0, g, hd, v1, 0)
    relax_loop(1, X0 - 2, g, hd, v1, writer(v2), 0)


def keep0_kernel(f, lower, upper, base, coef, g, hd, v2, v1):
    smooth0(f, lower, upper, g, hd, v2, v1)
    coef[0] = g[2, 2:20]
    coef[1:3] = hd[:, 2:20]
    relax_loop(2, X0 - 4, g, hd, v2, writer(v1), 0)

    def write(j, i, re, im):
        base[0, j], base[1, j] = re[4:20, 0:128], im[4:20, 0:128]

    relax_loop(3, X0 - 6, g, hd, v1, write, 0)


def down0_kernel(f, lower, upper, coarse, g, hd, v2, v1, sums):
    smooth0(f, lower, upper, g, hd, v2, v1)

    def store(k, parts):
        for c in range(3):
            row = pl.multiple_of((c * 8 + k) * 16, 16)
            for half in range(2):
                sums[half, pl.ds(row, 16), :] = parts[c][4:20, 128 * half : 128 * half + 128]

    blocks(8, 4, lambda k: residual_pair(g, v2, 3 + 2 * k, 0), store)
    own = matrix(128, 128, lambda r, l: r // 2 == l, 0.125)
    rest = matrix(
        128,
        128,
        lambda r, l: ((r < 12) | (r >= 116)) & (r // 2 + 64 == l),
        0.125,
    )
    total = select(pair_rows(sums.at[0], 384), own) + select(pair_rows(sums.at[1], 384), rest)
    coarse[...] = total.reshape(3, 8, 8, 128)


def smooth1(halos, g, hd, v2, v1):
    assemble(*halos, g)
    first_loop(0, X1D, g, hd, v1, 1)
    relax_loop(1, X1D - 2, g, hd, v1, writer(v2), 1)


def keep1_kernel(own, ylo, yhi, xlo, xhi, base, coef, mach2, g, hd, v2, v1, sums):
    smooth1((own, ylo, yhi, xlo, xhi), g, hd, v2, v1)
    coef[0] = g[2, 4:16, 4:20]
    coef[1:3] = hd[:, 4:16, 4:20]
    relax_loop(4, X1D - 8, g, hd, v2, writer(v1), 1)

    def write(j, i, re, im):
        base[0, j], base[1, j] = re[4:20, :], im[4:20, :]

    relax_loop(5, X1D - 10, g, hd, v1, write, 1)
    sums[...] = jnp.zeros_like(sums)
    for k in range(10):
        sums[2 * Y2 * k : 2 * Y2 * k + Y1D, :] = g[2, 2 * k] + g[2, 2 * k + 1]
    halve = matrix(
        128,
        128,
        lambda r, l: ((r < 70) & (r // 2 == l)) | ((r >= 122) & (r // 2 + 64 == l)),
        0.125,
    )
    mach2[0] = jnp.zeros((Y2, 128), F32)
    mach2[X2 - 1] = jnp.zeros((Y2, 128), F32)
    mach2[1 : X2 - 1] = select(pair_rows(sums, 20 * Y2), halve).reshape(10, Y2, 128)


def down1_kernel(own, ylo, yhi, xlo, xhi, chunk, g, hd, v2, v1, sums, g2, hd2, va, vb):
    smooth1((own, ylo, yhi, xlo, xhi), g, hd, v2, v1)
    sums[...] = jnp.zeros_like(sums)

    def store(k, parts):
        for c in range(3):
            row = pl.multiple_of((c * X2D + k) * 2 * Y2, 2 * Y2)
            sums[pl.ds(row, Y1D), :] = parts[c]

    blocks(X2D, 4, lambda k: residual_pair(g, v2, 2 + 2 * k, 1), store)
    halve = matrix(
        128,
        128,
        lambda r, l: ((r < 68) & (r // 2 == l)) | ((r >= 124) & (r // 2 + 64 == l)),
        0.125,
    )
    g2[...] = select(pair_rows(sums, 6 * X2D * Y2), halve).reshape(3, X2D, Y2, 128)
    first_loop(0, X2D, g2, hd2, va, 2)
    relax_loop(1, X2D - 2, g2, hd2, va, writer(vb), 2)
    lane = iota((Y2, 128), 1) // 32
    for c in range(4):
        source = (lambda x: g2[c, x]) if c < 2 else (lambda x: vb[c - 2, x])
        total = source(2)
        for x in range(1, 4):
            total = jnp.where(lane == x, pltpu.roll(source(2 + x), 32 * x, 1), total)
        for half in range(2):
            rows = total[4 + 2 * half : 6 + 2 * half, :]
            chunk[:, 1 + 2 * c + half] = jnp.broadcast_to(rows, (32, 2, 128))
    pairs = [residual_pair(g2, vb, 2 + 2 * x, 2) for x in range(2)]
    for c in range(3):
        for x in range(2):
            row = (c * 2 + x) * Y2
            sums[row : row + Y2, :] = pairs[x][c]
    halve = matrix(128, 128, lambda r, l: (r < 32) & (r // 2 == l), 0.125)
    small = select(pair_rows(sums, 6 * Y2), halve)
    total = None
    for k in range(6):
        value = small[8 * k : 8 * k + 8, :]
        value = pltpu.roll(value, 16 * k, 1) if k else value
        total = value if total is None else total + value
    chunk[:, 0] = jnp.broadcast_to(total[2:4, :], (32, 2, 128))


def spread3_kernel(parts, chunk, planes):
    for gz in range(4):
        for gy in range(8):
            planes[gz, 2 * gy : 2 * gy + 2, :] = parts[gy * 4 + gz, 0]
    lane = iota((Y3, 128), 1) // 16
    for c in range(3):
        total = jnp.zeros((Y3, 128), F32)
        for x in range(2):
            for gz in range(4):
                at = 4 * x + gz
                step = (16 * (at - 2 * c - x)) % 128
                value = planes[gz]
                value = pltpu.roll(value, step, 1) if step else value
                total = jnp.where(lane == at, value, total)
        chunk[:, Y3 * c : Y3 * (c + 1), :] = jnp.broadcast_to(total, (16, Y3, 128))


def pick2_kernel(parts, sheet):
    for bz in range(3):
        for by in range(3):
            y, z = lax.axis_index("gy") + (by - 1), lax.axis_index("gz") + (bz - 1)
            inside = (y >= 0) & (y < 8) & (z >= 0) & (z < 4)
            at = jnp.clip(y, 0, 7) * 4 + jnp.clip(z, 0, 3)
            factor = jnp.where(inside, 1.0, 0.0)
            for c in range(4):
                for half in range(2):
                    rows = parts[at, 1 + 2 * c + half] * factor
                    sheet[(bz * 3 + by) * 4 + c, 2 * half : 2 * half + 2, :] = rows


def window2_kernel(west, own, east, a, planes):
    lane = iota((Y2, 128), 1) // 32
    planes[...] = jnp.zeros_like(planes)
    low, high = ends()
    for bx, piece in enumerate((west, own, east)):
        factor = (low, None, high)[bx]

        def body(c, _):
            for bz in range(3):
                for by in range(3):
                    planes[bz, 4 * by : 4 * by + 4, :] = piece[(bz * 3 + by) * 4 + c]
            for x in range(4):
                total = jnp.zeros((Y2, 128), F32)
                for bz, group in enumerate((3, 0, 1)):
                    step = (32 * (group - x)) % 128
                    value = planes[bz]
                    value = pltpu.roll(value, step, 1) if step else value
                    total = jnp.where(lane == group, value, total)
                a[c, 4 * bx + x] = total if factor is None else total * factor
            return 0

        lax.fori_loop(0, 4, body, 0)


def up_kernel(
    parts3, a, mach2, base1, coef1, base0, coef0, out,
    g3, hd3, va3, vb3, s3, g4, hd4, va4, vb4, t4, w3, t3, hd2, va2, vb2, w2, t2, va1, vb1, t1, va0, vb0,
):
    gx, gy, gz = (lax.axis_index(n) for n in ("gx", "gy", "gz"))
    zero3 = jnp.zeros((Y3, 128), F32)
    for ref in (g3, hd3, va3, vb3):
        for c in range(ref.shape[0]):
            for i in range(PAD3):
                ref[c, i] = zero3
                ref[c, PAD3 + X3 + i] = zero3
    low = iota((Y3, 128), 1) < 64

    def spread(s):
        values = [parts3[s, Y3 * c : Y3 * (c + 1), :] for c in range(3)]
        return [(jnp.where(low, v, 0.0), jnp.where(low, pltpu.roll(v, 64, 1), 0.0)) for v in values]

    def keep(s, values):
        for c in range(3):
            g3[c, PAD3 + 2 * s], g3[c, PAD3 + 2 * s + 1] = values[c]

    blocks(16, 4, spread, keep)
    first_loop(PAD3, PAD3 + X3, g3, hd3, va3, 3)
    relax_loop(PAD3, X3, g3, hd3, va3, writer(vb3), 3, True)

    def keep3(k, parts):
        for c in range(3):
            s3[pl.ds(pl.multiple_of((c * X4 + k) * Y3, Y3), Y3), :] = parts[c]

    blocks(X4, 8, lambda k: residual_pair(g3, vb3, PAD3 + 2 * k, 3, True), keep3)
    halve = matrix(128, 128, lambda r, l: (r // 2 == l) & (r < 64), 0.125)
    g4[:, 1 : 1 + X4] = select(pair_rows(s3, 3 * X4 * Y3), halve).reshape(3, X4, Y4, 128)
    for ref in (va4, vb4):
        for c in range(2):
            ref[c, 0] = jnp.zeros((Y4, 128), F32)
            ref[c, X4 + 1] = jnp.zeros((Y4, 128), F32)
    first_loop(1, X4 + 1, g4, hd4, va4, 4)
    src, dst = va4, vb4
    for _ in range(5):
        relax_loop(1, X4, g4, hd4, src, writer(dst), 4, True)
        src, dst = dst, src
    double = matrix(128, 128, lambda r, l: l // 2 == r)
    twin_rows(t4, select(src[:, 1 : 1 + X4].reshape(2 * X4 * Y4, 128), double))

    def add3(k):
        values = [t4[pl.ds(pl.multiple_of((c * X4 + k) * Y3, Y3), Y3), :] for c in range(2)]
        at = PAD3 + 2 * k
        return [(vb3[c, at] + values[c], vb3[c, at + 1] + values[c]) for c in range(2)]

    def put3(k, values):
        at = PAD3 + 2 * k
        for c in range(2):
            vb3[c, at], vb3[c, at + 1] = values[c]

    blocks(X4, 4, add3, put3)
    base = PAD3 + 2 * gx
    relax_loop(base - 3, 8, g3, hd3, vb3, writer(va3), 3, True)

    w3[...] = jnp.zeros_like(w3)

    def write3(j, i, re, im):
        w3[0, j, 8 : 8 + Y3], w3[1, j, 8 : 8 + Y3] = re, im

    relax_loop(base - 2, 6, g3, hd3, va3, write3, 3, True)
    rows = w3[:, :, pl.ds(2 * gy + 6, 8), :].reshape(2 * 6 * 8, 128)

    def place2(r, l):
        at = jnp.where(l < 64, l, l - 128)
        return r == 16 * gz + (at + 128) // 2 - 64

    twin_rows(t3, select(rows, matrix(128, 128, place2)))

    for i in range(X2):
        hd2[0, i], hd2[1, i] = half_inverse(mach2[i], 2)
        for c in range(2):
            row = (c * 6 + i // 2) * Y2
            va2[c, i] = a[2 + c, i] + t3[row : row + Y2, :]

    relax_loop(1, X2 - 2, a, hd2, va2, writer(vb2), 2, mach=mach2)

    def write2(j, i, re, im):
        w2[0, j], w2[1, j] = re, im

    relax_loop(2, X2 - 4, a, hd2, vb2, write2, 2, mach=mach2)
    double = matrix(128, 128, lambda r, l: jnp.where(l < 96, l // 2, l // 2 + 64) == r)
    twin_rows(t2, select(w2[:, :, 2:10, :].reshape(2 * 8 * 8, 128), double))

    for i in range(1, X1 - 1):
        for c in range(2):
            row = (c * 8 + i // 2) * Y1
            va1[c, i] = t2[row : row + Y1, :]

    free_loop(2, X1 - 4, coef1, va1, writer(vb1), 1)

    def write1(j, i, re, im):
        va1[0, i], va1[1, i] = base1[0, j] + re, base1[1, j] + im

    free_loop(3, X1 - 6, coef1, vb1, write1, 1)
    own = va1[:, 3:13].reshape(2 * 10 * Y1, 128)
    for half in range(2):
        place = matrix(128, 128, lambda r, l: r == (l + 128 * half) // 2)
        twin_rows(t1.at[half], select(own, place))

    def start0(k, _):
        for c in range(2):
            row = (c * 10 + k) * 32 + 4
            for half in range(2):
                lanes = slice(128 * half, 128 * half + 128)
                value = t1[half, pl.ds(row, Y0), :]
                for i in range(2):
                    va0[c, 2 * k + 1 + i, :, lanes] = value
        return 0

    lax.fori_loop(0, 10, start0, 0)
    free_loop(2, X0 - 4, coef0, va0, writer(vb0), 0)

    def write0(j, i, re, im):
        out[0, j] = base0[0, j] + re[4:20, 0:128]
        out[1, j] = base0[1, j] + im[4:20, 0:128]

    free_loop(3, X0 - 6, coef0, vb0, write0, 0)


def call(kernel, outs, scratch, *args, limit=12, cost=None):
    spec = pl.BlockSpec(memory_space=pltpu.VMEM)
    return pl.pallas_call(
        kernel,
        out_shape=[jax.ShapeDtypeStruct(s, F32) for s in outs],
        in_specs=[spec] * len(args),
        out_specs=[spec] * len(outs),
        scratch_shapes=[pltpu.VMEM(s, F32) for s in scratch],
        compiler_params=pltpu.CompilerParams(vmem_limit_bytes=limit << 20),
        cost_estimate=cost and pl.CostEstimate(cost[0], 0, cost[1]),
    )(*args)


def shift(block, axis, step):
    count = lax.axis_size(axis)
    pairs = [(i, (i + step) % count) for i in range(count)]
    if axis != "gx":
        pairs = [(i, j) for i, j in pairs if j == i + step]
    return lax.ppermute(block, axis, pairs)


def halos(own, high, low, hx):
    count = own.shape[1]
    ylo, yhi = shift(high, "gy", 1), shift(low, "gy", -1)

    def edge(at):
        return jnp.concatenate([x[:, at : at + hx] for x in (ylo, own, yhi)], axis=2)

    return own, ylo, yhi, shift(edge(count - hx), "gx", 1), shift(edge(0), "gx", -1)


def around(block, axis):
    return shift(block, axis, 1), shift(block, axis, -1)


def shards(source_field, mach_number):
    edge = (3, 16, 4, 128)
    start = call(start_kernel, [(3, 16, 16, 128), edge, edge], [], source_field, mach_number)
    flat = (16, 3 * X0 * Y0)
    f0, low, high = call(
        gather0_kernel,
        [(3, X0, Y0, 128), flat, flat],
        [],
        *halos(*start, 3),
    )
    full0, full1 = (X0, Y0, L0), (X1, Y1, L1)
    block0 = (f0, shift(high, "gz", 1), shift(low, "gz", -1))
    smoothed0 = [(3,) + full0] + [(2,) + full0] * 3
    (own1,) = call(
        down0_kernel, [(3, 8, 8, 128)], smoothed0 + [(2, 384, 128)], *block0
    )
    wide1, wide2 = (X1D, Y1D, L1), (X2D, Y2, 128)
    block1 = halos(own1, own1, own1, 6)
    smoothed1 = [(3,) + wide1] + [(2,) + wide1] * 3
    (chunk2,) = call(
        down1_kernel,
        [(32, 9, 2, 128)],
        smoothed1 + [(6 * X2D * Y2, 128), (3,) + wide2] + [(2,) + wide2] * 3,
        *block1,
    )
    parts2 = lax.all_to_all(chunk2, ("gy", "gz"), 0, 0)
    base0, coef0 = call(
        keep0_kernel,
        [(2, 16, 16, 128), (3, 18, Y0, L0)],
        smoothed0,
        *block0,
        cost=(60 << 20, 8 << 20),
    )
    base1, coef1, mach2 = call(
        keep1_kernel,
        [(2, 10, Y1, 128), (3, 12, Y1, 128), (X2, Y2, 128)],
        smoothed1 + [(20 * Y2, 128)],
        *block1,
        cost=(8 << 20, 1 << 20),
    )
    parts2, *kept = lax.optimization_barrier((parts2, mach2, base1, coef1, base0, coef0))
    (chunk3,) = call(spread3_kernel, [(16, 48, 128)], [(4, Y3, 128)], parts2)
    parts3 = lax.all_to_all(chunk3, "gx", 0, 0)
    (sheet,) = call(pick2_kernel, [(36, 4, 128)], [], parts2)
    west, east = around(sheet, "gx")
    (a,) = call(
        window2_kernel,
        [(4, X2, Y2, 128)],
        [(3, Y2, 128)],
        west, sheet, east,
        cost=(4 << 20, 1 << 20),
    )
    wide3 = (X3 + 2 * PAD3, Y3, 128)
    wide4 = (X4 + 2, Y4, 128)
    scratch = [(3,) + wide3, (2,) + wide3, (2,) + wide3, (2,) + wide3, (3 * X4 * Y3, 128)]
    scratch += [(3,) + wide4, (2,) + wide4, (2,) + wide4, (2,) + wide4, (2 * X4 * Y3, 128)]
    scratch += [(2, 6, Y3 + 16, 128), (2 * 6 * Y2, 128)] + [(2, X2, Y2, 128)] * 3
    scratch += [(2, 8, Y2, 128), (2 * 8 * Y1, 128), (2,) + full1, (2,) + full1]
    scratch += [(2, 2 * 10 * 32, 128), (2,) + full0, (2,) + full0]
    return call(
        up_kernel,
        [(2, 16, 16, 128)],
        scratch,
        parts3, a, *kept,
        limit=16,
    )[0]


def solution(mesh):
    return jax.shard_map(
        shards,
        mesh=mesh,
        in_specs=(P(None, "gx", "gy", "gz"), P("gx", "gy", "gz")),
        out_specs=P(None, "gx", "gy", "gz"),
        check_vma=False,
    )
```

```python
import functools

import jax
import jax.numpy as jnp
from jax import lax
from jax.experimental import pallas as pl
from jax.experimental.pallas import tpu as pltpu
from jax.sharding import PartitionSpec as P

F32, BF16 = jnp.float32, jnp.bfloat16
WAVE = 0.0625
DIAG_I = 0.5 * WAVE
MOST = (11, 7, 6, 16, 16)

X0, Y0, L0 = 22, 24, 256
HZ = 14
X1D, Y1D = 20, 24
X1, Y1, L1 = 16, 16, 128
X2D, Y2 = 8, 16
X2 = 12
X3, Y3, PAD3 = 32, 16, 4
X4, Y4 = 16, 8


def iota(shape, dim):
    return lax.broadcasted_iota(jnp.int32, shape, dim)


def split(x):
    high = x.astype(BF16)
    rest = x - high.astype(F32)
    middle = rest.astype(BF16)
    return high, middle, (rest - middle.astype(F32)).astype(BF16)


def select(x, matrix, dims=(((1,), (0,)), ((), ()))):
    parts = [lax.dot_general(p, matrix, dims, preferred_element_type=F32) for p in split(x)]
    return parts[0] + (parts[1] + parts[2])


def coefficients(mach, level):
    scale = 0.25**level
    axial = scale * (1.0 - mach * mach)
    advect = (0.25 * 0.5**level) * mach
    diagonal = 2.0 * axial + (4.0 * scale - WAVE)
    return axial, advect, diagonal


def half_inverse(mach, level):
    diagonal = coefficients(mach, level)[2]
    scale = 0.5 / (diagonal * diagonal + DIAG_I * DIAG_I)
    inside = mach > 0.0
    return jnp.where(inside, diagonal * scale, 0.0), jnp.where(inside, -DIAG_I * scale, 0.0)


def transverse(c, ymask, zmask):
    rows, lanes = c.shape
    north, south = pltpu.roll(c, rows - 1, 0), pltpu.roll(c, 1, 0)
    upper, lower = pltpu.roll(c, lanes - 1, 1), pltpu.roll(c, 1, 1)
    if ymask:
        at = iota(c.shape, 0)
        north = jnp.where(at == rows - 1, 0.0, north)
        south = jnp.where(at == 0, 0.0, south)
    if zmask:
        at = iota(c.shape, 1)
        upper = jnp.where(at == lanes - 1, 0.0, upper)
        lower = jnp.where(at == 0, 0.0, lower)
    return (north + south) + (upper + lower)


def balance(source, mach, v, i, level, ymask, zmask):
    axial, advect, diagonal = coefficients(mach, level)
    scale = 0.25**level
    c_r, c_i = v[0, i], v[1, i]
    e_r, w_r, e_i, w_i = v[0, i + 1], v[0, i - 1], v[1, i + 1], v[1, i - 1]
    t_r = axial * (e_r + w_r) - advect * (e_i - w_i)
    t_i = axial * (e_i + w_i) + advect * (e_r - w_r)
    if source is not None:
        t_r, t_i = t_r + source[0], t_i + source[1]
    return (
        t_r + scale * transverse(c_r, ymask, zmask),
        t_i + scale * transverse(c_i, ymask, zmask),
        c_r,
        c_i,
        diagonal,
    )


def blocks(count, most, compute, store):
    unit = max(u for u in range(1, most + 1) if count % u == 0)

    def body(k, _):
        steps = [k * unit + u for u in range(unit)]
        for j, value in zip(steps, [compute(j) for j in steps]):
            store(j, value)
        return 0

    if count == unit:
        body(0, 0)
    else:
        lax.fori_loop(0, count // unit, body, 0)


def first_loop(lo, hi, g, hd, v, level):
    def compute(j):
        i = lo + j
        h_r, h_i = half_inverse(g[2, i], level)
        g_r, g_i = g[0, i], g[1, i]
        return h_r, h_i, h_r * g_r - h_i * g_i, h_r * g_i + h_i * g_r

    def store(j, value):
        i = lo + j
        hd[0, i], hd[1, i], v[0, i], v[1, i] = value

    blocks(hi - lo, MOST[level], compute, store)


def relax_loop(lo, count, g, hd, v, write, level, ymask=False, zmask=False, mach=None):
    mach = g.at[2] if mach is None else mach

    def compute(j):
        i = lo + j
        t_r, t_i, c_r, c_i, _ = balance((g[0, i], g[1, i]), mach[i], v, i, level, ymask, zmask)
        h_r, h_i = hd[0, i], hd[1, i]
        return 0.5 * c_r + (h_r * t_r - h_i * t_i), 0.5 * c_i + (h_r * t_i + h_i * t_r)

    blocks(count, MOST[level], compute, lambda j, value: write(j, lo + j, *value))


def free_loop(lo, count, coef, v, write, level):
    def compute(j):
        i = lo + j
        t_r, t_i, c_r, c_i, _ = balance(None, coef[0, i - 2], v, i, level, False, False)
        h_r, h_i = coef[1, i - 2], coef[2, i - 2]
        return 0.5 * c_r + (h_r * t_r - h_i * t_i), 0.5 * c_i + (h_r * t_i + h_i * t_r)

    blocks(count, MOST[level], compute, lambda j, value: write(j, lo + j, *value))


def writer(out):
    def write(j, i, re, im):
        out[0, i], out[1, i] = re, im

    return write


def residual(g, v, i, level, ymask=False, zmask=False):
    t_r, t_i, c_r, c_i, d = balance((g[0, i], g[1, i]), g[2, i], v, i, level, ymask, zmask)
    return t_r - (d * c_r - DIAG_I * c_i), t_i - (d * c_i + DIAG_I * c_r)


def residual_pair(g, v, i, level, ymask=False, zmask=False):
    a = residual(g, v, i, level, ymask, zmask)
    b = residual(g, v, i + 1, level, ymask, zmask)
    return a[0] + b[0], a[1] + b[1], g[2, i] + g[2, i + 1]


def pair_rows(ref, rows):
    return ref[pl.ds(0, rows // 2, stride=2), :] + ref[pl.ds(1, rows // 2, stride=2), :]


def twin_rows(ref, value):
    rows = value.shape[0]
    ref[pl.ds(0, rows, stride=2), :] = value
    ref[pl.ds(1, rows, stride=2), :] = value


def matrix(rows, lanes, rule, value=1.0):
    shape = (rows, lanes)
    return jnp.where(rule(iota(shape, 0), iota(shape, 1)), value, 0.0).astype(BF16)


def ends():
    at = lax.axis_index("gx")
    return jnp.where(at > 0, 1.0, 0.0), jnp.where(at < 15, 1.0, 0.0)


def assemble(own, ylo, yhi, xlo, xhi, f):
    count, rows, hx, hy = own.shape[1], own.shape[2], xlo.shape[1], ylo.shape[2]
    low, high = ends()
    for c in range(3):
        f[c, 0:hx] = xlo[c] if c < 2 else xlo[c] * low
        f[c, hx : hx + count, 0:hy] = ylo[c]
        f[c, hx : hx + count, hy : hy + rows] = own[c]
        f[c, hx : hx + count, hy + rows :] = yhi[c]
        f[c, hx + count :] = xhi[c] if c < 2 else xhi[c] * high


def start_kernel(source, mach, own, high, low):
    for c in range(3):
        own[c] = source[c] if c < 2 else mach[...].astype(F32)
        high[c], low[c] = own[c, :, 12:16], own[c, :, 0:4]


def gather0_kernel(own, ylo, yhi, xlo, xhi, f, low_lanes, high_lanes):
    assemble(own, ylo, yhi, xlo, xhi, f)
    parts = split(f[...].reshape(-1, 128))
    for out, start in ((low_lanes, 0), (high_lanes, 128 - HZ)):
        edge = matrix(16, 128, lambda r, l: (r < HZ) & (l == start + r))
        dims = (((1,), (1,)), ((), ()))
        terms = [lax.dot_general(edge, p, dims, preferred_element_type=F32) for p in parts]
        out[...] = terms[0] + (terms[1] + terms[2])


def smooth0(f, lower, upper, g, hd, v2, v1):
    both = jnp.concatenate([upper[...], lower[...]], axis=0)
    place = matrix(32, 128, lambda r, l: ((r < HZ) & (l == r)) | ((r >= 16) & (l == r + 112 - HZ)))
    tail = select(both, place, (((0,), (0,)), ((), ())))
    g[:, :, :, 0:128] = f[...]
    g[:, :, :, 128:256] = tail.reshape(3, X0, Y0, 128)
    first_loop(0, X0, g, hd, v1, 0)
    relax_loop(1, X0 - 2, g, hd, v1, writer(v2), 0)


def keep0_kernel(f, lower, upper, base, coef, g, hd, v2, v1):
    smooth0(f, lower, upper, g, hd, v2, v1)
    coef[0] = g[2, 2:20]
    coef[1:3] = hd[:, 2:20]
    relax_loop(2, X0 - 4, g, hd, v2, writer(v1), 0)

    def write(j, i, re, im):
        base[0, j], base[1, j] = re[4:20, 0:128], im[4:20, 0:128]

    relax_loop(3, X0 - 6, g, hd, v1, write, 0)


def down0_kernel(f, lower, upper, coarse, g, hd, v2, v1, sums):
    smooth0(f, lower, upper, g, hd, v2, v1)

    def store(k, parts):
        for c in range(3):
            row = pl.multiple_of((c * 8 + k) * 16, 16)
            for half in range(2):
                sums[half, pl.ds(row, 16), :] = parts[c][4:20, 128 * half : 128 * half + 128]

    blocks(8, 4, lambda k: residual_pair(g, v2, 3 + 2 * k, 0), store)
    own = matrix(128, 128, lambda r, l: r // 2 == l, 0.125)
    rest = matrix(
        128,
        128,
        lambda r, l: ((r < 12) | (r >= 116)) & (r // 2 + 64 == l),
        0.125,
    )
    total = select(pair_rows(sums.at[0], 384), own) + select(pair_rows(sums.at[1], 384), rest)
    coarse[...] = total.reshape(3, 8, 8, 128)


def smooth1(halos, g, hd, v2, v1):
    assemble(*halos, g)
    first_loop(0, X1D, g, hd, v1, 1)
    relax_loop(1, X1D - 2, g, hd, v1, writer(v2), 1)


def keep1_kernel(own, ylo, yhi, xlo, xhi, base, coef, mach2, g, hd, v2, v1, sums):
    smooth1((own, ylo, yhi, xlo, xhi), g, hd, v2, v1)
    coef[0] = g[2, 4:16, 4:20]
    coef[1:3] = hd[:, 4:16, 4:20]
    relax_loop(4, X1D - 8, g, hd, v2, writer(v1), 1)

    def write(j, i, re, im):
        base[0, j], base[1, j] = re[4:20, :], im[4:20, :]

    relax_loop(5, X1D - 10, g, hd, v1, write, 1)
    sums[...] = jnp.zeros_like(sums)
    for k in range(10):
        sums[2 * Y2 * k : 2 * Y2 * k + Y1D, :] = g[2, 2 * k] + g[2, 2 * k + 1]
    halve = matrix(
        128,
        128,
        lambda r, l: ((r < 70) & (r // 2 == l)) | ((r >= 122) & (r // 2 + 64 == l)),
        0.125,
    )
    mach2[0] = jnp.zeros((Y2, 128), F32)
    mach2[X2 - 1] = jnp.zeros((Y2, 128), F32)
    mach2[1 : X2 - 1] = select(pair_rows(sums, 20 * Y2), halve).reshape(10, Y2, 128)


def down1_kernel(own, ylo, yhi, xlo, xhi, chunk, g, hd, v2, v1, sums, g2, hd2, va, vb):
    smooth1((own, ylo, yhi, xlo, xhi), g, hd, v2, v1)
    sums[...] = jnp.zeros_like(sums)

    def store(k, parts):
        for c in range(3):
            row = pl.multiple_of((c * X2D + k) * 2 * Y2, 2 * Y2)
            sums[pl.ds(row, Y1D), :] = parts[c]

    blocks(X2D, 4, lambda k: residual_pair(g, v2, 2 + 2 * k, 1), store)
    halve = matrix(
        128,
        128,
        lambda r, l: ((r < 68) & (r // 2 == l)) | ((r >= 124) & (r // 2 + 64 == l)),
        0.125,
    )
    g2[...] = select(pair_rows(sums, 6 * X2D * Y2), halve).reshape(3, X2D, Y2, 128)
    first_loop(0, X2D, g2, hd2, va, 2)
    relax_loop(1, X2D - 2, g2, hd2, va, writer(vb), 2)
    lane = iota((Y2, 128), 1) // 32
    for c in range(4):
        source = (lambda x: g2[c, x]) if c < 2 else (lambda x: vb[c - 2, x])
        total = source(2)
        for x in range(1, 4):
            total = jnp.where(lane == x, pltpu.roll(source(2 + x), 32 * x, 1), total)
        for half in range(2):
            rows = total[4 + 2 * half : 6 + 2 * half, :]
            chunk[:, 1 + 2 * c + half] = jnp.broadcast_to(rows, (32, 2, 128))
    pairs = [residual_pair(g2, vb, 2 + 2 * x, 2) for x in range(2)]
    for c in range(3):
        for x in range(2):
            row = (c * 2 + x) * Y2
            sums[row : row + Y2, :] = pairs[x][c]
    halve = matrix(128, 128, lambda r, l: (r < 32) & (r // 2 == l), 0.125)
    small = select(pair_rows(sums, 6 * Y2), halve)
    total = None
    for k in range(6):
        value = small[8 * k : 8 * k + 8, :]
        value = pltpu.roll(value, 16 * k, 1) if k else value
        total = value if total is None else total + value
    chunk[:, 0] = jnp.broadcast_to(total[2:4, :], (32, 2, 128))


def spread3_kernel(parts, chunk, planes):
    for gz in range(4):
        for gy in range(8):
            planes[gz, 2 * gy : 2 * gy + 2, :] = parts[gy * 4 + gz, 0]
    lane = iota((Y3, 128), 1) // 16
    for c in range(3):
        total = jnp.zeros((Y3, 128), F32)
        for x in range(2):
            for gz in range(4):
                at = 4 * x + gz
                step = (16 * (at - 2 * c - x)) % 128
                value = planes[gz]
                value = pltpu.roll(value, step, 1) if step else value
                total = jnp.where(lane == at, value, total)
        chunk[:, Y3 * c : Y3 * (c + 1), :] = jnp.broadcast_to(total, (16, Y3, 128))


def pick2_kernel(parts, sheet):
    for bz in range(3):
        for by in range(3):
            y, z = lax.axis_index("gy") + (by - 1), lax.axis_index("gz") + (bz - 1)
            inside = (y >= 0) & (y < 8) & (z >= 0) & (z < 4)
            at = jnp.clip(y, 0, 7) * 4 + jnp.clip(z, 0, 3)
            factor = jnp.where(inside, 1.0, 0.0)
            for c in range(4):
                for half in range(2):
                    rows = parts[at, 1 + 2 * c + half] * factor
                    sheet[(bz * 3 + by) * 4 + c, 2 * half : 2 * half + 2, :] = rows


def window2_kernel(west, own, east, a, planes):
    lane = iota((Y2, 128), 1) // 32
    planes[...] = jnp.zeros_like(planes)
    low, high = ends()
    for bx, piece in enumerate((west, own, east)):
        factor = (low, None, high)[bx]

        def body(c, _):
            for bz in range(3):
                for by in range(3):
                    planes[bz, 4 * by : 4 * by + 4, :] = piece[(bz * 3 + by) * 4 + c]
            for x in range(4):
                total = jnp.zeros((Y2, 128), F32)
                for bz, group in enumerate((3, 0, 1)):
                    step = (32 * (group - x)) % 128
                    value = planes[bz]
                    value = pltpu.roll(value, step, 1) if step else value
                    total = jnp.where(lane == group, value, total)
                a[c, 4 * bx + x] = total if factor is None else total * factor
            return 0

        lax.fori_loop(0, 4, body, 0)


def up_kernel(
    parts3, a, mach2, base1, coef1, base0, coef0, out,
    g3, hd3, va3, vb3, s3, g4, hd4, va4, vb4, t4, w3, t3, hd2, va2, vb2, w2, t2, va1, vb1, t1, va0, vb0,
):
    gx, gy, gz = (lax.axis_index(n) for n in ("gx", "gy", "gz"))
    zero3 = jnp.zeros((Y3, 128), F32)
    for ref in (g3, hd3, va3, vb3):
        for c in range(ref.shape[0]):
            for i in range(PAD3):
                ref[c, i] = zero3
                ref[c, PAD3 + X3 + i] = zero3
    low = iota((Y3, 128), 1) < 64

    def spread(s):
        values = [parts3[s, Y3 * c : Y3 * (c + 1), :] for c in range(3)]
        return [(jnp.where(low, v, 0.0), jnp.where(low, pltpu.roll(v, 64, 1), 0.0)) for v in values]

    def keep(s, values):
        for c in range(3):
            g3[c, PAD3 + 2 * s], g3[c, PAD3 + 2 * s + 1] = values[c]

    blocks(16, 4, spread, keep)
    first_loop(PAD3, PAD3 + X3, g3, hd3, va3, 3)
    relax_loop(PAD3, X3, g3, hd3, va3, writer(vb3), 3, True)

    def keep3(k, parts):
        for c in range(3):
            s3[pl.ds(pl.multiple_of((c * X4 + k) * Y3, Y3), Y3), :] = parts[c]

    blocks(X4, 8, lambda k: residual_pair(g3, vb3, PAD3 + 2 * k, 3, True), keep3)
    halve = matrix(128, 128, lambda r, l: (r // 2 == l) & (r < 64), 0.125)
    g4[:, 1 : 1 + X4] = select(pair_rows(s3, 3 * X4 * Y3), halve).reshape(3, X4, Y4, 128)
    for ref in (va4, vb4):
        for c in range(2):
            ref[c, 0] = jnp.zeros((Y4, 128), F32)
            ref[c, X4 + 1] = jnp.zeros((Y4, 128), F32)
    first_loop(1, X4 + 1, g4, hd4, va4, 4)
    src, dst = va4, vb4
    for _ in range(5):
        relax_loop(1, X4, g4, hd4, src, writer(dst), 4, True)
        src, dst = dst, src
    double = matrix(128, 128, lambda r, l: l // 2 == r)
    twin_rows(t4, select(src[:, 1 : 1 + X4].reshape(2 * X4 * Y4, 128), double))

    def add3(k):
        values = [t4[pl.ds(pl.multiple_of((c * X4 + k) * Y3, Y3), Y3), :] for c in range(2)]
        at = PAD3 + 2 * k
        return [(vb3[c, at] + values[c], vb3[c, at + 1] + values[c]) for c in range(2)]

    def put3(k, values):
        at = PAD3 + 2 * k
        for c in range(2):
            vb3[c, at], vb3[c, at + 1] = values[c]

    blocks(X4, 4, add3, put3)
    base = PAD3 + 2 * gx
    relax_loop(base - 3, 8, g3, hd3, vb3, writer(va3), 3, True)

    w3[...] = jnp.zeros_like(w3)

    def write3(j, i, re, im):
        w3[0, j, 8 : 8 + Y3], w3[1, j, 8 : 8 + Y3] = re, im

    relax_loop(base - 2, 6, g3, hd3, va3, write3, 3, True)
    rows = w3[:, :, pl.ds(2 * gy + 6, 8), :].reshape(2 * 6 * 8, 128)

    def place2(r, l):
        at = jnp.where(l < 64, l, l - 128)
        return r == 16 * gz + (at + 128) // 2 - 64

    twin_rows(t3, select(rows, matrix(128, 128, place2)))

    for i in range(X2):
        hd2[0, i], hd2[1, i] = half_inverse(mach2[i], 2)
        for c in range(2):
            row = (c * 6 + i // 2) * Y2
            va2[c, i] = a[2 + c, i] + t3[row : row + Y2, :]

    relax_loop(1, X2 - 2, a, hd2, va2, writer(vb2), 2, mach=mach2)

    def write2(j, i, re, im):
        w2[0, j], w2[1, j] = re, im

    relax_loop(2, X2 - 4, a, hd2, vb2, write2, 2, mach=mach2)
    double = matrix(128, 128, lambda r, l: jnp.where(l < 96, l // 2, l // 2 + 64) == r)
    twin_rows(t2, select(w2[:, :, 2:10, :].reshape(2 * 8 * 8, 128), double))

    for i in range(1, X1 - 1):
        for c in range(2):
            row = (c * 8 + i // 2) * Y1
            va1[c, i] = t2[row : row + Y1, :]

    free_loop(2, X1 - 4, coef1, va1, writer(vb1), 1)

    def write1(j, i, re, im):
        va1[0, i], va1[1, i] = base1[0, j] + re, base1[1, j] + im

    free_loop(3, X1 - 6, coef1, vb1, write1, 1)
    own = va1[:, 3:13].reshape(2 * 10 * Y1, 128)
    for half in range(2):
        place = matrix(128, 128, lambda r, l: r == (l + 128 * half) // 2)
        twin_rows(t1.at[half], select(own, place))

    def start0(k, _):
        for c in range(2):
            row = (c * 10 + k) * 32 + 4
            for half in range(2):
                lanes = slice(128 * half, 128 * half + 128)
                value = t1[half, pl.ds(row, Y0), :]
                for i in range(2):
                    va0[c, 2 * k + 1 + i, :, lanes] = value
        return 0

    lax.fori_loop(0, 10, start0, 0)
    free_loop(2, X0 - 4, coef0, va0, writer(vb0), 0)

    def write0(j, i, re, im):
        out[0, j] = base0[0, j] + re[4:20, 0:128]
        out[1, j] = base0[1, j] + im[4:20, 0:128]

    free_loop(3, X0 - 6, coef0, vb0, write0, 0)


def call(kernel, outs, scratch, *args, limit=12, cost=None):
    spec = pl.BlockSpec(memory_space=pltpu.VMEM)
    return pl.pallas_call(
        kernel,
        out_shape=[jax.ShapeDtypeStruct(s, F32) for s in outs],
        in_specs=[spec] * len(args),
        out_specs=[spec] * len(outs),
        scratch_shapes=[pltpu.VMEM(s, F32) for s in scratch],
        compiler_params=pltpu.CompilerParams(vmem_limit_bytes=limit << 20),
        cost_estimate=cost and pl.CostEstimate(cost[0], 0, cost[1]),
    )(*args)


def shift(block, axis, step):
    count = lax.axis_size(axis)
    pairs = [(i, (i + step) % count) for i in range(count)]
    if axis != "gx":
        pairs = [(i, j) for i, j in pairs if j == i + step]
    return lax.ppermute(block, axis, pairs)


def halos(own, high, low, hx):
    count = own.shape[1]
    ylo, yhi = shift(high, "gy", 1), shift(low, "gy", -1)

    def edge(at):
        return jnp.concatenate([x[:, at : at + hx] for x in (ylo, own, yhi)], axis=2)

    return own, ylo, yhi, shift(edge(count - hx), "gx", 1), shift(edge(0), "gx", -1)


def around(block, axis):
    return shift(block, axis, 1), shift(block, axis, -1)


def shards(source_field, mach_number):
    edge = (3, 16, 4, 128)
    start = call(start_kernel, [(3, 16, 16, 128), edge, edge], [], source_field, mach_number)
    flat = (16, 3 * X0 * Y0)
    f0, low, high = call(
        gather0_kernel,
        [(3, X0, Y0, 128), flat, flat],
        [],
        *halos(*start, 3),
    )
    full0, full1 = (X0, Y0, L0), (X1, Y1, L1)
    block0 = (f0, shift(high, "gz", 1), shift(low, "gz", -1))
    smoothed0 = [(3,) + full0] + [(2,) + full0] * 3
    (own1,) = call(
        down0_kernel, [(3, 8, 8, 128)], smoothed0 + [(2, 384, 128)], *block0
    )
    wide1, wide2 = (X1D, Y1D, L1), (X2D, Y2, 128)
    block1 = halos(own1, own1, own1, 6)
    smoothed1 = [(3,) + wide1] + [(2,) + wide1] * 3
    (chunk2,) = call(
        down1_kernel,
        [(32, 9, 2, 128)],
        smoothed1 + [(6 * X2D * Y2, 128), (3,) + wide2] + [(2,) + wide2] * 3,
        *block1,
    )
    parts2 = lax.all_to_all(chunk2, ("gy", "gz"), 0, 0)
    (chunk3,) = call(spread3_kernel, [(16, 48, 128)], [(4, Y3, 128)], parts2)
    chunk3, block0, block1 = lax.optimization_barrier((chunk3, block0, tuple(block1)))
    base0, coef0 = call(
        keep0_kernel,
        [(2, 16, 16, 128), (3, 18, Y0, L0)],
        smoothed0,
        *block0,
        cost=(60 << 20, 8 << 20),
    )
    base1, coef1, mach2 = call(
        keep1_kernel,
        [(2, 10, Y1, 128), (3, 12, Y1, 128), (X2, Y2, 128)],
        smoothed1 + [(20 * Y2, 128)],
        *block1,
        cost=(8 << 20, 1 << 20),
    )
    kept = (mach2, base1, coef1, base0, coef0)
    parts3 = lax.all_to_all(chunk3, "gx", 0, 0)
    (sheet,) = call(pick2_kernel, [(36, 4, 128)], [], parts2)
    west, east = around(sheet, "gx")
    (a,) = call(
        window2_kernel,
        [(4, X2, Y2, 128)],
        [(3, Y2, 128)],
        west, sheet, east,
        cost=(4 << 20, 1 << 20),
    )
    wide3 = (X3 + 2 * PAD3, Y3, 128)
    wide4 = (X4 + 2, Y4, 128)
    scratch = [(3,) + wide3, (2,) + wide3, (2,) + wide3, (2,) + wide3, (3 * X4 * Y3, 128)]
    scratch += [(3,) + wide4, (2,) + wide4, (2,) + wide4, (2,) + wide4, (2 * X4 * Y3, 128)]
    scratch += [(2, 6, Y3 + 16, 128), (2 * 6 * Y2, 128)] + [(2, X2, Y2, 128)] * 3
    scratch += [(2, 8, Y2, 128), (2 * 8 * Y1, 128), (2,) + full1, (2,) + full1]
    scratch += [(2, 2 * 10 * 32, 128), (2,) + full0, (2,) + full0]
    return call(
        up_kernel,
        [(2, 16, 16, 128)],
        scratch,
        parts3, a, *kept,
        limit=16,
    )[0]


def solution(mesh):
    return jax.shard_map(
        shards,
        mesh=mesh,
        in_specs=(P(None, "gx", "gy", "gz"), P("gx", "gy", "gz")),
        out_specs=P(None, "gx", "gy", "gz"),
        check_vma=False,
    )
```

```python
import functools

import jax
import jax.numpy as jnp
from jax import lax
from jax.experimental import pallas as pl
from jax.experimental.pallas import tpu as pltpu
from jax.sharding import PartitionSpec as P

F32, BF16 = jnp.float32, jnp.bfloat16
WAVE = 0.0625
DIAG_I = 0.5 * WAVE
MOST = (11, 7, 6, 16, 16)

X0, Y0, L0 = 22, 24, 256
HZ = 14
X1D, Y1D = 20, 24
X1, Y1, L1 = 16, 16, 128
X2D, Y2 = 8, 16
X2 = 12
X3, Y3, PAD3 = 32, 16, 4
X4, Y4 = 16, 8


def iota(shape, dim):
    return lax.broadcasted_iota(jnp.int32, shape, dim)


def split(x):
    high = x.astype(BF16)
    rest = x - high.astype(F32)
    middle = rest.astype(BF16)
    return high, middle, (rest - middle.astype(F32)).astype(BF16)


def select(x, matrix, dims=(((1,), (0,)), ((), ()))):
    parts = [lax.dot_general(p, matrix, dims, preferred_element_type=F32) for p in split(x)]
    return parts[0] + (parts[1] + parts[2])


def coefficients(mach, level):
    scale = 0.25**level
    axial = scale * (1.0 - mach * mach)
    advect = (0.25 * 0.5**level) * mach
    diagonal = 2.0 * axial + (4.0 * scale - WAVE)
    return axial, advect, diagonal


def half_inverse(mach, level):
    diagonal = coefficients(mach, level)[2]
    scale = 0.5 / (diagonal * diagonal + DIAG_I * DIAG_I)
    inside = mach > 0.0
    return jnp.where(inside, diagonal * scale, 0.0), jnp.where(inside, -DIAG_I * scale, 0.0)


def transverse(c, ymask, zmask):
    rows, lanes = c.shape
    north, south = pltpu.roll(c, rows - 1, 0), pltpu.roll(c, 1, 0)
    upper, lower = pltpu.roll(c, lanes - 1, 1), pltpu.roll(c, 1, 1)
    if ymask:
        at = iota(c.shape, 0)
        north = jnp.where(at == rows - 1, 0.0, north)
        south = jnp.where(at == 0, 0.0, south)
    if zmask:
        at = iota(c.shape, 1)
        upper = jnp.where(at == lanes - 1, 0.0, upper)
        lower = jnp.where(at == 0, 0.0, lower)
    return (north + south) + (upper + lower)


def balance(source, mach, v, i, level, ymask, zmask):
    axial, advect, diagonal = coefficients(mach, level)
    scale = 0.25**level
    c_r, c_i = v[0, i], v[1, i]
    e_r, w_r, e_i, w_i = v[0, i + 1], v[0, i - 1], v[1, i + 1], v[1, i - 1]
    t_r = axial * (e_r + w_r) - advect * (e_i - w_i)
    t_i = axial * (e_i + w_i) + advect * (e_r - w_r)
    if source is not None:
        t_r, t_i = t_r + source[0], t_i + source[1]
    return (
        t_r + scale * transverse(c_r, ymask, zmask),
        t_i + scale * transverse(c_i, ymask, zmask),
        c_r,
        c_i,
        diagonal,
    )


def blocks(count, most, compute, store):
    unit = max(u for u in range(1, most + 1) if count % u == 0)

    def body(k, _):
        steps = [k * unit + u for u in range(unit)]
        for j, value in zip(steps, [compute(j) for j in steps]):
            store(j, value)
        return 0

    if count == unit:
        body(0, 0)
    else:
        lax.fori_loop(0, count // unit, body, 0)


def first_loop(lo, hi, g, hd, v, level):
    def compute(j):
        i = lo + j
        h_r, h_i = half_inverse(g[2, i], level)
        g_r, g_i = g[0, i], g[1, i]
        return h_r, h_i, h_r * g_r - h_i * g_i, h_r * g_i + h_i * g_r

    def store(j, value):
        i = lo + j
        hd[0, i], hd[1, i], v[0, i], v[1, i] = value

    blocks(hi - lo, MOST[level], compute, store)


def relax_loop(lo, count, g, hd, v, write, level, ymask=False, zmask=False, mach=None):
    mach = g.at[2] if mach is None else mach

    def compute(j):
        i = lo + j
        t_r, t_i, c_r, c_i, _ = balance((g[0, i], g[1, i]), mach[i], v, i, level, ymask, zmask)
        h_r, h_i = hd[0, i], hd[1, i]
        return 0.5 * c_r + (h_r * t_r - h_i * t_i), 0.5 * c_i + (h_r * t_i + h_i * t_r)

    blocks(count, MOST[level], compute, lambda j, value: write(j, lo + j, *value))


def free_loop(lo, count, coef, v, write, level):
    def compute(j):
        i = lo + j
        t_r, t_i, c_r, c_i, _ = balance(None, coef[0, i - 2], v, i, level, False, False)
        h_r, h_i = coef[1, i - 2], coef[2, i - 2]
        return 0.5 * c_r + (h_r * t_r - h_i * t_i), 0.5 * c_i + (h_r * t_i + h_i * t_r)

    blocks(count, MOST[level], compute, lambda j, value: write(j, lo + j, *value))


def writer(out):
    def write(j, i, re, im):
        out[0, i], out[1, i] = re, im

    return write


def residual(g, v, i, level, ymask=False, zmask=False):
    t_r, t_i, c_r, c_i, d = balance((g[0, i], g[1, i]), g[2, i], v, i, level, ymask, zmask)
    return t_r - (d * c_r - DIAG_I * c_i), t_i - (d * c_i + DIAG_I * c_r)


def residual_pair(g, v, i, level, ymask=False, zmask=False):
    a = residual(g, v, i, level, ymask, zmask)
    b = residual(g, v, i + 1, level, ymask, zmask)
    return a[0] + b[0], a[1] + b[1], g[2, i] + g[2, i + 1]


def pair_rows(ref, rows):
    return ref[pl.ds(0, rows // 2, stride=2), :] + ref[pl.ds(1, rows // 2, stride=2), :]


def twin_rows(ref, value):
    rows = value.shape[0]
    ref[pl.ds(0, rows, stride=2), :] = value
    ref[pl.ds(1, rows, stride=2), :] = value


def matrix(rows, lanes, rule, value=1.0):
    shape = (rows, lanes)
    return jnp.where(rule(iota(shape, 0), iota(shape, 1)), value, 0.0).astype(BF16)


def ends(axis):
    at = lax.axis_index(axis)
    return jnp.where(at > 0, 1.0, 0.0), jnp.where(at < lax.axis_size(axis) - 1, 1.0, 0.0)


def assemble(own, ylo, yhi, xlo, xhi, f):
    count, rows, hx, hy = own.shape[1], own.shape[2], xlo.shape[1], ylo.shape[2]
    low, high = ends("gx")
    for c in range(3):
        f[c, 0:hx] = xlo[c] if c < 2 else xlo[c] * low
        f[c, hx : hx + count, 0:hy] = ylo[c]
        f[c, hx : hx + count, hy : hy + rows] = own[c]
        f[c, hx : hx + count, hy + rows :] = yhi[c]
        f[c, hx + count :] = xhi[c] if c < 2 else xhi[c] * high
    low, high = ends("gy")
    f[2, :, 0:hy] = f[2, :, 0:hy] * low
    f[2, :, hy + rows :] = f[2, :, hy + rows :] * high


def start_kernel(source, mach, own, high, low):
    for c in range(3):
        own[c] = source[c] if c < 2 else mach[...].astype(F32)
        high[c], low[c] = own[c, :, 12:16], own[c, :, 0:4]


def gather0_kernel(own, ylo, yhi, xlo, xhi, f, low_lanes, high_lanes):
    assemble(own, ylo, yhi, xlo, xhi, f)
    parts = split(f[...].reshape(-1, 128))
    for out, start in ((low_lanes, 0), (high_lanes, 128 - HZ)):
        edge = matrix(16, 128, lambda r, l: (r < HZ) & (l == start + r))
        dims = (((1,), (1,)), ((), ()))
        terms = [lax.dot_general(edge, p, dims, preferred_element_type=F32) for p in parts]
        out[...] = terms[0] + (terms[1] + terms[2])


def smooth0(f, lower, upper, g, hd, v2, v1):
    both = jnp.concatenate([upper[...], lower[...]], axis=0)
    place = matrix(32, 128, lambda r, l: ((r < HZ) & (l == r)) | ((r >= 16) & (l == r + 112 - HZ)))
    tail = select(both, place, (((0,), (0,)), ((), ())))
    g[:, :, :, 0:128] = f[...]
    g[:, :, :, 128:256] = tail.reshape(3, X0, Y0, 128)
    first_loop(0, X0, g, hd, v1, 0)
    relax_loop(1, X0 - 2, g, hd, v1, writer(v2), 0)


def keep0_kernel(f, lower, upper, base, coef, g, hd, v2, v1):
    smooth0(f, lower, upper, g, hd, v2, v1)
    coef[0] = g[2, 2:20]
    coef[1:3] = hd[:, 2:20]
    relax_loop(2, X0 - 4, g, hd, v2, writer(v1), 0)

    def write(j, i, re, im):
        base[0, j], base[1, j] = re[4:20, 0:128], im[4:20, 0:128]

    relax_loop(3, X0 - 6, g, hd, v1, write, 0)


def down0_kernel(f, lower, upper, coarse, g, hd, v2, v1, sums):
    smooth0(f, lower, upper, g, hd, v2, v1)

    def store(k, parts):
        for c in range(3):
            row = pl.multiple_of((c * 8 + k) * 16, 16)
            for half in range(2):
                sums[half, pl.ds(row, 16), :] = parts[c][4:20, 128 * half : 128 * half + 128]

    blocks(8, 4, lambda k: residual_pair(g, v2, 3 + 2 * k, 0), store)
    own = matrix(128, 128, lambda r, l: r // 2 == l, 0.125)
    rest = matrix(
        128,
        128,
        lambda r, l: ((r < 12) | (r >= 116)) & (r // 2 + 64 == l),
        0.125,
    )
    total = select(pair_rows(sums.at[0], 384), own) + select(pair_rows(sums.at[1], 384), rest)
    coarse[...] = total.reshape(3, 8, 8, 128)


def smooth1(halos, g, hd, v2, v1):
    assemble(*halos, g)
    first_loop(0, X1D, g, hd, v1, 1)
    relax_loop(1, X1D - 2, g, hd, v1, writer(v2), 1)


def keep1_kernel(own, ylo, yhi, xlo, xhi, base, coef, mach2, g, hd, v2, v1, sums):
    smooth1((own, ylo, yhi, xlo, xhi), g, hd, v2, v1)
    coef[0] = g[2, 4:16, 4:20]
    coef[1:3] = hd[:, 4:16, 4:20]
    relax_loop(4, X1D - 8, g, hd, v2, writer(v1), 1)

    def write(j, i, re, im):
        base[0, j], base[1, j] = re[4:20, :], im[4:20, :]

    relax_loop(5, X1D - 10, g, hd, v1, write, 1)
    sums[...] = jnp.zeros_like(sums)
    for k in range(10):
        sums[2 * Y2 * k : 2 * Y2 * k + Y1D, :] = g[2, 2 * k] + g[2, 2 * k + 1]
    halve = matrix(
        128,
        128,
        lambda r, l: ((r < 70) & (r // 2 == l)) | ((r >= 122) & (r // 2 + 64 == l)),
        0.125,
    )
    mach2[0] = jnp.zeros((Y2, 128), F32)
    mach2[X2 - 1] = jnp.zeros((Y2, 128), F32)
    mach2[1 : X2 - 1] = select(pair_rows(sums, 20 * Y2), halve).reshape(10, Y2, 128)


def down1_kernel(own, ylo, yhi, xlo, xhi, chunk, g, hd, v2, v1, sums, g2, hd2, va, vb):
    smooth1((own, ylo, yhi, xlo, xhi), g, hd, v2, v1)
    sums[...] = jnp.zeros_like(sums)

    def store(k, parts):
        for c in range(3):
            row = pl.multiple_of((c * X2D + k) * 2 * Y2, 2 * Y2)
            sums[pl.ds(row, Y1D), :] = parts[c]

    blocks(X2D, 4, lambda k: residual_pair(g, v2, 2 + 2 * k, 1), store)
    halve = matrix(
        128,
        128,
        lambda r, l: ((r < 68) & (r // 2 == l)) | ((r >= 124) & (r // 2 + 64 == l)),
        0.125,
    )
    g2[...] = select(pair_rows(sums, 6 * X2D * Y2), halve).reshape(3, X2D, Y2, 128)
    first_loop(0, X2D, g2, hd2, va, 2)
    relax_loop(1, X2D - 2, g2, hd2, va, writer(vb), 2)
    lane = iota((Y2, 128), 1) // 32
    for c in range(4):
        source = (lambda x: g2[c, x]) if c < 2 else (lambda x: vb[c - 2, x])
        total = source(2)
        for x in range(1, 4):
            total = jnp.where(lane == x, pltpu.roll(source(2 + x), 32 * x, 1), total)
        for half in range(2):
            rows = total[4 + 2 * half : 6 + 2 * half, :]
            chunk[:, 1 + 2 * c + half] = jnp.broadcast_to(rows, (32, 2, 128))
    pairs = [residual_pair(g2, vb, 2 + 2 * x, 2) for x in range(2)]
    for c in range(3):
        for x in range(2):
            row = (c * 2 + x) * Y2
            sums[row : row + Y2, :] = pairs[x][c]
    halve = matrix(128, 128, lambda r, l: (r < 32) & (r // 2 == l), 0.125)
    small = select(pair_rows(sums, 6 * Y2), halve)
    total = None
    for k in range(6):
        value = small[8 * k : 8 * k + 8, :]
        value = pltpu.roll(value, 16 * k, 1) if k else value
        total = value if total is None else total + value
    chunk[:, 0] = jnp.broadcast_to(total[2:4, :], (32, 2, 128))


def spread3_kernel(parts, chunk, planes):
    for gz in range(4):
        for gy in range(8):
            planes[gz, 2 * gy : 2 * gy + 2, :] = parts[gy * 4 + gz, 0]
    lane = iota((Y3, 128), 1) // 16
    for c in range(3):
        total = jnp.zeros((Y3, 128), F32)
        for x in range(2):
            for gz in range(4):
                at = 4 * x + gz
                step = (16 * (at - 2 * c - x)) % 128
                value = planes[gz]
                value = pltpu.roll(value, step, 1) if step else value
                total = jnp.where(lane == at, value, total)
        chunk[:, Y3 * c : Y3 * (c + 1), :] = jnp.broadcast_to(total, (16, Y3, 128))


def pick2_kernel(parts, sheet):
    for bz in range(3):
        for by in range(3):
            y, z = lax.axis_index("gy") + (by - 1), lax.axis_index("gz") + (bz - 1)
            inside = (y >= 0) & (y < 8) & (z >= 0) & (z < 4)
            at = jnp.clip(y, 0, 7) * 4 + jnp.clip(z, 0, 3)
            factor = jnp.where(inside, 1.0, 0.0)
            for c in range(4):
                for half in range(2):
                    rows = parts[at, 1 + 2 * c + half] * factor
                    sheet[(bz * 3 + by) * 4 + c, 2 * half : 2 * half + 2, :] = rows


def window2_kernel(west, own, east, a, planes):
    lane = iota((Y2, 128), 1) // 32
    planes[...] = jnp.zeros_like(planes)
    low, high = ends("gx")
    for bx, piece in enumerate((west, own, east)):
        factor = (low, None, high)[bx]

        def body(c, _):
            for bz in range(3):
                for by in range(3):
                    planes[bz, 4 * by : 4 * by + 4, :] = piece[(bz * 3 + by) * 4 + c]
            for x in range(4):
                total = jnp.zeros((Y2, 128), F32)
                for bz, group in enumerate((3, 0, 1)):
                    step = (32 * (group - x)) % 128
                    value = planes[bz]
                    value = pltpu.roll(value, step, 1) if step else value
                    total = jnp.where(lane == group, value, total)
                a[c, 4 * bx + x] = total if factor is None else total * factor
            return 0

        lax.fori_loop(0, 4, body, 0)


def up_kernel(
    parts3, a, mach2, base1, coef1, base0, coef0, out,
    g3, hd3, va3, vb3, s3, g4, hd4, va4, vb4, t4, w3, t3, hd2, va2, vb2, w2, t2, va1, vb1, t1, va0, vb0,
):
    gx, gy, gz = (lax.axis_index(n) for n in ("gx", "gy", "gz"))
    zero3 = jnp.zeros((Y3, 128), F32)
    for ref in (g3, hd3, va3, vb3):
        for c in range(ref.shape[0]):
            for i in range(PAD3):
                ref[c, i] = zero3
                ref[c, PAD3 + X3 + i] = zero3
    low = iota((Y3, 128), 1) < 64

    def spread(s):
        values = [parts3[s, Y3 * c : Y3 * (c + 1), :] for c in range(3)]
        return [(jnp.where(low, v, 0.0), jnp.where(low, pltpu.roll(v, 64, 1), 0.0)) for v in values]

    def keep(s, values):
        for c in range(3):
            g3[c, PAD3 + 2 * s], g3[c, PAD3 + 2 * s + 1] = values[c]

    blocks(16, 4, spread, keep)
    first_loop(PAD3, PAD3 + X3, g3, hd3, va3, 3)
    relax_loop(PAD3, X3, g3, hd3, va3, writer(vb3), 3, True)

    def keep3(k, parts):
        for c in range(3):
            s3[pl.ds(pl.multiple_of((c * X4 + k) * Y3, Y3), Y3), :] = parts[c]

    blocks(X4, 8, lambda k: residual_pair(g3, vb3, PAD3 + 2 * k, 3, True), keep3)
    halve = matrix(128, 128, lambda r, l: (r // 2 == l) & (r < 64), 0.125)
    g4[:, 1 : 1 + X4] = select(pair_rows(s3, 3 * X4 * Y3), halve).reshape(3, X4, Y4, 128)
    for ref in (va4, vb4):
        for c in range(2):
            ref[c, 0] = jnp.zeros((Y4, 128), F32)
            ref[c, X4 + 1] = jnp.zeros((Y4, 128), F32)
    first_loop(1, X4 + 1, g4, hd4, va4, 4)
    src, dst = va4, vb4
    for _ in range(5):
        relax_loop(1, X4, g4, hd4, src, writer(dst), 4, True)
        src, dst = dst, src
    double = matrix(128, 128, lambda r, l: l // 2 == r)
    twin_rows(t4, select(src[:, 1 : 1 + X4].reshape(2 * X4 * Y4, 128), double))

    def add3(k):
        values = [t4[pl.ds(pl.multiple_of((c * X4 + k) * Y3, Y3), Y3), :] for c in range(2)]
        at = PAD3 + 2 * k
        return [(vb3[c, at] + values[c], vb3[c, at + 1] + values[c]) for c in range(2)]

    def put3(k, values):
        at = PAD3 + 2 * k
        for c in range(2):
            vb3[c, at], vb3[c, at + 1] = values[c]

    blocks(X4, 4, add3, put3)
    base = PAD3 + 2 * gx
    relax_loop(base - 3, 8, g3, hd3, vb3, writer(va3), 3, True)

    w3[...] = jnp.zeros_like(w3)

    def write3(j, i, re, im):
        w3[0, j, 8 : 8 + Y3], w3[1, j, 8 : 8 + Y3] = re, im

    relax_loop(base - 2, 6, g3, hd3, va3, write3, 3, True)
    rows = w3[:, :, pl.ds(2 * gy + 6, 8), :].reshape(2 * 6 * 8, 128)

    def place2(r, l):
        at = jnp.where(l < 64, l, l - 128)
        return r == 16 * gz + (at + 128) // 2 - 64

    twin_rows(t3, select(rows, matrix(128, 128, place2)))

    for i in range(X2):
        hd2[0, i], hd2[1, i] = half_inverse(mach2[i], 2)
        for c in range(2):
            row = (c * 6 + i // 2) * Y2
            va2[c, i] = a[2 + c, i] + t3[row : row + Y2, :]

    relax_loop(1, X2 - 2, a, hd2, va2, writer(vb2), 2, mach=mach2)

    def write2(j, i, re, im):
        w2[0, j], w2[1, j] = re, im

    relax_loop(2, X2 - 4, a, hd2, vb2, write2, 2, mach=mach2)
    double = matrix(128, 128, lambda r, l: jnp.where(l < 96, l // 2, l // 2 + 64) == r)
    twin_rows(t2, select(w2[:, :, 2:10, :].reshape(2 * 8 * 8, 128), double))

    for i in range(1, X1 - 1):
        for c in range(2):
            row = (c * 8 + i // 2) * Y1
            va1[c, i] = t2[row : row + Y1, :]

    free_loop(2, X1 - 4, coef1, va1, writer(vb1), 1)

    def write1(j, i, re, im):
        va1[0, i], va1[1, i] = base1[0, j] + re, base1[1, j] + im

    free_loop(3, X1 - 6, coef1, vb1, write1, 1)
    own = va1[:, 3:13].reshape(2 * 10 * Y1, 128)
    for half in range(2):
        place = matrix(128, 128, lambda r, l: r == (l + 128 * half) // 2)
        twin_rows(t1.at[half], select(own, place))

    def start0(k, _):
        for c in range(2):
            row = (c * 10 + k) * 32 + 4
            for half in range(2):
                lanes = slice(128 * half, 128 * half + 128)
                value = t1[half, pl.ds(row, Y0), :]
                for i in range(2):
                    va0[c, 2 * k + 1 + i, :, lanes] = value
        return 0

    lax.fori_loop(0, 10, start0, 0)
    free_loop(2, X0 - 4, coef0, va0, writer(vb0), 0)

    def write0(j, i, re, im):
        out[0, j] = base0[0, j] + re[4:20, 0:128]
        out[1, j] = base0[1, j] + im[4:20, 0:128]

    free_loop(3, X0 - 6, coef0, vb0, write0, 0)


def call(kernel, outs, scratch, *args, limit=12, cost=None):
    spec = pl.BlockSpec(memory_space=pltpu.VMEM)
    return pl.pallas_call(
        kernel,
        out_shape=[jax.ShapeDtypeStruct(s, F32) for s in outs],
        in_specs=[spec] * len(args),
        out_specs=[spec] * len(outs),
        scratch_shapes=[pltpu.VMEM(s, F32) for s in scratch],
        compiler_params=pltpu.CompilerParams(vmem_limit_bytes=limit << 20),
        cost_estimate=cost and pl.CostEstimate(cost[0], 0, cost[1]),
    )(*args)


def shift(block, axis, step):
    count = lax.axis_size(axis)
    pairs = [(i, (i + step) % count) for i in range(count)]
    if axis == "gz":
        pairs = [(i, j) for i, j in pairs if j == i + step]
    return lax.ppermute(block, axis, pairs)


def halos(own, high, low, hx):
    count = own.shape[1]
    ylo, yhi = shift(high, "gy", 1), shift(low, "gy", -1)

    def edge(at):
        return jnp.concatenate([x[:, at : at + hx] for x in (ylo, own, yhi)], axis=2)

    return own, ylo, yhi, shift(edge(count - hx), "gx", 1), shift(edge(0), "gx", -1)


def around(block, axis):
    return shift(block, axis, 1), shift(block, axis, -1)


def shards(source_field, mach_number):
    edge = (3, 16, 4, 128)
    start = call(start_kernel, [(3, 16, 16, 128), edge, edge], [], source_field, mach_number)
    flat = (16, 3 * X0 * Y0)
    f0, low, high = call(
        gather0_kernel,
        [(3, X0, Y0, 128), flat, flat],
        [],
        *halos(*start, 3),
    )
    full0, full1 = (X0, Y0, L0), (X1, Y1, L1)
    block0 = (f0, shift(high, "gz", 1), shift(low, "gz", -1))
    smoothed0 = [(3,) + full0] + [(2,) + full0] * 3
    (own1,) = call(
        down0_kernel, [(3, 8, 8, 128)], smoothed0 + [(2, 384, 128)], *block0
    )
    wide1, wide2 = (X1D, Y1D, L1), (X2D, Y2, 128)
    block1 = halos(own1, own1, own1, 6)
    smoothed1 = [(3,) + wide1] + [(2,) + wide1] * 3
    (chunk2,) = call(
        down1_kernel,
        [(32, 9, 2, 128)],
        smoothed1 + [(6 * X2D * Y2, 128), (3,) + wide2] + [(2,) + wide2] * 3,
        *block1,
    )
    parts2 = lax.all_to_all(chunk2, ("gy", "gz"), 0, 0)
    base0, coef0 = call(
        keep0_kernel,
        [(2, 16, 16, 128), (3, 18, Y0, L0)],
        smoothed0,
        *block0,
        cost=(60 << 20, 8 << 20),
    )
    base1, coef1, mach2 = call(
        keep1_kernel,
        [(2, 10, Y1, 128), (3, 12, Y1, 128), (X2, Y2, 128)],
        smoothed1 + [(20 * Y2, 128)],
        *block1,
        cost=(8 << 20, 1 << 20),
    )
    parts2, *kept = lax.optimization_barrier((parts2, mach2, base1, coef1, base0, coef0))
    (chunk3,) = call(spread3_kernel, [(16, 48, 128)], [(4, Y3, 128)], parts2)
    parts3 = lax.all_to_all(chunk3, "gx", 0, 0)
    (sheet,) = call(pick2_kernel, [(36, 4, 128)], [], parts2)
    west, east = around(sheet, "gx")
    (a,) = call(
        window2_kernel,
        [(4, X2, Y2, 128)],
        [(3, Y2, 128)],
        west, sheet, east,
        cost=(4 << 20, 1 << 20),
    )
    wide3 = (X3 + 2 * PAD3, Y3, 128)
    wide4 = (X4 + 2, Y4, 128)
    scratch = [(3,) + wide3, (2,) + wide3, (2,) + wide3, (2,) + wide3, (3 * X4 * Y3, 128)]
    scratch += [(3,) + wide4, (2,) + wide4, (2,) + wide4, (2,) + wide4, (2 * X4 * Y3, 128)]
    scratch += [(2, 6, Y3 + 16, 128), (2 * 6 * Y2, 128)] + [(2, X2, Y2, 128)] * 3
    scratch += [(2, 8, Y2, 128), (2 * 8 * Y1, 128), (2,) + full1, (2,) + full1]
    scratch += [(2, 2 * 10 * 32, 128), (2,) + full0, (2,) + full0]
    return call(
        up_kernel,
        [(2, 16, 16, 128)],
        scratch,
        parts3, a, *kept,
        limit=16,
    )[0]


def solution(mesh):
    return jax.shard_map(
        shards,
        mesh=mesh,
        in_specs=(P(None, "gx", "gy", "gz"), P("gx", "gy", "gz")),
        out_specs=P(None, "gx", "gy", "gz"),
        check_vma=False,
    )
```

```python
import functools

import jax
import jax.numpy as jnp
from jax import lax
from jax.experimental import pallas as pl
from jax.experimental.pallas import tpu as pltpu
from jax.sharding import PartitionSpec as P

F32, BF16 = jnp.float32, jnp.bfloat16
WAVE = 0.0625
DIAG_I = 0.5 * WAVE
MOST = (11, 7, 6, 16, 16)

X0, Y0, L0 = 22, 24, 256
HZ = 14
X1D, Y1D = 20, 24
X1, Y1, L1 = 16, 16, 128
X2D, Y2 = 8, 16
X2 = 12
X3, Y3, PAD3 = 32, 16, 4
X4, Y4 = 16, 8


def iota(shape, dim):
    return lax.broadcasted_iota(jnp.int32, shape, dim)


def split(x):
    high = x.astype(BF16)
    return high, (x - high.astype(F32)).astype(BF16)


def select(x, matrix, dims=(((1,), (0,)), ((), ()))):
    parts = [lax.dot_general(p, matrix, dims, preferred_element_type=F32) for p in split(x)]
    return parts[0] + parts[1]


def coefficients(mach, level):
    scale = 0.25**level
    axial = scale * (1.0 - mach * mach)
    advect = (0.25 * 0.5**level) * mach
    diagonal = 2.0 * axial + (4.0 * scale - WAVE)
    return axial, advect, diagonal


def half_inverse(mach, level):
    diagonal = coefficients(mach, level)[2]
    scale = 0.5 / (diagonal * diagonal + DIAG_I * DIAG_I)
    inside = mach > 0.0
    return jnp.where(inside, diagonal * scale, 0.0), jnp.where(inside, -DIAG_I * scale, 0.0)


def transverse(c, ymask, zmask):
    rows, lanes = c.shape
    north, south = pltpu.roll(c, rows - 1, 0), pltpu.roll(c, 1, 0)
    upper, lower = pltpu.roll(c, lanes - 1, 1), pltpu.roll(c, 1, 1)
    if ymask:
        at = iota(c.shape, 0)
        north = jnp.where(at == rows - 1, 0.0, north)
        south = jnp.where(at == 0, 0.0, south)
    if zmask:
        at = iota(c.shape, 1)
        upper = jnp.where(at == lanes - 1, 0.0, upper)
        lower = jnp.where(at == 0, 0.0, lower)
    return (north + south) + (upper + lower)


def balance(source, mach, v, i, level, ymask, zmask):
    axial, advect, diagonal = coefficients(mach, level)
    scale = 0.25**level
    c_r, c_i = v[0, i], v[1, i]
    e_r, w_r, e_i, w_i = v[0, i + 1], v[0, i - 1], v[1, i + 1], v[1, i - 1]
    t_r = axial * (e_r + w_r) - advect * (e_i - w_i)
    t_i = axial * (e_i + w_i) + advect * (e_r - w_r)
    if source is not None:
        t_r, t_i = t_r + source[0], t_i + source[1]
    return (
        t_r + scale * transverse(c_r, ymask, zmask),
        t_i + scale * transverse(c_i, ymask, zmask),
        c_r,
        c_i,
        diagonal,
    )


def blocks(count, most, compute, store):
    unit = max(u for u in range(1, most + 1) if count % u == 0)

    def body(k, _):
        steps = [k * unit + u for u in range(unit)]
        for j, value in zip(steps, [compute(j) for j in steps]):
            store(j, value)
        return 0

    if count == unit:
        body(0, 0)
    else:
        lax.fori_loop(0, count // unit, body, 0)


def first_loop(lo, hi, g, hd, v, level):
    def compute(j):
        i = lo + j
        h_r, h_i = half_inverse(g[2, i], level)
        g_r, g_i = g[0, i], g[1, i]
        return h_r, h_i, h_r * g_r - h_i * g_i, h_r * g_i + h_i * g_r

    def store(j, value):
        i = lo + j
        hd[0, i], hd[1, i], v[0, i], v[1, i] = value

    blocks(hi - lo, MOST[level], compute, store)


def relax_loop(lo, count, g, hd, v, write, level, ymask=False, zmask=False, mach=None):
    mach = g.at[2] if mach is None else mach

    def compute(j):
        i = lo + j
        t_r, t_i, c_r, c_i, _ = balance((g[0, i], g[1, i]), mach[i], v, i, level, ymask, zmask)
        h_r, h_i = hd[0, i], hd[1, i]
        return 0.5 * c_r + (h_r * t_r - h_i * t_i), 0.5 * c_i + (h_r * t_i + h_i * t_r)

    blocks(count, MOST[level], compute, lambda j, value: write(j, lo + j, *value))


def free_loop(lo, count, coef, v, write, level):
    def compute(j):
        i = lo + j
        t_r, t_i, c_r, c_i, _ = balance(None, coef[0, i - 2], v, i, level, False, False)
        h_r, h_i = coef[1, i - 2], coef[2, i - 2]
        return 0.5 * c_r + (h_r * t_r - h_i * t_i), 0.5 * c_i + (h_r * t_i + h_i * t_r)

    blocks(count, MOST[level], compute, lambda j, value: write(j, lo + j, *value))


def writer(out):
    def write(j, i, re, im):
        out[0, i], out[1, i] = re, im

    return write


def residual(g, v, i, level, ymask=False, zmask=False):
    t_r, t_i, c_r, c_i, d = balance((g[0, i], g[1, i]), g[2, i], v, i, level, ymask, zmask)
    return t_r - (d * c_r - DIAG_I * c_i), t_i - (d * c_i + DIAG_I * c_r)


def residual_pair(g, v, i, level, ymask=False, zmask=False):
    a = residual(g, v, i, level, ymask, zmask)
    b = residual(g, v, i + 1, level, ymask, zmask)
    return a[0] + b[0], a[1] + b[1], g[2, i] + g[2, i + 1]


def pair_rows(ref, rows):
    return ref[pl.ds(0, rows // 2, stride=2), :] + ref[pl.ds(1, rows // 2, stride=2), :]


def twin_rows(ref, value):
    rows = value.shape[0]
    ref[pl.ds(0, rows, stride=2), :] = value
    ref[pl.ds(1, rows, stride=2), :] = value


def matrix(rows, lanes, rule, value=1.0):
    shape = (rows, lanes)
    return jnp.where(rule(iota(shape, 0), iota(shape, 1)), value, 0.0).astype(BF16)


def ends():
    at = lax.axis_index("gx")
    return jnp.where(at > 0, 1.0, 0.0), jnp.where(at < 15, 1.0, 0.0)


def assemble(own, ylo, yhi, xlo, xhi, f):
    count, rows, hx, hy = own.shape[1], own.shape[2], xlo.shape[1], ylo.shape[2]
    low, high = ends()
    for c in range(3):
        f[c, 0:hx] = xlo[c] if c < 2 else xlo[c] * low
        f[c, hx : hx + count, 0:hy] = ylo[c]
        f[c, hx : hx + count, hy : hy + rows] = own[c]
        f[c, hx : hx + count, hy + rows :] = yhi[c]
        f[c, hx + count :] = xhi[c] if c < 2 else xhi[c] * high


def start_kernel(source, mach, own, high, low):
    for c in range(3):
        own[c] = source[c] if c < 2 else mach[...].astype(F32)
        high[c], low[c] = own[c, :, 12:16], own[c, :, 0:4]


def gather0_kernel(own, ylo, yhi, xlo, xhi, f, low_lanes, high_lanes):
    assemble(own, ylo, yhi, xlo, xhi, f)
    parts = split(f[...].reshape(-1, 128))
    for out, start in ((low_lanes, 0), (high_lanes, 128 - HZ)):
        edge = matrix(16, 128, lambda r, l: (r < HZ) & (l == start + r))
        dims = (((1,), (1,)), ((), ()))
        terms = [lax.dot_general(edge, p, dims, preferred_element_type=F32) for p in parts]
        out[...] = terms[0] + terms[1]


def smooth0(f, lower, upper, g, hd, v2, v1):
    both = jnp.concatenate([upper[...], lower[...]], axis=0)
    place = matrix(32, 128, lambda r, l: ((r < HZ) & (l == r)) | ((r >= 16) & (l == r + 112 - HZ)))
    tail = select(both, place, (((0,), (0,)), ((), ())))
    g[:, :, :, 0:128] = f[...]
    g[:, :, :, 128:256] = tail.reshape(3, X0, Y0, 128)
    first_loop(0, X0, g, hd, v1, 0)
    relax_loop(1, X0 - 2, g, hd, v1, writer(v2), 0)


def keep0_kernel(f, lower, upper, base, coef, g, hd, v2, v1):
    smooth0(f, lower, upper, g, hd, v2, v1)
    coef[0] = g[2, 2:20]
    coef[1:3] = hd[:, 2:20]
    relax_loop(2, X0 - 4, g, hd, v2, writer(v1), 0)

    def write(j, i, re, im):
        base[0, j], base[1, j] = re[4:20, 0:128], im[4:20, 0:128]

    relax_loop(3, X0 - 6, g, hd, v1, write, 0)


def down0_kernel(f, lower, upper, coarse, g, hd, v2, v1, sums):
    smooth0(f, lower, upper, g, hd, v2, v1)

    def store(k, parts):
        for c in range(3):
            row = pl.multiple_of((c * 8 + k) * 16, 16)
            for half in range(2):
                sums[half, pl.ds(row, 16), :] = parts[c][4:20, 128 * half : 128 * half + 128]

    blocks(8, 4, lambda k: residual_pair(g, v2, 3 + 2 * k, 0), store)
    own = matrix(128, 128, lambda r, l: r // 2 == l, 0.125)
    rest = matrix(
        128,
        128,
        lambda r, l: ((r < 12) | (r >= 116)) & (r // 2 + 64 == l),
        0.125,
    )
    total = select(pair_rows(sums.at[0], 384), own) + select(pair_rows(sums.at[1], 384), rest)
    coarse[...] = total.reshape(3, 8, 8, 128)


def smooth1(halos, g, hd, v2, v1):
    assemble(*halos, g)
    first_loop(0, X1D, g, hd, v1, 1)
    relax_loop(1, X1D - 2, g, hd, v1, writer(v2), 1)


def keep1_kernel(own, ylo, yhi, xlo, xhi, base, coef, mach2, g, hd, v2, v1, sums):
    smooth1((own, ylo, yhi, xlo, xhi), g, hd, v2, v1)
    coef[0] = g[2, 4:16, 4:20]
    coef[1:3] = hd[:, 4:16, 4:20]
    relax_loop(4, X1D - 8, g, hd, v2, writer(v1), 1)

    def write(j, i, re, im):
        base[0, j], base[1, j] = re[4:20, :], im[4:20, :]

    relax_loop(5, X1D - 10, g, hd, v1, write, 1)
    sums[...] = jnp.zeros_like(sums)
    for k in range(10):
        sums[2 * Y2 * k : 2 * Y2 * k + Y1D, :] = g[2, 2 * k] + g[2, 2 * k + 1]
    halve = matrix(
        128,
        128,
        lambda r, l: ((r < 70) & (r // 2 == l)) | ((r >= 122) & (r // 2 + 64 == l)),
        0.125,
    )
    mach2[0] = jnp.zeros((Y2, 128), F32)
    mach2[X2 - 1] = jnp.zeros((Y2, 128), F32)
    mach2[1 : X2 - 1] = select(pair_rows(sums, 20 * Y2), halve).reshape(10, Y2, 128)


def down1_kernel(own, ylo, yhi, xlo, xhi, chunk, g, hd, v2, v1, sums, g2, hd2, va, vb):
    smooth1((own, ylo, yhi, xlo, xhi), g, hd, v2, v1)
    sums[...] = jnp.zeros_like(sums)

    def store(k, parts):
        for c in range(3):
            row = pl.multiple_of((c * X2D + k) * 2 * Y2, 2 * Y2)
            sums[pl.ds(row, Y1D), :] = parts[c]

    blocks(X2D, 4, lambda k: residual_pair(g, v2, 2 + 2 * k, 1), store)
    halve = matrix(
        128,
        128,
        lambda r, l: ((r < 68) & (r // 2 == l)) | ((r >= 124) & (r // 2 + 64 == l)),
        0.125,
    )
    g2[...] = select(pair_rows(sums, 6 * X2D * Y2), halve).reshape(3, X2D, Y2, 128)
    first_loop(0, X2D, g2, hd2, va, 2)
    relax_loop(1, X2D - 2, g2, hd2, va, writer(vb), 2)
    lane = iota((Y2, 128), 1) // 32
    for c in range(4):
        source = (lambda x: g2[c, x]) if c < 2 else (lambda x: vb[c - 2, x])
        total = source(2)
        for x in range(1, 4):
            total = jnp.where(lane == x, pltpu.roll(source(2 + x), 32 * x, 1), total)
        for half in range(2):
            rows = total[4 + 2 * half : 6 + 2 * half, :]
            chunk[:, 1 + 2 * c + half] = jnp.broadcast_to(rows, (32, 2, 128))
    pairs = [residual_pair(g2, vb, 2 + 2 * x, 2) for x in range(2)]
    for c in range(3):
        for x in range(2):
            row = (c * 2 + x) * Y2
            sums[row : row + Y2, :] = pairs[x][c]
    halve = matrix(128, 128, lambda r, l: (r < 32) & (r // 2 == l), 0.125)
    small = select(pair_rows(sums, 6 * Y2), halve)
    total = None
    for k in range(6):
        value = small[8 * k : 8 * k + 8, :]
        value = pltpu.roll(value, 16 * k, 1) if k else value
        total = value if total is None else total + value
    chunk[:, 0] = jnp.broadcast_to(total[2:4, :], (32, 2, 128))


def spread3_kernel(parts, chunk, planes):
    for gz in range(4):
        for gy in range(8):
            planes[gz, 2 * gy : 2 * gy + 2, :] = parts[gy * 4 + gz, 0]
    lane = iota((Y3, 128), 1) // 16
    for c in range(3):
        total = jnp.zeros((Y3, 128), F32)
        for x in range(2):
            for gz in range(4):
                at = 4 * x + gz
                step = (16 * (at - 2 * c - x)) % 128
                value = planes[gz]
                value = pltpu.roll(value, step, 1) if step else value
                total = jnp.where(lane == at, value, total)
        chunk[:, Y3 * c : Y3 * (c + 1), :] = jnp.broadcast_to(total, (16, Y3, 128))


def pick2_kernel(parts, sheet):
    for bz in range(3):
        for by in range(3):
            y, z = lax.axis_index("gy") + (by - 1), lax.axis_index("gz") + (bz - 1)
            inside = (y >= 0) & (y < 8) & (z >= 0) & (z < 4)
            at = jnp.clip(y, 0, 7) * 4 + jnp.clip(z, 0, 3)
            factor = jnp.where(inside, 1.0, 0.0)
            for c in range(4):
                for half in range(2):
                    rows = parts[at, 1 + 2 * c + half] * factor
                    sheet[(bz * 3 + by) * 4 + c, 2 * half : 2 * half + 2, :] = rows


def window2_kernel(west, own, east, a, planes):
    lane = iota((Y2, 128), 1) // 32
    planes[...] = jnp.zeros_like(planes)
    low, high = ends()
    for bx, piece in enumerate((west, own, east)):
        factor = (low, None, high)[bx]

        def body(c, _):
            for bz in range(3):
                for by in range(3):
                    planes[bz, 4 * by : 4 * by + 4, :] = piece[(bz * 3 + by) * 4 + c]
            for x in range(4):
                total = jnp.zeros((Y2, 128), F32)
                for bz, group in enumerate((3, 0, 1)):
                    step = (32 * (group - x)) % 128
                    value = planes[bz]
                    value = pltpu.roll(value, step, 1) if step else value
                    total = jnp.where(lane == group, value, total)
                a[c, 4 * bx + x] = total if factor is None else total * factor
            return 0

        lax.fori_loop(0, 4, body, 0)


def up_kernel(
    parts3, a, mach2, base1, coef1, base0, coef0, out,
    g3, hd3, va3, vb3, s3, g4, hd4, va4, vb4, t4, w3, t3, hd2, va2, vb2, w2, t2, va1, vb1, t1, va0, vb0,
):
    gx, gy, gz = (lax.axis_index(n) for n in ("gx", "gy", "gz"))
    zero3 = jnp.zeros((Y3, 128), F32)
    for ref in (g3, hd3, va3, vb3):
        for c in range(ref.shape[0]):
            for i in range(PAD3):
                ref[c, i] = zero3
                ref[c, PAD3 + X3 + i] = zero3
    low = iota((Y3, 128), 1) < 64

    def spread(s):
        values = [parts3[s, Y3 * c : Y3 * (c + 1), :] for c in range(3)]
        return [(jnp.where(low, v, 0.0), jnp.where(low, pltpu.roll(v, 64, 1), 0.0)) for v in values]

    def keep(s, values):
        for c in range(3):
            g3[c, PAD3 + 2 * s], g3[c, PAD3 + 2 * s + 1] = values[c]

    blocks(16, 4, spread, keep)
    first_loop(PAD3, PAD3 + X3, g3, hd3, va3, 3)
    relax_loop(PAD3, X3, g3, hd3, va3, writer(vb3), 3, True)

    def keep3(k, parts):
        for c in range(3):
            s3[pl.ds(pl.multiple_of((c * X4 + k) * Y3, Y3), Y3), :] = parts[c]

    blocks(X4, 8, lambda k: residual_pair(g3, vb3, PAD3 + 2 * k, 3, True), keep3)
    halve = matrix(128, 128, lambda r, l: (r // 2 == l) & (r < 64), 0.125)
    g4[:, 1 : 1 + X4] = select(pair_rows(s3, 3 * X4 * Y3), halve).reshape(3, X4, Y4, 128)
    for ref in (va4, vb4):
        for c in range(2):
            ref[c, 0] = jnp.zeros((Y4, 128), F32)
            ref[c, X4 + 1] = jnp.zeros((Y4, 128), F32)
    first_loop(1, X4 + 1, g4, hd4, va4, 4)
    src, dst = va4, vb4
    for _ in range(5):
        relax_loop(1, X4, g4, hd4, src, writer(dst), 4, True)
        src, dst = dst, src
    double = matrix(128, 128, lambda r, l: l // 2 == r)
    twin_rows(t4, select(src[:, 1 : 1 + X4].reshape(2 * X4 * Y4, 128), double))

    def add3(k):
        values = [t4[pl.ds(pl.multiple_of((c * X4 + k) * Y3, Y3), Y3), :] for c in range(2)]
        at = PAD3 + 2 * k
        return [(vb3[c, at] + values[c], vb3[c, at + 1] + values[c]) for c in range(2)]

    def put3(k, values):
        at = PAD3 + 2 * k
        for c in range(2):
            vb3[c, at], vb3[c, at + 1] = values[c]

    blocks(X4, 4, add3, put3)
    base = PAD3 + 2 * gx
    relax_loop(base - 3, 8, g3, hd3, vb3, writer(va3), 3, True)

    w3[...] = jnp.zeros_like(w3)

    def write3(j, i, re, im):
        w3[0, j, 8 : 8 + Y3], w3[1, j, 8 : 8 + Y3] = re, im

    relax_loop(base - 2, 6, g3, hd3, va3, write3, 3, True)
    rows = w3[:, :, pl.ds(2 * gy + 6, 8), :].reshape(2 * 6 * 8, 128)

    def place2(r, l):
        at = jnp.where(l < 64, l, l - 128)
        return r == 16 * gz + (at + 128) // 2 - 64

    twin_rows(t3, select(rows, matrix(128, 128, place2)))

    for i in range(X2):
        hd2[0, i], hd2[1, i] = half_inverse(mach2[i], 2)
        for c in range(2):
            row = (c * 6 + i // 2) * Y2
            va2[c, i] = a[2 + c, i] + t3[row : row + Y2, :]

    relax_loop(1, X2 - 2, a, hd2, va2, writer(vb2), 2, mach=mach2)

    def write2(j, i, re, im):
        w2[0, j], w2[1, j] = re, im

    relax_loop(2, X2 - 4, a, hd2, vb2, write2, 2, mach=mach2)
    double = matrix(128, 128, lambda r, l: jnp.where(l < 96, l // 2, l // 2 + 64) == r)
    twin_rows(t2, select(w2[:, :, 2:10, :].reshape(2 * 8 * 8, 128), double))

    for i in range(1, X1 - 1):
        for c in range(2):
            row = (c * 8 + i // 2) * Y1
            va1[c, i] = t2[row : row + Y1, :]

    free_loop(2, X1 - 4, coef1, va1, writer(vb1), 1)

    def write1(j, i, re, im):
        va1[0, i], va1[1, i] = base1[0, j] + re, base1[1, j] + im

    free_loop(3, X1 - 6, coef1, vb1, write1, 1)
    own = va1[:, 3:13].reshape(2 * 10 * Y1, 128)
    for half in range(2):
        place = matrix(128, 128, lambda r, l: r == (l + 128 * half) // 2)
        twin_rows(t1.at[half], select(own, place))

    def start0(k, _):
        for c in range(2):
            row = (c * 10 + k) * 32 + 4
            for half in range(2):
                lanes = slice(128 * half, 128 * half + 128)
                value = t1[half, pl.ds(row, Y0), :]
                for i in range(2):
                    va0[c, 2 * k + 1 + i, :, lanes] = value
        return 0

    lax.fori_loop(0, 10, start0, 0)
    free_loop(2, X0 - 4, coef0, va0, writer(vb0), 0)

    def write0(j, i, re, im):
        out[0, j] = base0[0, j] + re[4:20, 0:128]
        out[1, j] = base0[1, j] + im[4:20, 0:128]

    free_loop(3, X0 - 6, coef0, vb0, write0, 0)


def call(kernel, outs, scratch, *args, limit=12, cost=None):
    spec = pl.BlockSpec(memory_space=pltpu.VMEM)
    return pl.pallas_call(
        kernel,
        out_shape=[jax.ShapeDtypeStruct(s, F32) for s in outs],
        in_specs=[spec] * len(args),
        out_specs=[spec] * len(outs),
        scratch_shapes=[pltpu.VMEM(s, F32) for s in scratch],
        compiler_params=pltpu.CompilerParams(vmem_limit_bytes=limit << 20),
        cost_estimate=cost and pl.CostEstimate(cost[0], 0, cost[1]),
    )(*args)


def shift(block, axis, step):
    count = lax.axis_size(axis)
    pairs = [(i, (i + step) % count) for i in range(count)]
    if axis != "gx":
        pairs = [(i, j) for i, j in pairs if j == i + step]
    return lax.ppermute(block, axis, pairs)


def halos(own, high, low, hx):
    count = own.shape[1]
    ylo, yhi = shift(high, "gy", 1), shift(low, "gy", -1)

    def edge(at):
        return jnp.concatenate([x[:, at : at + hx] for x in (ylo, own, yhi)], axis=2)

    return own, ylo, yhi, shift(edge(count - hx), "gx", 1), shift(edge(0), "gx", -1)


def around(block, axis):
    return shift(block, axis, 1), shift(block, axis, -1)


def shards(source_field, mach_number):
    edge = (3, 16, 4, 128)
    start = call(start_kernel, [(3, 16, 16, 128), edge, edge], [], source_field, mach_number)
    flat = (16, 3 * X0 * Y0)
    f0, low, high = call(
        gather0_kernel,
        [(3, X0, Y0, 128), flat, flat],
        [],
        *halos(*start, 3),
    )
    full0, full1 = (X0, Y0, L0), (X1, Y1, L1)
    block0 = (f0, shift(high, "gz", 1), shift(low, "gz", -1))
    smoothed0 = [(3,) + full0] + [(2,) + full0] * 3
    (own1,) = call(
        down0_kernel, [(3, 8, 8, 128)], smoothed0 + [(2, 384, 128)], *block0
    )
    wide1, wide2 = (X1D, Y1D, L1), (X2D, Y2, 128)
    block1 = halos(own1, own1, own1, 6)
    smoothed1 = [(3,) + wide1] + [(2,) + wide1] * 3
    (chunk2,) = call(
        down1_kernel,
        [(32, 9, 2, 128)],
        smoothed1 + [(6 * X2D * Y2, 128), (3,) + wide2] + [(2,) + wide2] * 3,
        *block1,
    )
    parts2 = lax.all_to_all(chunk2, ("gy", "gz"), 0, 0)
    base0, coef0 = call(
        keep0_kernel,
        [(2, 16, 16, 128), (3, 18, Y0, L0)],
        smoothed0,
        *block0,
        cost=(60 << 20, 8 << 20),
    )
    base1, coef1, mach2 = call(
        keep1_kernel,
        [(2, 10, Y1, 128), (3, 12, Y1, 128), (X2, Y2, 128)],
        smoothed1 + [(20 * Y2, 128)],
        *block1,
        cost=(8 << 20, 1 << 20),
    )
    parts2, *kept = lax.optimization_barrier((parts2, mach2, base1, coef1, base0, coef0))
    (chunk3,) = call(spread3_kernel, [(16, 48, 128)], [(4, Y3, 128)], parts2)
    parts3 = lax.all_to_all(chunk3, "gx", 0, 0)
    (sheet,) = call(pick2_kernel, [(36, 4, 128)], [], parts2)
    west, east = around(sheet, "gx")
    (a,) = call(
        window2_kernel,
        [(4, X2, Y2, 128)],
        [(3, Y2, 128)],
        west, sheet, east,
        cost=(4 << 20, 1 << 20),
    )
    wide3 = (X3 + 2 * PAD3, Y3, 128)
    wide4 = (X4 + 2, Y4, 128)
    scratch = [(3,) + wide3, (2,) + wide3, (2,) + wide3, (2,) + wide3, (3 * X4 * Y3, 128)]
    scratch += [(3,) + wide4, (2,) + wide4, (2,) + wide4, (2,) + wide4, (2 * X4 * Y3, 128)]
    scratch += [(2, 6, Y3 + 16, 128), (2 * 6 * Y2, 128)] + [(2, X2, Y2, 128)] * 3
    scratch += [(2, 8, Y2, 128), (2 * 8 * Y1, 128), (2,) + full1, (2,) + full1]
    scratch += [(2, 2 * 10 * 32, 128), (2,) + full0, (2,) + full0]
    return call(
        up_kernel,
        [(2, 16, 16, 128)],
        scratch,
        parts3, a, *kept,
        limit=16,
    )[0]


def solution(mesh):
    return jax.shard_map(
        shards,
        mesh=mesh,
        in_specs=(P(None, "gx", "gy", "gz"), P("gx", "gy", "gz")),
        out_specs=P(None, "gx", "gy", "gz"),
        check_vma=False,
    )
```
